32 devices in a mesh: rows: 4 (over y, x), cols: 8 (over z, core).
Axes of the slice: x: 2, y: 2, z: 4, core: 2. Of those that a mesh axis runs over, the one named last changes fastest.
Arguments:
- embeddings: bfloat16 [4096, 768], P(('rows', 'cols')), may hold values from -6 to 6
- document_cluster_index: int32 [4096], P(('rows', 'cols')), may hold values from 0 to 63, as said below
Outputs:
- max_similarity: float32 [4096], P(('rows', 'cols'))
- histogram: float32 [128], replicated
The draws below stay inside these ranges and needn't reach their ends.
Inputs may be any that keep to these rules, and one draw needn't show every extreme that they name: `document_cluster_index`: cluster r * 16 to (r + 1) * 16 - 1 form row group r. Each device's block of 128 documents names at most 64 documents of any one row group, and exactly 64 of one. The documents that the devices with one index along cols name for one row group hold at most 32 documents of any one cluster, and in every draw some such set holds exactly 32 of one cluster.
All inputs are finite; a program needn't handle non-finite values.
Results may differ from the reference program's by a relative error of at most 0.0014.
Values may be sent and summed in bfloat16 or wider, within the bound.
A program may use at most 64 MiB of HBM per device.

```python
import jax
import jax.numpy as jnp
from jax import lax

D = 768
CAP = 64
GROUP_CLUSTERS = 16
BINS = 128
CLUSTER_DOC_PEAK = 32
DOC_DEV = 128
DOCS = 4096
N_ROWS = 4
N_COLS = 8


def draw_document_cluster_index(key, part):
    row_offset = jax.random.randint(jax.random.fold_in(key, 7), (N_ROWS,), 0, GROUP_CLUSTERS)
    fixed_col = jax.random.randint(jax.random.fold_in(key, 8), (), 0, N_COLS)
    fixed_row = jax.random.randint(jax.random.fold_in(key, 9), (), 0, N_ROWS)
    device_base = jax.random.fold_in(key, 11)
    order_base = jax.random.fold_in(key, 12)
    pool_rows = jnp.arange((N_ROWS - 1) * CAP, dtype=jnp.int32) // CAP

    def one_device(device_index):
        device_key = jax.random.fold_in(device_base, device_index)
        first_row = jax.random.randint(jax.random.fold_in(device_key, 1), (), 0, N_ROWS)
        first_row = jnp.where(device_index % N_COLS == fixed_col, fixed_row, first_row).astype(jnp.int32)
        other_rows = (first_row + 1 + pool_rows) % N_ROWS
        other_rows = jax.random.permutation(jax.random.fold_in(device_key, 2), other_rows)[:DOC_DEV - CAP]
        targets = jnp.concatenate([jnp.full((CAP,), first_row, jnp.int32), other_rows.astype(jnp.int32)])
        return jax.random.permutation(jax.random.fold_in(device_key, 3), targets).astype(jnp.int32)
    targets = jax.vmap(one_device)(jnp.arange(N_ROWS * N_COLS, dtype=jnp.int32))
    column_wise = targets.reshape(N_ROWS, N_COLS, DOC_DEV).transpose(1, 0, 2).reshape(N_COLS, N_ROWS * DOC_DEV)
    onehot = (column_wise[:, :, None] == jnp.arange(N_ROWS, dtype=jnp.int32)[None, None, :]).astype(jnp.int32)
    ranks = jnp.sum((jnp.cumsum(onehot, axis=1) - 1) * onehot, axis=2).astype(jnp.int32)
    pooled_clusters = jnp.arange(GROUP_CLUSTERS * CLUSTER_DOC_PEAK, dtype=jnp.int32) // CLUSTER_DOC_PEAK
    stride_length = max(1, 2 ** 20 // GROUP_CLUSTERS)

    def single_order(order_index):
        row_group = order_index % N_ROWS
        sorting_key = jax.random.fold_in(order_base, order_index)
        current_best = (pooled_clusters - row_offset[row_group]) % GROUP_CLUSTERS
        similarity_scores = jax.random.randint(sorting_key, (GROUP_CLUSTERS * CLUSTER_DOC_PEAK,), 0, 2 ** 20) + current_best * stride_length
        similarity_scores = jnp.where(current_best == 0, -1, similarity_scores)
        return pooled_clusters[jnp.argsort(similarity_scores, stable=True)].astype(jnp.int32)
    order_list = jax.vmap(single_order)(jnp.arange(N_COLS * N_ROWS, dtype=jnp.int32)).reshape(N_COLS, N_ROWS, GROUP_CLUSTERS * CLUSTER_DOC_PEAK)
    cluster_member = order_list[jnp.arange(N_COLS, dtype=jnp.int32)[:, None], column_wise, ranks]
    cluster_labels = column_wise * GROUP_CLUSTERS + cluster_member
    return cluster_labels.reshape(N_COLS, N_ROWS, DOC_DEV).transpose(1, 0, 2).reshape(-1).astype(jnp.int32)


def shard_levels(stream_key, dims, split, least, high):
    def one(axis_at, blocks):
        steps = jax.random.uniform(jax.random.fold_in(jax.random.fold_in(stream_key, 6), axis_at), (blocks,), jnp.float32, least / len(split), high / len(split))
        return jnp.repeat(jnp.exp(steps), dims[axis_at] // blocks).reshape((-1,) + (1,) * (len(dims) - axis_at - 1))

    gain = one(*split[0])
    for cut in split[1:]:
        gain = gain * one(*cut)
    return gain


def noise(rng, shape, scale, limit, split=(), kind=jnp.bfloat16):
    loudness = shard_levels(rng, shape, split, -0.22, 0.18) if split else 1.0
    result = jax.random.normal(rng, shape, jnp.float32) * scale * loudness
    return jnp.minimum(jnp.maximum(result, -limit), limit).astype(kind)


def setup_inputs(seed: int = 0) -> dict:
    arg_keys = jax.random.split(jax.random.key(seed), 3)
    embeddings = noise(arg_keys[0], (DOCS, D), 1.0, 6.0, ((0, 32),))
    document_cluster_index = draw_document_cluster_index(jax.random.fold_in(arg_keys[2], 71), 0)
    return dict(embeddings=embeddings, document_cluster_index=document_cluster_index)


def reference(embeddings, document_cluster_index):
    values = embeddings.astype(jnp.float32)
    normed = (values * lax.rsqrt(lax.optimization_barrier(jnp.sum(values * values, axis=1, keepdims=True)) + 1e-06)).astype(jnp.bfloat16)
    doc_total = document_cluster_index.shape[0]
    owner_devices = (document_cluster_index // GROUP_CLUSTERS).astype(jnp.int32)
    doc_order = jnp.argsort(owner_devices, stable=True).astype(jnp.int32)
    counts = lax.optimization_barrier(jnp.sum((owner_devices[:, None] == jnp.arange(N_ROWS, dtype=jnp.int32)[None, :]).astype(jnp.int32), axis=0))
    starts = (jnp.cumsum(counts) - counts).astype(jnp.int32)
    row_span = CAP * N_ROWS * N_COLS
    tile_rows = min(512, row_span)
    sorted_rows = jnp.concatenate([normed[doc_order].astype(jnp.float32), jnp.zeros((row_span, normed.shape[1]), jnp.float32)], axis=0)
    cluster_labels = jnp.concatenate([document_cluster_index[doc_order].astype(jnp.int32), jnp.full((row_span,), -1, jnp.int32)], axis=0)
    span_index = jnp.arange(row_span, dtype=jnp.int32)

    def per_group(row_group):
        group_rows = lax.dynamic_slice_in_dim(sorted_rows, starts[row_group], row_span, 0)
        group_labels = lax.dynamic_slice_in_dim(cluster_labels, starts[row_group], row_span, 0)
        group_labels = jnp.where(span_index < counts[row_group], group_labels, -1)

        def per_tile(tile_index):
            tile_start = (tile_index * tile_rows).astype(jnp.int32)
            tile = lax.dynamic_slice_in_dim(group_rows, tile_start, tile_rows, 0)
            tile_labels = lax.dynamic_slice_in_dim(group_labels, tile_start, tile_rows, 0)
            similarity_scores = jnp.dot(tile, group_rows.T, precision=lax.Precision.HIGHEST)
            tile_index_rows = tile_start + jnp.arange(tile_rows, dtype=jnp.int32)
            same_cluster = (tile_labels[:, None] == group_labels[None, :]) & (tile_labels[:, None] >= 0)
            same_cluster = same_cluster & (tile_index_rows[:, None] != span_index[None, :])
            return lax.optimization_barrier(jnp.max(jnp.where(same_cluster, similarity_scores, -1.0), axis=1))
        return lax.map(per_tile, jnp.arange(row_span // tile_rows, dtype=jnp.int32)).reshape(row_span)
    results = lax.map(per_group, jnp.arange(N_ROWS, dtype=jnp.int32))
    sorted_owner = owner_devices[doc_order]
    offsets = (jnp.arange(doc_total, dtype=jnp.int32) - starts[sorted_owner]).astype(jnp.int32)
    sorted_values = results[sorted_owner, offsets]
    max_similarity = jnp.zeros((doc_total,), jnp.float32).at[doc_order].set(sorted_values)
    bin_width = 2.0 / (BINS - 1)
    centers = -1.0 + jnp.arange(BINS, dtype=jnp.float32) * bin_width
    bin_weights = jax.nn.relu(1.0 - jnp.abs(max_similarity[:, None] - centers[None, :]) / bin_width)
    histogram = lax.optimization_barrier(jnp.sum(bin_weights, axis=0)) / doc_total
    return (max_similarity, histogram)
```

```python
import functools

import jax
import jax.numpy as jnp
from jax import lax
from jax.experimental import pallas as pl
from jax.experimental.pallas import tpu as pltpu
from jax.sharding import PartitionSpec as P

CAP = 64
GROUP_CLUSTERS = 16
BINS = 128
CORES = 2


def from_partner(value, axis, bit):
    mask = 2**bit
    pairs = [(source, source ^ mask) for source in range(lax.axis_size(axis))]
    return lax.ppermute(value, axis, pairs)


def rank_among_equals(keys):
    places = jnp.arange(keys.shape[0], dtype=jnp.int32)
    earlier_equal = (keys[:, None] == keys[None, :]) & (places[None, :] < places[:, None])
    return jnp.sum(earlier_equal.astype(jnp.int32), axis=1)


def shards(embeddings, document_cluster_index):
    row_count = lax.axis_size("rows")
    col_count = lax.axis_size("cols")
    doc_count = embeddings.shape[0]
    width = embeddings.shape[1]
    slot_count = CAP * row_count
    values = embeddings.astype(jnp.float32)
    normed = (values * lax.rsqrt(jnp.sum(values * values, axis=1, keepdims=True) + 1e-06)).astype(
        jnp.bfloat16
    )
    owner_devices = document_cluster_index // GROUP_CLUSTERS
    within_cluster = (document_cluster_index % GROUP_CLUSTERS).astype(jnp.float32)
    slot_ranks = rank_among_equals(owner_devices)
    places = owner_devices * CAP + slot_ranks
    outgoing = jnp.zeros((slot_count, width), jnp.bfloat16).at[places].set(normed)
    out_labels = (
        jnp.full((slot_count,), -1.0, jnp.float32)
        .at[places]
        .set(within_cluster)
        .astype(jnp.bfloat16)
    )
    resident, res_labels = (
        lax.all_to_all(outgoing, "rows", split_axis=0, concat_axis=0, tiled=True),
        lax.all_to_all(out_labels, "rows", split_axis=0, concat_axis=0, tiled=True),
    )
    home_labels = res_labels.astype(jnp.float32)
    partner_count = max(1, col_count // GROUP_CLUSTERS)
    owned_count = max(1, GROUP_CLUSTERS // col_count)
    slot_quota = 2 * slot_count // GROUP_CLUSTERS // partner_count
    send_total = col_count * owned_count * slot_quota
    local_cluster = res_labels.astype(jnp.int32)
    occupied = local_cluster >= 0
    cluster_rank = rank_among_equals(local_cluster)
    member_slot = cluster_rank % partner_count
    cluster_depth = cluster_rank // partner_count
    destination = local_cluster // owned_count * partner_count + member_slot
    send_place = (
        destination * (owned_count * slot_quota)
        + local_cluster % owned_count * slot_quota
        + cluster_depth
    )
    send_place = jnp.where(occupied, send_place, send_total)
    send_rows = (
        jnp.zeros((send_total, width), jnp.bfloat16).at[send_place].set(resident, mode="drop")
    )
    send_labels = (
        jnp.full((send_total,), -1.0, jnp.float32)
        .at[send_place]
        .set(home_labels, mode="drop")
        .astype(jnp.bfloat16)
    )
    got_rows, got_labels = (
        lax.all_to_all(send_rows, "cols", split_axis=0, concat_axis=0, tiled=True),
        lax.all_to_all(send_labels, "cols", split_axis=0, concat_axis=0, tiled=True),
    )
    member_index = lax.axis_index("cols") % partner_count
    gathered_rows, gathered_labels = (got_rows, got_labels)
    for bit in range(partner_count.bit_length() - 1):
        other_rows, other_labels = from_partner((gathered_rows, gathered_labels), "cols", bit)
        upper = member_index // 2**bit % 2 == 1
        gathered_rows = jnp.where(
            upper,
            jnp.concatenate([other_rows, gathered_rows], axis=0),
            jnp.concatenate([gathered_rows, other_rows], axis=0),
        )
        gathered_labels = jnp.where(
            upper,
            jnp.concatenate([other_labels, gathered_labels], axis=0),
            jnp.concatenate([gathered_labels, other_labels], axis=0),
        )
    similarity_scores = lax.dot_general(
        got_rows, gathered_rows, (((1,), (1,)), ((), ())), preferred_element_type=jnp.float32
    )
    own_labels = got_labels.astype(jnp.float32)
    all_labels = gathered_labels.astype(jnp.float32)
    column_index = jnp.arange(gathered_rows.shape[0], dtype=jnp.int32)
    own_index = member_index * send_total + jnp.arange(send_total, dtype=jnp.int32)
    same_cluster = (own_labels[:, None] == all_labels[None, :]) & (own_labels[:, None] >= 0.0)
    same_cluster = same_cluster & (own_index[:, None] != column_index[None, :])
    best_owned = jnp.max(jnp.where(same_cluster, similarity_scores, -1.0), axis=1)
    came_back = lax.all_to_all(best_owned, "cols", split_axis=0, concat_axis=0, tiled=True)
    row_best = jnp.where(occupied, came_back[jnp.minimum(send_place, send_total - 1)], -1.0)
    answers = lax.all_to_all(row_best, "rows", split_axis=0, concat_axis=0, tiled=True)
    max_similarity = answers[places]
    bin_width = 2.0 / (BINS - 1)
    centers = -1.0 + jnp.arange(BINS, dtype=jnp.float32) * bin_width
    bin_weights = jax.nn.relu(1.0 - jnp.abs(max_similarity[:, None] - centers[None, :]) / bin_width)
    bin_totals = lax.psum(jnp.sum(bin_weights, axis=0), ("rows", "cols"))
    return (max_similarity, bin_totals / (doc_count * row_count * col_count))


CHUNKS = (32, 32, 32, 16, 16)


def meet_kernel(doc_total, emb_hbm, cluster_hbm, best_ref, hist_ref, emb_ref, cluster_ref, keys, blocks, key_labels,
                block_labels, label_columns, key_best, row_best, above, slices, final_send, final_box, answer_send,
                answer_box, in_sems, plane_sems, chunk_sems, block_sems, label_sems, partial_sems, slice_sems, final_sems,
                answer_sems):
    row, col = lax.axis_index("rows"), lax.axis_index("cols")
    z, core = col // CORES, col % CORES
    row_at = (row, row + 1 - 2 * (row % 2), row + 2 - 4 * (row // 2), 3 - row)
    core_at = (core, 1 - core)
    near = len(row_at)
    slots = near * CORES
    docs, width = emb_ref.shape
    half = docs // 2

    def at_slot(slot, plane):
        return (row_at[slot % near], plane * CORES + core_at[slot // near])

    def above_me(plane):
        return (row, plane * CORES + core)

    x_peer, y_peer, core_peer = at_slot(1, z), at_slot(2, z), at_slot(near, z)

    def copy(source, target, sems, at, where):
        return pltpu.make_async_remote_copy(
            src_ref=source, dst_ref=target, send_sem=sems.at[(0, *at)], recv_sem=sems.at[(1, *at)],
            device_id=where, device_id_type=pl.DeviceIdType.MESH)

    barrier = pltpu.get_barrier_semaphore()

    def greet(where):
        pl.semaphore_signal(barrier, inc=1, device_id=where, device_id_type=pl.DeviceIdType.MESH)

    senders = {0: (1, 2, 3), 1: (0, 2, 3), 2: (), 3: (2,)}
    for plane, sources in senders.items():
        @pl.when(z == plane)
        def _():
            for source in sources:
                greet(above_me(source))
    for peer in (x_peer, y_peer, core_peer):
        greet(peer)
    load = pltpu.make_async_copy(emb_hbm, emb_ref, in_sems.at[0])
    load_labels = pltpu.make_async_copy(cluster_hbm, cluster_ref, in_sems.at[1])
    load.start()
    load_labels.start()
    load_labels.wait()
    key_labels[0] = cluster_ref[...].astype(jnp.float32)
    load.wait()
    values = emb_ref[...].astype(jnp.float32)
    normed = values * lax.rsqrt(jnp.sum(values * values, axis=1, keepdims=True) + 1e-06)
    keys[0:docs, :] = normed.astype(jnp.bfloat16)
    for plane in senders:
        @pl.when(z == plane)
        def _():
            pl.semaphore_wait(barrier, 3 + sum(plane in sources for sources in senders.values()))

    def part(slot, first, size):
        return keys.at[pl.ds(slot * docs + first, size)]

    def plane_copy(n):
        source, target, first, size, where = (
            (0, 1, 0, half, x_peer),
            (0, 2, half, half, y_peer),
            (0, 1, half, half, x_peer),
            (0, 2, 0, half, y_peer),
            (1, 3, 0, half, y_peer),
            (2, 3, half, half, x_peer),
            (0, 4, 0, docs, core_peer),
            (1, 5, 0, docs, core_peer),
            (2, 6, 0, docs, core_peer),
            (3, 7, 0, docs, core_peer),
        )[n]
        return copy(part(source, first, size), part(target, first, size), plane_sems, (n,), where)

    def plane_label(n):
        source, target, count, where = ((0, 1, 1, x_peer), (0, 2, 1, y_peer), (1, 3, 1, y_peer), (0, near, near, core_peer))[n]
        return copy(key_labels.at[pl.ds(source, count)], key_labels.at[pl.ds(target, count)], label_sems, (n,), where)

    def start(*copies):
        for item in copies:
            item.start()

    def arrive(*copies):
        for item in copies:
            item.wait_recv()

    def sent(*copies):
        for item in copies:
            item.wait_send()

    firsts = [sum(CHUNKS[:i]) for i in range(len(CHUNKS))]

    def chunk(n, i, source, plane):
        rows = pl.ds(firsts[i], CHUNKS[i])
        block = blocks.at[n, rows]
        return copy(keys.at[rows] if source is None else block, block, chunk_sems, (n, i), above_me(plane))

    def whole(n, plane):
        return copy(keys.at[pl.ds(0, docs)], blocks.at[n], block_sems, (n,), above_me(plane))

    def block_label(n, plane):
        return copy(key_labels.at[0], block_labels.at[n], label_sems, (4 + n,), above_me(plane))

    def label_up(plane):
        return copy(key_labels.at[0], block_labels.at[0], label_sems, (8,), above_me(plane))

    def both_labels(plane):
        pair = block_labels.at[pl.ds(0, 2)]
        return copy(pair, pair, label_sems, (7,), above_me(plane))

    def plane_start():
        start(plane_label(0), plane_label(1), plane_copy(0), plane_copy(1), plane_copy(2), plane_copy(3), plane_copy(6))

    def plane_diagonal():
        arrive(plane_copy(0))
        start(plane_copy(4))
        arrive(plane_copy(1))
        start(plane_copy(5))
        arrive(plane_label(0))
        start(plane_label(2))

    def plane_across():
        arrive(plane_copy(2))
        start(plane_copy(7))
        arrive(plane_copy(3))
        start(plane_copy(8))

    def plane_last():
        arrive(plane_copy(4), plane_copy(5))
        start(plane_copy(9))
        arrive(plane_label(1), plane_label(2))
        start(plane_label(3))

    def plane_ready():
        arrive(plane_label(3))
        for slot in range(slots):
            label_columns[slot] = jnp.broadcast_to(key_labels[slot], (docs, docs)).T
        arrive(*[plane_copy(n) for n in range(6, 10)])

    def plane_sent():
        sent(*[plane_copy(n) for n in range(10)], *[plane_label(n) for n in range(4)])

    same_place = lax.broadcasted_iota(jnp.int32, (docs, docs), 0) == lax.broadcasted_iota(jnp.int32, (docs, docs), 1)

    def score(queries, labels, own, fresh=True, keep=True):
        parts = len(queries)
        query = queries[0] if parts == 1 else jnp.concatenate(queries, axis=0)
        scores = lax.dot_general(keys[...], query, (((1,), (1,)), ((), ())), preferred_element_type=jnp.float32)
        tops = [jnp.full((8, docs), -1.0, jnp.float32) for _ in queries]
        for slot in range(slots):
            both = None
            for n in range(parts):
                same = label_columns[slot] == labels[n]
                if own and n == 0 and slot == 0:
                    same = same & jnp.logical_not(same_place)
                found = jnp.where(same, scores[slot * docs:(slot + 1) * docs, n * docs:(n + 1) * docs], -1.0)
                tops[n] = jnp.maximum(tops[n], jnp.max(found.reshape(docs // 8, 8, docs), axis=0))
                both = found if both is None else jnp.maximum(both, found)
            if keep:
                key_best[slot] = both if fresh else jnp.maximum(key_best[slot], both)
        return [jnp.max(top, axis=0, keepdims=True) for top in tops]

    def best_of_keys(slot):
        return jnp.max(key_best[slot].T, axis=0, keepdims=True)

    bin_width = 2.0 / (BINS - 1)
    centers = -1.0 + lax.broadcasted_iota(jnp.int32, (BINS, docs), 0).astype(jnp.float32) * bin_width

    def histogram(tiles):
        weights = sum(jnp.maximum(1.0 - jnp.abs(tile - centers) / bin_width, 0.0) for tile in tiles)
        return jnp.sum(weights.T, axis=0, keepdims=True)

    spans = {1: (0, 3), 2: (3, 1), 3: (4, 2)}

    def partials(plane):
        first, count = spans[plane]
        return copy(row_best.at[pl.ds(0, count)], above.at[pl.ds(first, count)], partial_sems, (plane,), above_me(0))

    def slice_copy(slot, plane):
        return copy(final_send.at[slot], slices.at[slot], slice_sems, (slot,), at_slot(slot, plane))

    def final_copy(slot):
        return copy(final_send, final_box.at[slot], final_sems, (slot,), at_slot(slot, z))

    def answer_copy(plane):
        return copy(answer_send.at[plane], answer_box.at[0], answer_sems, (0, plane), above_me(plane))

    def total_copy(plane):
        return copy(answer_send.at[0], answer_box.at[1], answer_sems, (1, plane), above_me(plane))

    def take_answer(plane):
        arrive(answer_copy(plane))
        best_ref[...] = answer_box[0]
        arrive(total_copy(plane))
        hist_ref[...] = answer_box[1]

    every = range(len(CHUNKS))

    @pl.when(z == 3)
    def _():
        start(block_label(1, 1))
        start(*[chunk(1, i, None, 1) for i in every])
        plane_start()
        plane_diagonal()
        plane_across()
        plane_last()
        plane_ready()
        arrive(label_up(3), whole(0, 3))
        mine, theirs = score([keys[0:docs, :], blocks[0]], [key_labels[0], block_labels[0]], True)
        for slot in range(1, slots):
            final_send[slot] = best_of_keys(slot)
            slice_copy(slot, 3).start()
        slices[0] = jnp.maximum(mine, best_of_keys(0))
        row_best[0] = theirs
        arrive(*[slice_copy(slot, 3) for slot in range(1, slots)])
        row_best[1] = jnp.max(slices[...], axis=0)
        start(partials(3))
        sent(block_label(1, 1), *[chunk(1, i, None, 1) for i in every], *[slice_copy(slot, 3) for slot in range(1, slots)])
        plane_sent()
        sent(partials(3))
        take_answer(3)

    @pl.when(z == 2)
    def _():
        start(block_label(0, 1), label_up(3))
        start(*[chunk(0, i, None, 1) for i in every])
        start(whole(0, 3))
        plane_start()
        plane_diagonal()
        plane_across()
        plane_last()
        plane_ready()
        row_best[0] = score([keys[0:docs, :]], [key_labels[0]], True, keep=False)[0]
        start(partials(2))
        sent(block_label(0, 1), label_up(3), *[chunk(0, i, None, 1) for i in every], whole(0, 3))
        plane_sent()
        sent(partials(2))
        take_answer(2)

    @pl.when(z == 1)
    def _():
        plane_start()

        def forward(i):
            for n in range(2):
                arrive(chunk(n, i, n, 0))
                start(chunk(n, i, n, 0))

        forward(0)
        plane_diagonal()
        arrive(block_label(0, 1), block_label(1, 1))
        start(both_labels(0))
        forward(1)
        plane_across()
        forward(2)
        plane_last()
        plane_ready()
        arrive(block_label(2, 1), whole(2, 1))
        mine, theirs = score([keys[0:docs, :], blocks[2]], [key_labels[0], block_labels[2]], True)
        row_best[0] = theirs
        for i in every[3:]:
            forward(i)
        row_best[1], row_best[2] = score([blocks[0], blocks[1]], [block_labels[0], block_labels[1]], False, fresh=False)
        start(partials(1))
        for slot in range(slots):
            final_send[slot] = best_of_keys(slot) if slot else jnp.maximum(mine, best_of_keys(0))
            slice_copy(slot, 0).start()
        sent(both_labels(0), *[chunk(n, i, n, 0) for n in range(2) for i in every])
        plane_sent()
        sent(partials(1), *[slice_copy(slot, 0) for slot in range(slots)])
        take_answer(1)

    @pl.when(z == 0)
    def _():
        start(block_label(2, 1), whole(2, 1))
        plane_start()
        plane_diagonal()
        plane_across()
        plane_last()
        plane_ready()
        mine = score([keys[0:docs, :]], [key_labels[0]], True)[0]
        arrive(both_labels(0))
        for i in every:
            for n in range(2):
                arrive(chunk(n, i, n, 0))
        second, third = score([blocks[0], blocks[1]], [block_labels[0], block_labels[1]], False, fresh=False)
        arrive(partials(1), partials(2), partials(3))
        arrive(*[slice_copy(slot, 0) for slot in range(slots)])
        first = jnp.max(slices[...], axis=0)
        second = jnp.maximum(jnp.maximum(second, above[1]), jnp.maximum(above[3], above[4]))
        third = jnp.maximum(third, jnp.maximum(above[2], above[5]))
        for slot in range(slots):
            final_send[slot] = best_of_keys(slot) if slot else jnp.maximum(jnp.maximum(mine, above[0]), best_of_keys(0))
        final_send[slots] = histogram([first, second, third])
        for slot in range(1, slots):
            final_copy(slot).start()
        for plane, found in ((1, first), (2, second), (3, third)):
            answer_send[plane] = found
            answer_copy(plane).start()
        final_box[0] = final_send[...]
        arrive(*[final_copy(slot) for slot in range(1, slots)])
        found = []
        for slot in range(slots):
            tile = final_box[0, slot]
            for sender in range(1, slots):
                tile = jnp.maximum(tile, final_box[sender, slot ^ sender])
            found.append(tile)
        totals = histogram(found)
        for slot in range(slots):
            totals = totals + final_box[slot, slots]
        answer_send[0] = totals / doc_total
        for plane in (3, 2, 1):
            total_copy(plane).start()
        best_ref[...] = found[0]
        hist_ref[...] = answer_send[0]
        sent(block_label(2, 1), whole(2, 1))
        plane_sent()
        sent(*[final_copy(slot) for slot in range(1, slots)])
        for plane in (1, 2, 3):
            sent(answer_copy(plane), total_copy(plane))


def meet_shards(embeddings, document_cluster_index):
    rows, cols = lax.axis_size("rows"), lax.axis_size("cols")
    docs, width = embeddings.shape
    slots = rows * CORES
    hbm, vmem = pl.BlockSpec(memory_space=pl.ANY), pl.BlockSpec(memory_space=pltpu.VMEM)
    dma = pltpu.SemaphoreType.DMA
    line = lambda *lead: pltpu.VMEM((*lead, 1, docs), jnp.float32)
    best, histogram = pl.pallas_call(
        functools.partial(meet_kernel, docs * rows * cols),
        out_shape=(pltpu.VMEM((1, docs), jnp.float32), pltpu.VMEM((1, BINS), jnp.float32)),
        in_specs=[hbm, hbm],
        out_specs=(vmem, vmem),
        scratch_shapes=[
            pltpu.VMEM((docs, width), jnp.bfloat16),
            pltpu.VMEM((1, docs), jnp.int32),
            pltpu.VMEM((slots * docs, width), jnp.bfloat16),
            pltpu.VMEM((3, docs, width), jnp.bfloat16),
            line(slots),
            line(3),
            pltpu.VMEM((slots, docs, docs), jnp.float32),
            pltpu.VMEM((slots, docs, docs), jnp.float32),
            line(3),
            line(6),
            line(slots),
            line(slots + 1),
            line(slots, slots + 1),
            line(4),
            line(2),
            dma((2,)),
            dma((2, 10)),
            dma((2, 2, len(CHUNKS))),
            dma((2, 3)),
            dma((2, 9)),
            dma((2, 4)),
            dma((2, slots)),
            dma((2, slots)),
            dma((2, 2, 4)),
        ],
        compiler_params=pltpu.CompilerParams(collective_id=0, has_side_effects=True),
    )(embeddings, document_cluster_index.reshape(1, docs))
    return best.reshape(docs), histogram.reshape(BINS)


def solution(mesh):
    placed = (P(("rows", "cols"), None), P(("rows", "cols")))
    rows, planes = mesh.shape["rows"], mesh.shape["cols"] // CORES
    direct = rows == 4 and planes == rows
    return jax.shard_map(
        meet_shards if direct else shards, mesh=mesh, in_specs=placed,
        out_specs=(P(("rows", "cols")), P()), check_vma=False
    )
```

```python
import functools

import jax
import jax.numpy as jnp
from jax import lax
from jax.experimental import pallas as pl
from jax.experimental.pallas import tpu as pltpu
from jax.sharding import PartitionSpec as P

CAP = 64
GROUP_CLUSTERS = 16
BINS = 128
CORES = 2


def from_partner(value, axis, bit):
    mask = 2**bit
    pairs = [(source, source ^ mask) for source in range(lax.axis_size(axis))]
    return lax.ppermute(value, axis, pairs)


def rank_among_equals(keys):
    places = jnp.arange(keys.shape[0], dtype=jnp.int32)
    earlier_equal = (keys[:, None] == keys[None, :]) & (places[None, :] < places[:, None])
    return jnp.sum(earlier_equal.astype(jnp.int32), axis=1)


def shards(embeddings, document_cluster_index):
    row_count = lax.axis_size("rows")
    col_count = lax.axis_size("cols")
    doc_count = embeddings.shape[0]
    width = embeddings.shape[1]
    slot_count = CAP * row_count
    values = embeddings.astype(jnp.float32)
    normed = (values * lax.rsqrt(jnp.sum(values * values, axis=1, keepdims=True) + 1e-06)).astype(
        jnp.bfloat16
    )
    owner_devices = document_cluster_index // GROUP_CLUSTERS
    within_cluster = (document_cluster_index % GROUP_CLUSTERS).astype(jnp.float32)
    slot_ranks = rank_among_equals(owner_devices)
    places = owner_devices * CAP + slot_ranks
    outgoing = jnp.zeros((slot_count, width), jnp.bfloat16).at[places].set(normed)
    out_labels = (
        jnp.full((slot_count,), -1.0, jnp.float32)
        .at[places]
        .set(within_cluster)
        .astype(jnp.bfloat16)
    )
    resident, res_labels = (
        lax.all_to_all(outgoing, "rows", split_axis=0, concat_axis=0, tiled=True),
        lax.all_to_all(out_labels, "rows", split_axis=0, concat_axis=0, tiled=True),
    )
    home_labels = res_labels.astype(jnp.float32)
    partner_count = max(1, col_count // GROUP_CLUSTERS)
    owned_count = max(1, GROUP_CLUSTERS // col_count)
    slot_quota = 2 * slot_count // GROUP_CLUSTERS // partner_count
    send_total = col_count * owned_count * slot_quota
    local_cluster = res_labels.astype(jnp.int32)
    occupied = local_cluster >= 0
    cluster_rank = rank_among_equals(local_cluster)
    member_slot = cluster_rank % partner_count
    cluster_depth = cluster_rank // partner_count
    destination = local_cluster // owned_count * partner_count + member_slot
    send_place = (
        destination * (owned_count * slot_quota)
        + local_cluster % owned_count * slot_quota
        + cluster_depth
    )
    send_place = jnp.where(occupied, send_place, send_total)
    send_rows = (
        jnp.zeros((send_total, width), jnp.bfloat16).at[send_place].set(resident, mode="drop")
    )
    send_labels = (
        jnp.full((send_total,), -1.0, jnp.float32)
        .at[send_place]
        .set(home_labels, mode="drop")
        .astype(jnp.bfloat16)
    )
    got_rows, got_labels = (
        lax.all_to_all(send_rows, "cols", split_axis=0, concat_axis=0, tiled=True),
        lax.all_to_all(send_labels, "cols", split_axis=0, concat_axis=0, tiled=True),
    )
    member_index = lax.axis_index("cols") % partner_count
    gathered_rows, gathered_labels = (got_rows, got_labels)
    for bit in range(partner_count.bit_length() - 1):
        other_rows, other_labels = from_partner((gathered_rows, gathered_labels), "cols", bit)
        upper = member_index // 2**bit % 2 == 1
        gathered_rows = jnp.where(
            upper,
            jnp.concatenate([other_rows, gathered_rows], axis=0),
            jnp.concatenate([gathered_rows, other_rows], axis=0),
        )
        gathered_labels = jnp.where(
            upper,
            jnp.concatenate([other_labels, gathered_labels], axis=0),
            jnp.concatenate([gathered_labels, other_labels], axis=0),
        )
    similarity_scores = lax.dot_general(
        got_rows, gathered_rows, (((1,), (1,)), ((), ())), preferred_element_type=jnp.float32
    )
    own_labels = got_labels.astype(jnp.float32)
    all_labels = gathered_labels.astype(jnp.float32)
    column_index = jnp.arange(gathered_rows.shape[0], dtype=jnp.int32)
    own_index = member_index * send_total + jnp.arange(send_total, dtype=jnp.int32)
    same_cluster = (own_labels[:, None] == all_labels[None, :]) & (own_labels[:, None] >= 0.0)
    same_cluster = same_cluster & (own_index[:, None] != column_index[None, :])
    best_owned = jnp.max(jnp.where(same_cluster, similarity_scores, -1.0), axis=1)
    came_back = lax.all_to_all(best_owned, "cols", split_axis=0, concat_axis=0, tiled=True)
    row_best = jnp.where(occupied, came_back[jnp.minimum(send_place, send_total - 1)], -1.0)
    answers = lax.all_to_all(row_best, "rows", split_axis=0, concat_axis=0, tiled=True)
    max_similarity = answers[places]
    bin_width = 2.0 / (BINS - 1)
    centers = -1.0 + jnp.arange(BINS, dtype=jnp.float32) * bin_width
    bin_weights = jax.nn.relu(1.0 - jnp.abs(max_similarity[:, None] - centers[None, :]) / bin_width)
    bin_totals = lax.psum(jnp.sum(bin_weights, axis=0), ("rows", "cols"))
    return (max_similarity, bin_totals / (doc_count * row_count * col_count))


CHUNKS = (16, 32, 32, 32, 16)


def meet_kernel(doc_total, emb_hbm, cluster_hbm, out_ref, emb_ref, cluster_ref, keys, blocks, key_labels,
                block_labels, label_columns, key_best, row_best, above, final_send, final_box, answer_send,
                packets, answer_box, in_sems, plane_sems, chunk_sems, block_sems, label_sems, partial_sems, final_sems,
                answer_sems, packet_sems):
    row, col = lax.axis_index("rows"), lax.axis_index("cols")
    z, core = col // CORES, col % CORES
    row_at = (row, row + 1 - 2 * (row % 2), row + 2 - 4 * (row // 2), 3 - row)
    core_at = (core, 1 - core)
    near = len(row_at)
    slots = near * CORES
    docs, width = emb_ref.shape
    half = docs // 2

    def at_slot(slot, plane):
        return (row_at[slot % near], plane * CORES + core_at[slot // near])

    def above_me(plane):
        return (row, plane * CORES + core)

    x_peer, y_peer, core_peer = at_slot(1, z), at_slot(2, z), at_slot(near, z)

    def copy(source, target, sems, at, where):
        return pltpu.make_async_remote_copy(
            src_ref=source, dst_ref=target, send_sem=sems.at[(0, *at)], recv_sem=sems.at[(1, *at)],
            device_id=where, device_id_type=pl.DeviceIdType.MESH)

    barrier = pltpu.get_barrier_semaphore()

    def greet(where):
        pl.semaphore_signal(barrier, inc=1, device_id=where, device_id_type=pl.DeviceIdType.MESH)

    senders = {0: (1, 2, 3), 1: (0, 2, 3), 2: (3,), 3: (2,)}
    for plane, sources in senders.items():
        @pl.when(z == plane)
        def _():
            for source in sources:
                greet(above_me(source))
    for peer in (x_peer, y_peer, core_peer):
        greet(peer)
    load = pltpu.make_async_copy(emb_hbm, emb_ref, in_sems.at[0])
    load_labels = pltpu.make_async_copy(cluster_hbm, cluster_ref, in_sems.at[1])
    load.start()
    load_labels.start()
    load_labels.wait()
    key_labels[0] = cluster_ref[...].astype(jnp.float32)
    load.wait()
    values = emb_ref[...].astype(jnp.float32)
    normed = values * lax.rsqrt(jnp.sum(values * values, axis=1, keepdims=True) + 1e-06)
    keys[0:docs, :] = normed.astype(jnp.bfloat16)
    for plane in senders:
        @pl.when(z == plane)
        def _():
            pl.semaphore_wait(barrier, 3 + sum(plane in sources for sources in senders.values()))

    def part(slot, first, size):
        return keys.at[pl.ds(slot * docs + first, size)]

    def plane_copy(n):
        source, target, first, size, where = (
            (0, 1, 0, half, x_peer),
            (0, 2, half, half, y_peer),
            (0, 1, half, half, x_peer),
            (0, 2, 0, half, y_peer),
            (1, 3, 0, half, y_peer),
            (2, 3, half, half, x_peer),
            (0, 4, 0, docs, core_peer),
            (1, 5, 0, docs, core_peer),
            (2, 6, 0, docs, core_peer),
            (3, 7, 0, docs, core_peer),
        )[n]
        return copy(part(source, first, size), part(target, first, size), plane_sems, (n,), where)

    def plane_label(n):
        source, target, count, where = ((0, 1, 1, x_peer), (0, 2, 1, y_peer), (1, 3, 1, y_peer), (0, near, near, core_peer))[n]
        return copy(key_labels.at[pl.ds(source, count)], key_labels.at[pl.ds(target, count)], label_sems, (n,), where)

    def start(*copies):
        for item in copies:
            item.start()

    def arrive(*copies):
        for item in copies:
            item.wait_recv()

    def sent(*copies):
        for item in copies:
            item.wait_send()

    firsts = [sum(CHUNKS[:i]) for i in range(len(CHUNKS))]

    def chunk(n, i, source, plane):
        rows = pl.ds(firsts[i], CHUNKS[i])
        block = blocks.at[n, rows]
        return copy(keys.at[rows] if source is None else block, block, chunk_sems, (n, i), above_me(plane))

    def whole(n, plane):
        return copy(keys.at[pl.ds(0, docs)], blocks.at[n], block_sems, (n,), above_me(plane))

    def block_label(n, plane):
        return copy(key_labels.at[0], block_labels.at[n], label_sems, (4 + n,), above_me(plane))

    def swap(plane):
        block = blocks.at[2]
        return copy(keys.at[pl.ds(0, docs)], block, block_sems, (0,), above_me(plane))

    def swap_label(plane):
        return copy(key_labels.at[0], block_labels.at[2], label_sems, (8,), above_me(plane))

    def both_labels(plane):
        pair = block_labels.at[pl.ds(0, 2)]
        return copy(pair, pair, label_sems, (7,), above_me(plane))

    def plane_start():
        start(plane_label(0), plane_label(1), plane_copy(0), plane_copy(1), plane_copy(2), plane_copy(3), plane_copy(6))

    def plane_diagonal():
        arrive(plane_copy(0))
        start(plane_copy(4))
        arrive(plane_copy(1))
        start(plane_copy(5))
        arrive(plane_label(0))
        start(plane_label(2))

    def plane_across():
        arrive(plane_copy(2))
        start(plane_copy(7))
        arrive(plane_copy(3))
        start(plane_copy(8))

    def plane_last():
        arrive(plane_copy(4), plane_copy(5))
        start(plane_copy(9))
        arrive(plane_label(1), plane_label(2))
        start(plane_label(3))

    def plane_ready():
        arrive(plane_label(3))
        for slot in range(slots):
            label_columns[slot] = jnp.broadcast_to(key_labels[slot], (docs, docs)).T
        arrive(*[plane_copy(n) for n in range(6, 10)])

    def plane_sent():
        sent(*[plane_copy(n) for n in range(10)], *[plane_label(n) for n in range(4)])

    same_place = lax.broadcasted_iota(jnp.int32, (docs, docs), 0) == lax.broadcasted_iota(jnp.int32, (docs, docs), 1)

    def score(queries, labels, own, fresh=True, keep=True):
        parts = len(queries)
        query = queries[0] if parts == 1 else jnp.concatenate(queries, axis=0)
        scores = lax.dot_general(keys[...], query, (((1,), (1,)), ((), ())), preferred_element_type=jnp.float32)
        tops = [jnp.full((8, docs), -1.0, jnp.float32) for _ in queries]
        for slot in range(slots):
            both = None
            for n in range(parts):
                same = label_columns[slot] == labels[n]
                if own and n == 0 and slot == 0:
                    same = same & jnp.logical_not(same_place)
                found = jnp.where(same, scores[slot * docs:(slot + 1) * docs, n * docs:(n + 1) * docs], -1.0)
                tops[n] = jnp.maximum(tops[n], jnp.max(found.reshape(docs // 8, 8, docs), axis=0))
                both = found if both is None else jnp.maximum(both, found)
            if keep:
                key_best[slot] = both if fresh else jnp.maximum(key_best[slot], both)
        return [jnp.max(top, axis=0, keepdims=True) for top in tops]

    def best_of_keys(slot):
        return jnp.max(key_best[slot].T, axis=0, keepdims=True)

    bin_width = 2.0 / (BINS - 1)
    centers = -1.0 + lax.broadcasted_iota(jnp.int32, (BINS, docs), 0).astype(jnp.float32) * bin_width

    def histogram(tiles):
        weights = sum(jnp.maximum(1.0 - jnp.abs(tile - centers) / bin_width, 0.0) for tile in tiles)
        return jnp.sum(weights.T, axis=0, keepdims=True)

    spans = {1: (0, slots + 3), 2: (slots + 3, 2), 3: (slots + 5, 2)}

    def partials(plane):
        first, count = spans[plane]
        return copy(row_best.at[pl.ds(0, count)], above.at[pl.ds(first, count)], partial_sems, (plane,), above_me(0))

    def final_copy(slot):
        return copy(final_send, final_box.at[slot], final_sems, (slot,), at_slot(slot, z))

    def answer_copy(plane):
        return copy(answer_send.at[plane - 2], answer_box.at[0], answer_sems, (plane - 2,), above_me(plane))

    def packet(slot, plane):
        first = 0 if plane == 1 else 1
        rows = pl.ds(first, 2 - first)
        return copy(packets.at[slot, rows], answer_box.at[rows], packet_sems, (slot, plane), at_slot(slot, plane))

    def take_answer(plane):
        if plane > 1:
            arrive(answer_copy(plane))

        def take(slot):
            arrive(packet(slot, plane))

        pl.when(row == 0)(lambda: take(1))
        pl.when(row != 0)(lambda: take(0))
        out_ref[...] = answer_box[...]

    every = range(len(CHUNKS))

    for plane in (2, 3):
        @pl.when(z == plane)
        def _():
            other, n = 5 - plane, plane - 2
            down = [block_label(n, 1), *[chunk(n, i, None, 1) for i in every]]
            aside = [swap_label(other), swap(other)]
            start(*(aside + down if plane == 2 else down + aside))
            plane_start()
            plane_diagonal()
            plane_across()
            plane_last()
            plane_ready()
            arrive(swap_label(plane), swap(plane))
            row_best[0], row_best[1] = score([keys[0:docs, :], blocks[2]], [key_labels[0], block_labels[2]], True, keep=False)
            start(partials(plane))
            sent(*down, *aside)
            plane_sent()
            sent(partials(plane))
            take_answer(plane)

    @pl.when(z == 1)
    def _():
        plane_start()
        arrivals = [(n, i) for n in (1, 0) for i in every]

        def forward(first, last):
            for n, i in arrivals[first:last]:
                arrive(chunk(n, i, n, 0))
                start(chunk(n, i, n, 0))

        forward(0, 1)
        plane_diagonal()
        forward(1, 4)
        plane_across()
        forward(4, 6)
        arrive(block_label(0, 1), block_label(1, 1))
        start(both_labels(0))
        plane_last()
        forward(6, 8)
        plane_ready()
        arrive(block_label(2, 1), whole(2, 1))
        mine, row_best[slots] = score([keys[0:docs, :], blocks[2]], [key_labels[0], block_labels[2]], True)
        forward(8, len(arrivals))
        row_best[slots + 1], row_best[slots + 2] = score(
            [blocks[0], blocks[1]], [block_labels[0], block_labels[1]], False, fresh=False)
        for slot in range(slots):
            row_best[slot] = best_of_keys(slot) if slot else jnp.maximum(mine, best_of_keys(0))
        start(partials(1))
        sent(both_labels(0), *[chunk(n, i, n, 0) for n, i in arrivals])
        plane_sent()
        sent(partials(1))
        take_answer(1)

    @pl.when(z == 0)
    def _():
        start(block_label(2, 1), whole(2, 1))
        plane_start()
        plane_diagonal()
        plane_across()
        plane_last()
        plane_ready()
        mine = score([keys[0:docs, :]], [key_labels[0]], True)[0]
        arrive(both_labels(0))
        for n in (1, 0):
            arrive(*[chunk(n, i, n, 0) for i in every])
        second, third = score([blocks[0], blocks[1]], [block_labels[0], block_labels[1]], False, fresh=False)
        for slot in range(1, slots):
            final_send[slot] = best_of_keys(slot)
        final_send[0] = jnp.maximum(mine, best_of_keys(0))
        arrive(partials(2), partials(3), partials(1))
        second = jnp.maximum(jnp.maximum(second, above[slots + 1]), jnp.maximum(above[slots + 3], above[slots + 6]))
        third = jnp.maximum(jnp.maximum(third, above[slots + 2]), jnp.maximum(above[slots + 4], above[slots + 5]))
        final_send[0] = jnp.maximum(final_send[0], above[slots])
        for slot in range(slots):
            final_send[slots + slot] = above[slot]
        final_send[2 * slots] = histogram([second, third])
        for slot in range(1, slots):
            final_copy(slot).start()
        for plane, found in ((2, second), (3, third)):
            answer_send[plane - 2] = found
            answer_copy(plane).start()
        final_box[0] = final_send[...]
        arrive(*[final_copy(slot) for slot in range(1, slots)])
        found = []
        for plane in range(2):
            for slot in range(slots):
                tile = final_box[0, plane * slots + slot]
                for sender in range(1, slots):
                    tile = jnp.maximum(tile, final_box[sender, plane * slots + (slot ^ sender)])
                found.append(tile)
        totals = histogram(found)
        for slot in range(slots):
            totals = totals + final_box[slot, 2 * slots]
        totals = totals / doc_total

        def finish(targets):
            for slot in targets:
                packets[slot, 0] = found[slots + slot]
                packets[slot, 1] = totals
                for plane in (3, 2, 1):
                    packet(slot, plane).start()

        pl.when(row == 1)(lambda: finish((1,)))
        pl.when(row != 0)(lambda: finish((0,)))
        out_ref[0] = found[0]
        out_ref[1] = totals
        sent(block_label(2, 1), whole(2, 1))
        plane_sent()
        sent(*[final_copy(slot) for slot in range(1, slots)], answer_copy(2), answer_copy(3))

        def finished(targets):
            sent(*[packet(slot, plane) for slot in targets for plane in (3, 2, 1)])

        pl.when(row == 1)(lambda: finished((1,)))
        pl.when(row != 0)(lambda: finished((0,)))


def meet_shards(embeddings, document_cluster_index):
    rows, cols = lax.axis_size("rows"), lax.axis_size("cols")
    docs, width = embeddings.shape
    slots = rows * CORES
    hbm, vmem = pl.BlockSpec(memory_space=pl.ANY), pl.BlockSpec(memory_space=pltpu.VMEM)
    dma = pltpu.SemaphoreType.DMA
    line = lambda *lead: pltpu.VMEM((*lead, 1, docs), jnp.float32)
    found = pl.pallas_call(
        functools.partial(meet_kernel, docs * rows * cols),
        out_shape=pltpu.VMEM((2, 1, docs), jnp.float32),
        in_specs=[hbm, hbm],
        out_specs=vmem,
        scratch_shapes=[
            pltpu.VMEM((docs, width), jnp.bfloat16),
            pltpu.VMEM((1, docs), jnp.int32),
            pltpu.VMEM((slots * docs, width), jnp.bfloat16),
            pltpu.VMEM((3, docs, width), jnp.bfloat16),
            line(slots),
            line(3),
            pltpu.VMEM((slots, docs, docs), jnp.float32),
            pltpu.VMEM((slots, docs, docs), jnp.float32),
            line(slots + 3),
            line(slots + 7),
            line(2 * slots + 1),
            line(slots, 2 * slots + 1),
            line(2),
            line(2, 2),
            line(2),
            dma((2,)),
            dma((2, 10)),
            dma((2, 2, len(CHUNKS))),
            dma((2, 3)),
            dma((2, 9)),
            dma((2, 4)),
            dma((2, slots)),
            dma((2, 2)),
            dma((2, 2, 4)),
        ],
        compiler_params=pltpu.CompilerParams(collective_id=0, has_side_effects=True),
    )(embeddings, document_cluster_index.reshape(1, docs))
    return found[0, 0], found[1, 0]


def solution(mesh):
    placed = (P(("rows", "cols"), None), P(("rows", "cols")))
    rows, planes = mesh.shape["rows"], mesh.shape["cols"] // CORES
    direct = rows == 4 and planes == rows
    return jax.shard_map(
        meet_shards if direct else shards, mesh=mesh, in_specs=placed,
        out_specs=(P(("rows", "cols")), P()), check_vma=False
    )
```

```python
import functools

import jax
import jax.numpy as jnp
from jax import lax
from jax.experimental import pallas as pl
from jax.experimental.pallas import tpu as pltpu
from jax.sharding import PartitionSpec as P

CAP = 64
GROUP_CLUSTERS = 16
BINS = 128
CORES = 2


def from_partner(value, axis, bit):
    mask = 2**bit
    pairs = [(source, source ^ mask) for source in range(lax.axis_size(axis))]
    return lax.ppermute(value, axis, pairs)


def rank_among_equals(keys):
    places = jnp.arange(keys.shape[0], dtype=jnp.int32)
    earlier_equal = (keys[:, None] == keys[None, :]) & (places[None, :] < places[:, None])
    return jnp.sum(earlier_equal.astype(jnp.int32), axis=1)


def shards(embeddings, document_cluster_index):
    row_count = lax.axis_size("rows")
    col_count = lax.axis_size("cols")
    doc_count = embeddings.shape[0]
    width = embeddings.shape[1]
    slot_count = CAP * row_count
    values = embeddings.astype(jnp.float32)
    normed = (values * lax.rsqrt(jnp.sum(values * values, axis=1, keepdims=True) + 1e-06)).astype(
        jnp.bfloat16
    )
    owner_devices = document_cluster_index // GROUP_CLUSTERS
    within_cluster = (document_cluster_index % GROUP_CLUSTERS).astype(jnp.float32)
    slot_ranks = rank_among_equals(owner_devices)
    places = owner_devices * CAP + slot_ranks
    outgoing = jnp.zeros((slot_count, width), jnp.bfloat16).at[places].set(normed)
    out_labels = (
        jnp.full((slot_count,), -1.0, jnp.float32)
        .at[places]
        .set(within_cluster)
        .astype(jnp.bfloat16)
    )
    resident, res_labels = (
        lax.all_to_all(outgoing, "rows", split_axis=0, concat_axis=0, tiled=True),
        lax.all_to_all(out_labels, "rows", split_axis=0, concat_axis=0, tiled=True),
    )
    home_labels = res_labels.astype(jnp.float32)
    partner_count = max(1, col_count // GROUP_CLUSTERS)
    owned_count = max(1, GROUP_CLUSTERS // col_count)
    slot_quota = 2 * slot_count // GROUP_CLUSTERS // partner_count
    send_total = col_count * owned_count * slot_quota
    local_cluster = res_labels.astype(jnp.int32)
    occupied = local_cluster >= 0
    cluster_rank = rank_among_equals(local_cluster)
    member_slot = cluster_rank % partner_count
    cluster_depth = cluster_rank // partner_count
    destination = local_cluster // owned_count * partner_count + member_slot
    send_place = (
        destination * (owned_count * slot_quota)
        + local_cluster % owned_count * slot_quota
        + cluster_depth
    )
    send_place = jnp.where(occupied, send_place, send_total)
    send_rows = (
        jnp.zeros((send_total, width), jnp.bfloat16).at[send_place].set(resident, mode="drop")
    )
    send_labels = (
        jnp.full((send_total,), -1.0, jnp.float32)
        .at[send_place]
        .set(home_labels, mode="drop")
        .astype(jnp.bfloat16)
    )
    got_rows, got_labels = (
        lax.all_to_all(send_rows, "cols", split_axis=0, concat_axis=0, tiled=True),
        lax.all_to_all(send_labels, "cols", split_axis=0, concat_axis=0, tiled=True),
    )
    member_index = lax.axis_index("cols") % partner_count
    gathered_rows, gathered_labels = (got_rows, got_labels)
    for bit in range(partner_count.bit_length() - 1):
        other_rows, other_labels = from_partner((gathered_rows, gathered_labels), "cols", bit)
        upper = member_index // 2**bit % 2 == 1
        gathered_rows = jnp.where(
            upper,
            jnp.concatenate([other_rows, gathered_rows], axis=0),
            jnp.concatenate([gathered_rows, other_rows], axis=0),
        )
        gathered_labels = jnp.where(
            upper,
            jnp.concatenate([other_labels, gathered_labels], axis=0),
            jnp.concatenate([gathered_labels, other_labels], axis=0),
        )
    similarity_scores = lax.dot_general(
        got_rows, gathered_rows, (((1,), (1,)), ((), ())), preferred_element_type=jnp.float32
    )
    own_labels = got_labels.astype(jnp.float32)
    all_labels = gathered_labels.astype(jnp.float32)
    column_index = jnp.arange(gathered_rows.shape[0], dtype=jnp.int32)
    own_index = member_index * send_total + jnp.arange(send_total, dtype=jnp.int32)
    same_cluster = (own_labels[:, None] == all_labels[None, :]) & (own_labels[:, None] >= 0.0)
    same_cluster = same_cluster & (own_index[:, None] != column_index[None, :])
    best_owned = jnp.max(jnp.where(same_cluster, similarity_scores, -1.0), axis=1)
    came_back = lax.all_to_all(best_owned, "cols", split_axis=0, concat_axis=0, tiled=True)
    row_best = jnp.where(occupied, came_back[jnp.minimum(send_place, send_total - 1)], -1.0)
    answers = lax.all_to_all(row_best, "rows", split_axis=0, concat_axis=0, tiled=True)
    max_similarity = answers[places]
    bin_width = 2.0 / (BINS - 1)
    centers = -1.0 + jnp.arange(BINS, dtype=jnp.float32) * bin_width
    bin_weights = jax.nn.relu(1.0 - jnp.abs(max_similarity[:, None] - centers[None, :]) / bin_width)
    bin_totals = lax.psum(jnp.sum(bin_weights, axis=0), ("rows", "cols"))
    return (max_similarity, bin_totals / (doc_count * row_count * col_count))


CHUNKS = (16, 32, 32, 32, 16)


def meet_kernel(doc_total, emb_hbm, cluster_hbm, out_ref, emb_ref, cluster_ref, keys, blocks, key_labels,
                block_labels, label_columns, key_best, row_best, above, final_send, final_box, final_best, answer_send,
                packets, answer_box, in_sems, plane_sems, chunk_sems, block_sems, label_sems, partial_sems, final_sems,
                answer_sems, packet_sems):
    row, col = lax.axis_index("rows"), lax.axis_index("cols")
    z, core = col // CORES, col % CORES
    row_at = (row, row + 1 - 2 * (row % 2), row + 2 - 4 * (row // 2), 3 - row)
    core_at = (core, 1 - core)
    near = len(row_at)
    slots = near * CORES
    docs, width = emb_ref.shape
    half = docs // 2

    def at_slot(slot, plane):
        return (row_at[slot % near], plane * CORES + core_at[slot // near])

    def above_me(plane):
        return (row, plane * CORES + core)

    me = core * near + row

    def order_of(slot):
        return core_at[slot // near] * near + row_at[slot % near]

    x_peer, y_peer, core_peer = at_slot(1, z), at_slot(2, z), at_slot(near, z)

    def copy(source, target, sems, at, where):
        return pltpu.make_async_remote_copy(
            src_ref=source, dst_ref=target, send_sem=sems.at[(0, *at)], recv_sem=sems.at[(1, *at)],
            device_id=where, device_id_type=pl.DeviceIdType.MESH)

    barrier = pltpu.get_barrier_semaphore()

    def greet(where):
        pl.semaphore_signal(barrier, inc=1, device_id=where, device_id_type=pl.DeviceIdType.MESH)

    senders = {0: (1, 2, 3), 1: (0, 2, 3), 2: (3,), 3: (2,)}
    for plane, sources in senders.items():
        @pl.when(z == plane)
        def _():
            for source in sources:
                greet(above_me(source))
    for peer in (x_peer, y_peer, core_peer):
        greet(peer)
    load = pltpu.make_async_copy(emb_hbm, emb_ref, in_sems.at[0])
    load_labels = pltpu.make_async_copy(cluster_hbm, cluster_ref, in_sems.at[1])
    load.start()
    load_labels.start()
    load_labels.wait()
    key_labels[0] = cluster_ref[...].astype(jnp.float32)
    load.wait()
    values = emb_ref[...].astype(jnp.float32)
    normed = values * lax.rsqrt(jnp.sum(values * values, axis=1, keepdims=True) + 1e-06)
    keys[0:docs, :] = normed.astype(jnp.bfloat16)
    for plane in senders:
        @pl.when(z == plane)
        def _():
            pl.semaphore_wait(barrier, 3 + sum(plane in sources for sources in senders.values()))

    def part(slot, first, size):
        return keys.at[pl.ds(slot * docs + first, size)]

    def plane_copy(n):
        source, target, first, size, where = (
            (0, 1, 0, half, x_peer),
            (0, 2, half, half, y_peer),
            (0, 1, half, half, x_peer),
            (0, 2, 0, half, y_peer),
            (1, 3, 0, half, y_peer),
            (2, 3, half, half, x_peer),
            (0, 4, 0, docs, core_peer),
            (1, 5, 0, docs, core_peer),
            (2, 6, 0, docs, core_peer),
            (3, 7, 0, docs, core_peer),
        )[n]
        return copy(part(source, first, size), part(target, first, size), plane_sems, (n,), where)

    def plane_label(n):
        source, target, count, where = ((0, 1, 1, x_peer), (0, 2, 1, y_peer), (1, 3, 1, y_peer), (0, near, near, core_peer))[n]
        return copy(key_labels.at[pl.ds(source, count)], key_labels.at[pl.ds(target, count)], label_sems, (n,), where)

    def start(*copies):
        for item in copies:
            item.start()

    def arrive(*copies):
        for item in copies:
            item.wait_recv()

    def sent(*copies):
        for item in copies:
            item.wait_send()

    firsts = [sum(CHUNKS[:i]) for i in range(len(CHUNKS))]

    def chunk(n, i, source, plane):
        rows = pl.ds(firsts[i], CHUNKS[i])
        block = blocks.at[n, rows]
        return copy(keys.at[rows] if source is None else block, block, chunk_sems, (n, i), above_me(plane))

    def whole(n, plane):
        return copy(keys.at[pl.ds(0, docs)], blocks.at[n], block_sems, (n,), above_me(plane))

    def block_label(n, plane):
        return copy(key_labels.at[0], block_labels.at[n], label_sems, (4 + n,), above_me(plane))

    def swap(plane):
        block = blocks.at[2]
        return copy(keys.at[pl.ds(0, docs)], block, block_sems, (0,), above_me(plane))

    def swap_label(plane):
        return copy(key_labels.at[0], block_labels.at[2], label_sems, (8,), above_me(plane))

    def both_labels(plane):
        pair = block_labels.at[pl.ds(0, 2)]
        return copy(pair, pair, label_sems, (7,), above_me(plane))

    def plane_start():
        start(plane_label(0), plane_label(1), plane_copy(0), plane_copy(1), plane_copy(2), plane_copy(3), plane_copy(6))

    def plane_diagonal():
        arrive(plane_copy(0))
        start(plane_copy(4))
        arrive(plane_copy(1))
        start(plane_copy(5))
        arrive(plane_label(0))
        start(plane_label(2))

    def plane_across():
        arrive(plane_copy(2))
        start(plane_copy(7))
        arrive(plane_copy(3))
        start(plane_copy(8))

    def plane_last():
        arrive(plane_copy(4), plane_copy(5))
        start(plane_copy(9))
        arrive(plane_label(1), plane_label(2))
        start(plane_label(3))

    def plane_ready():
        arrive(plane_label(3))
        for slot in range(slots):
            label_columns[slot] = jnp.broadcast_to(key_labels[slot], (docs, docs)).T
        arrive(*[plane_copy(n) for n in range(6, 10)])

    def plane_sent():
        sent(*[plane_copy(n) for n in range(10)], *[plane_label(n) for n in range(4)])

    same_place = lax.broadcasted_iota(jnp.int32, (docs, docs), 0) == lax.broadcasted_iota(jnp.int32, (docs, docs), 1)

    def score(queries, labels, own, fresh=True, keep=True):
        parts = len(queries)
        query = queries[0] if parts == 1 else jnp.concatenate(queries, axis=0)
        scores = lax.dot_general(keys[...], query, (((1,), (1,)), ((), ())), preferred_element_type=jnp.float32)
        tops = [jnp.full((8, docs), -1.0, jnp.float32) for _ in queries]
        for slot in range(slots):
            both = None
            for n in range(parts):
                same = label_columns[slot] == labels[n]
                if own and n == 0 and slot == 0:
                    same = same & jnp.logical_not(same_place)
                found = jnp.where(same, scores[slot * docs:(slot + 1) * docs, n * docs:(n + 1) * docs], -1.0)
                tops[n] = jnp.maximum(tops[n], jnp.max(found.reshape(docs // 8, 8, docs), axis=0))
                both = found if both is None else jnp.maximum(both, found)
            if keep:
                key_best[slot] = both if fresh else jnp.maximum(key_best[slot], both)
        return [jnp.max(top, axis=0, keepdims=True) for top in tops]

    def best_of_keys(slot):
        return jnp.max(key_best[slot].T, axis=0, keepdims=True)

    bin_width = 2.0 / (BINS - 1)
    centers = -1.0 + lax.broadcasted_iota(jnp.int32, (BINS, docs), 0).astype(jnp.float32) * bin_width

    def histogram(tiles):
        weights = sum(jnp.maximum(1.0 - jnp.abs(tile - centers) * ((BINS - 1) / 2.0), 0.0) for tile in tiles)
        return jnp.sum(weights.T, axis=0, keepdims=True)

    spans = {1: (0, slots + 3), 2: (slots + 3, 2), 3: (slots + 5, 2)}

    def partials(plane):
        first, count = spans[plane]
        return copy(row_best.at[pl.ds(0, count)], above.at[pl.ds(first, count)], partial_sems, (plane,), above_me(0))

    def final_copy(to, source):
        return pltpu.make_async_remote_copy(
            src_ref=final_send, dst_ref=final_box.at[source], send_sem=final_sems.at[0, to], recv_sem=final_sems.at[1, source],
            device_id=(to % near, z * CORES + to // near), device_id_type=pl.DeviceIdType.MESH)

    def with_others(act):
        for other in range(slots):
            pl.when(other != me)(functools.partial(act, other))

    def answer_copy(plane):
        return copy(answer_send.at[plane - 2], answer_box.at[0], answer_sems, (plane - 2,), above_me(plane))

    def packet(slot, plane):
        first = 0 if plane == 1 else 1
        rows = pl.ds(first, 2 - first)
        return copy(packets.at[slot, rows], answer_box.at[rows], packet_sems, (slot, plane), at_slot(slot, plane))

    def take_answer(plane):
        if plane > 1:
            arrive(answer_copy(plane))

        def take(slot):
            arrive(packet(slot, plane))

        pl.when(row == 0)(lambda: take(1))
        pl.when(row != 0)(lambda: take(0))
        out_ref[...] = answer_box[...]

    every = range(len(CHUNKS))

    for plane in (2, 3):
        @pl.when(z == plane)
        def _():
            other, n = 5 - plane, plane - 2
            down = [block_label(n, 1), *[chunk(n, i, None, 1) for i in every]]
            aside = [swap_label(other), swap(other)]
            start(*(aside + down if plane == 2 else down + aside))
            plane_start()
            plane_diagonal()
            plane_across()
            plane_last()
            plane_ready()
            arrive(swap_label(plane), swap(plane))
            row_best[0], row_best[1] = score([keys[0:docs, :], blocks[2]], [key_labels[0], block_labels[2]], True, keep=False)
            start(partials(plane))
            sent(*down, *aside)
            plane_sent()
            sent(partials(plane))
            take_answer(plane)

    @pl.when(z == 1)
    def _():
        plane_start()
        arrivals = [(n, i) for n in (1, 0) for i in every]

        def forward(first, last):
            for n, i in arrivals[first:last]:
                arrive(chunk(n, i, n, 0))
                start(chunk(n, i, n, 0))

        forward(0, 1)
        plane_diagonal()
        forward(1, 4)
        plane_across()
        forward(4, 6)
        arrive(block_label(0, 1), block_label(1, 1))
        start(both_labels(0))
        plane_last()
        forward(6, 8)
        plane_ready()
        arrive(block_label(2, 1), whole(2, 1))
        mine, row_best[slots] = score([keys[0:docs, :], blocks[2]], [key_labels[0], block_labels[2]], True)
        forward(8, len(arrivals))
        row_best[slots + 1], row_best[slots + 2] = score(
            [blocks[0], blocks[1]], [block_labels[0], block_labels[1]], False, fresh=False)
        for slot in range(slots):
            row_best[slot] = best_of_keys(slot) if slot else jnp.maximum(mine, best_of_keys(0))
        start(partials(1))
        sent(both_labels(0), *[chunk(n, i, n, 0) for n, i in arrivals])
        plane_sent()
        sent(partials(1))
        take_answer(1)

    @pl.when(z == 0)
    def _():
        start(block_label(2, 1), whole(2, 1))
        plane_start()
        plane_diagonal()
        plane_across()
        plane_last()
        plane_ready()
        mine = score([keys[0:docs, :]], [key_labels[0]], True)[0]
        arrive(both_labels(0))
        for n in (1, 0):
            arrive(*[chunk(n, i, n, 0) for i in every])
        second, third = score([blocks[0], blocks[1]], [block_labels[0], block_labels[1]], False, fresh=False)
        for slot in range(1, slots):
            final_send[pl.ds(order_of(slot), 1), :] = best_of_keys(slot)
        mine = jnp.maximum(mine, best_of_keys(0))
        arrive(partials(2), partials(3), partials(1))
        second = jnp.maximum(jnp.maximum(second, above[slots + 1]), jnp.maximum(above[slots + 3], above[slots + 6]))
        third = jnp.maximum(jnp.maximum(third, above[slots + 2]), jnp.maximum(above[slots + 4], above[slots + 5]))
        final_send[pl.ds(me, 1), :] = jnp.maximum(mine, above[slots])
        for slot in range(slots):
            final_send[pl.ds(slots + order_of(slot), 1), :] = above[slot]
        final_send[2 * slots:2 * slots + 1, :] = histogram([second, third])
        with_others(lambda other: final_copy(other, me).start())
        for plane, found in ((2, second), (3, third)):
            answer_send[plane - 2] = found
            answer_copy(plane).start()
        final_box[pl.ds(me, 1)] = final_send[...].reshape(1, 2 * slots + 1, docs)
        sent(block_label(2, 1), whole(2, 1))
        plane_sent()
        with_others(lambda other: final_copy(other, other).wait_recv())
        found = jnp.max(final_box[:, :2 * slots, :], axis=0)
        final_best[...] = found
        totals = histogram([found[n:n + 1] for n in range(2 * slots)])
        totals = (totals + jnp.sum(final_box[:, 2 * slots, :], axis=0, keepdims=True)) / doc_total
        out_ref[0] = final_best[pl.ds(me, 1), :]
        out_ref[1] = totals

        def finish(targets):
            for slot in targets:
                packets[slot, 0] = final_best[pl.ds(slots + order_of(slot), 1), :]
                packets[slot, 1] = totals
                for plane in (3, 2, 1):
                    packet(slot, plane).start()

        pl.when(row == 1)(lambda: finish((1,)))
        pl.when(row != 0)(lambda: finish((0,)))
        with_others(lambda other: final_copy(other, other).wait_send())
        sent(answer_copy(2), answer_copy(3))

        def finished(targets):
            sent(*[packet(slot, plane) for slot in targets for plane in (3, 2, 1)])

        pl.when(row == 1)(lambda: finished((1,)))
        pl.when(row != 0)(lambda: finished((0,)))


def meet_shards(embeddings, document_cluster_index):
    rows, cols = lax.axis_size("rows"), lax.axis_size("cols")
    docs, width = embeddings.shape
    slots = rows * CORES
    hbm, vmem = pl.BlockSpec(memory_space=pl.ANY), pl.BlockSpec(memory_space=pltpu.VMEM)
    dma = pltpu.SemaphoreType.DMA
    line = lambda *lead: pltpu.VMEM((*lead, 1, docs), jnp.float32)
    found = pl.pallas_call(
        functools.partial(meet_kernel, docs * rows * cols),
        out_shape=pltpu.VMEM((2, 1, docs), jnp.float32),
        in_specs=[hbm, hbm],
        out_specs=vmem,
        scratch_shapes=[
            pltpu.VMEM((docs, width), jnp.bfloat16),
            pltpu.VMEM((1, docs), jnp.int32),
            pltpu.VMEM((slots * docs, width), jnp.bfloat16),
            pltpu.VMEM((3, docs, width), jnp.bfloat16),
            line(slots),
            line(3),
            pltpu.VMEM((slots, docs, docs), jnp.float32),
            pltpu.VMEM((slots, docs, docs), jnp.float32),
            line(slots + 3),
            line(slots + 7),
            pltpu.VMEM((2 * slots + 1, docs), jnp.float32),
            pltpu.VMEM((slots, 2 * slots + 1, docs), jnp.float32),
            pltpu.VMEM((2 * slots, docs), jnp.float32),
            line(2),
            line(2, 2),
            line(2),
            dma((2,)),
            dma((2, 10)),
            dma((2, 2, len(CHUNKS))),
            dma((2, 3)),
            dma((2, 9)),
            dma((2, 4)),
            dma((2, slots)),
            dma((2, 2)),
            dma((2, 2, 4)),
        ],
        compiler_params=pltpu.CompilerParams(collective_id=0, has_side_effects=True),
    )(embeddings, document_cluster_index.reshape(1, docs))
    return found[0, 0], found[1, 0]


def solution(mesh):
    placed = (P(("rows", "cols"), None), P(("rows", "cols")))
    rows, planes = mesh.shape["rows"], mesh.shape["cols"] // CORES
    direct = rows == 4 and planes == rows
    return jax.shard_map(
        meet_shards if direct else shards, mesh=mesh, in_specs=placed,
        out_specs=(P(("rows", "cols")), P()), check_vma=False
    )
```

```python
import functools

import jax
import jax.numpy as jnp
from jax import lax
from jax.experimental import pallas as pl
from jax.experimental.pallas import tpu as pltpu
from jax.sharding import PartitionSpec as P

CAP = 64
GROUP_CLUSTERS = 16
BINS = 128
CORES = 2


def from_partner(value, axis, bit):
    mask = 2**bit
    pairs = [(source, source ^ mask) for source in range(lax.axis_size(axis))]
    return lax.ppermute(value, axis, pairs)


def rank_among_equals(keys):
    places = jnp.arange(keys.shape[0], dtype=jnp.int32)
    earlier_equal = (keys[:, None] == keys[None, :]) & (places[None, :] < places[:, None])
    return jnp.sum(earlier_equal.astype(jnp.int32), axis=1)


def shards(embeddings, document_cluster_index):
    row_count = lax.axis_size("rows")
    col_count = lax.axis_size("cols")
    doc_count = embeddings.shape[0]
    width = embeddings.shape[1]
    slot_count = CAP * row_count
    values = embeddings.astype(jnp.float32)
    normed = (values * lax.rsqrt(jnp.sum(values * values, axis=1, keepdims=True) + 1e-06)).astype(
        jnp.bfloat16
    )
    owner_devices = document_cluster_index // GROUP_CLUSTERS
    within_cluster = (document_cluster_index % GROUP_CLUSTERS).astype(jnp.float32)
    slot_ranks = rank_among_equals(owner_devices)
    places = owner_devices * CAP + slot_ranks
    outgoing = jnp.zeros((slot_count, width), jnp.bfloat16).at[places].set(normed)
    out_labels = (
        jnp.full((slot_count,), -1.0, jnp.float32)
        .at[places]
        .set(within_cluster)
        .astype(jnp.bfloat16)
    )
    resident, res_labels = (
        lax.all_to_all(outgoing, "rows", split_axis=0, concat_axis=0, tiled=True),
        lax.all_to_all(out_labels, "rows", split_axis=0, concat_axis=0, tiled=True),
    )
    home_labels = res_labels.astype(jnp.float32)
    partner_count = max(1, col_count // GROUP_CLUSTERS)
    owned_count = max(1, GROUP_CLUSTERS // col_count)
    slot_quota = 2 * slot_count // GROUP_CLUSTERS // partner_count
    send_total = col_count * owned_count * slot_quota
    local_cluster = res_labels.astype(jnp.int32)
    occupied = local_cluster >= 0
    cluster_rank = rank_among_equals(local_cluster)
    member_slot = cluster_rank % partner_count
    cluster_depth = cluster_rank // partner_count
    destination = local_cluster // owned_count * partner_count + member_slot
    send_place = (
        destination * (owned_count * slot_quota)
        + local_cluster % owned_count * slot_quota
        + cluster_depth
    )
    send_place = jnp.where(occupied, send_place, send_total)
    send_rows = (
        jnp.zeros((send_total, width), jnp.bfloat16).at[send_place].set(resident, mode="drop")
    )
    send_labels = (
        jnp.full((send_total,), -1.0, jnp.float32)
        .at[send_place]
        .set(home_labels, mode="drop")
        .astype(jnp.bfloat16)
    )
    got_rows, got_labels = (
        lax.all_to_all(send_rows, "cols", split_axis=0, concat_axis=0, tiled=True),
        lax.all_to_all(send_labels, "cols", split_axis=0, concat_axis=0, tiled=True),
    )
    member_index = lax.axis_index("cols") % partner_count
    gathered_rows, gathered_labels = (got_rows, got_labels)
    for bit in range(partner_count.bit_length() - 1):
        other_rows, other_labels = from_partner((gathered_rows, gathered_labels), "cols", bit)
        upper = member_index // 2**bit % 2 == 1
        gathered_rows = jnp.where(
            upper,
            jnp.concatenate([other_rows, gathered_rows], axis=0),
            jnp.concatenate([gathered_rows, other_rows], axis=0),
        )
        gathered_labels = jnp.where(
            upper,
            jnp.concatenate([other_labels, gathered_labels], axis=0),
            jnp.concatenate([gathered_labels, other_labels], axis=0),
        )
    similarity_scores = lax.dot_general(
        got_rows, gathered_rows, (((1,), (1,)), ((), ())), preferred_element_type=jnp.float32
    )
    own_labels = got_labels.astype(jnp.float32)
    all_labels = gathered_labels.astype(jnp.float32)
    column_index = jnp.arange(gathered_rows.shape[0], dtype=jnp.int32)
    own_index = member_index * send_total + jnp.arange(send_total, dtype=jnp.int32)
    same_cluster = (own_labels[:, None] == all_labels[None, :]) & (own_labels[:, None] >= 0.0)
    same_cluster = same_cluster & (own_index[:, None] != column_index[None, :])
    best_owned = jnp.max(jnp.where(same_cluster, similarity_scores, -1.0), axis=1)
    came_back = lax.all_to_all(best_owned, "cols", split_axis=0, concat_axis=0, tiled=True)
    row_best = jnp.where(occupied, came_back[jnp.minimum(send_place, send_total - 1)], -1.0)
    answers = lax.all_to_all(row_best, "rows", split_axis=0, concat_axis=0, tiled=True)
    max_similarity = answers[places]
    bin_width = 2.0 / (BINS - 1)
    centers = -1.0 + jnp.arange(BINS, dtype=jnp.float32) * bin_width
    bin_weights = jax.nn.relu(1.0 - jnp.abs(max_similarity[:, None] - centers[None, :]) / bin_width)
    bin_totals = lax.psum(jnp.sum(bin_weights, axis=0), ("rows", "cols"))
    return (max_similarity, bin_totals / (doc_count * row_count * col_count))


CHUNKS = (32, 32, 32, 16, 16)
TWICE = 1


def meet_kernel(doc_total, emb_hbm, cluster_hbm, out_ref, emb_ref, cluster_ref, keys, blocks, key_labels,
                block_labels, label_columns, key_best, row_best, above, final_send, final_box, side_box, final_best,
                packets, answer_box, in_sems, plane_sems, chunk_sems, twice_sems, block_sems, label_sems, partial_sems, final_sems,
                side_sems, packet_sems):
    row, col = lax.axis_index("rows"), lax.axis_index("cols")
    z, core = col // CORES, col % CORES
    row_at = (row, row + 1 - 2 * (row % 2), row + 2 - 4 * (row // 2), 3 - row)
    core_at = (core, 1 - core)
    near = len(row_at)
    slots = near * CORES
    docs, width = emb_ref.shape
    half = docs // 2

    def at_slot(slot, plane):
        return (row_at[slot % near], plane * CORES + core_at[slot // near])

    def above_me(plane):
        return (row, plane * CORES + core)

    me = core * near + row

    def order_of(slot):
        return core_at[slot // near] * near + row_at[slot % near]

    x_peer, y_peer, core_peer = at_slot(1, z), at_slot(2, z), at_slot(near, z)

    def copy(source, target, sems, at, where):
        return pltpu.make_async_remote_copy(
            src_ref=source, dst_ref=target, send_sem=sems.at[(0, *at)], recv_sem=sems.at[(1, *at)],
            device_id=where, device_id_type=pl.DeviceIdType.MESH)

    barrier = pltpu.get_barrier_semaphore()

    def greet(where):
        pl.semaphore_signal(barrier, inc=1, device_id=where, device_id_type=pl.DeviceIdType.MESH)

    senders = {0: (1, 2, 3), 1: (0, 2), 2: (3,), 3: (2,)}
    for plane, sources in senders.items():
        @pl.when(z == plane)
        def _():
            for source in sources:
                greet(above_me(source))
    for peer in (x_peer, y_peer, core_peer):
        greet(peer)
    load = pltpu.make_async_copy(emb_hbm, emb_ref, in_sems.at[0])
    load_labels = pltpu.make_async_copy(cluster_hbm, cluster_ref, in_sems.at[1])
    load.start()
    load_labels.start()
    load_labels.wait()
    key_labels[0] = cluster_ref[...].astype(jnp.float32)
    load.wait()
    values = emb_ref[...].astype(jnp.float32)
    normed = values * lax.rsqrt(jnp.sum(values * values, axis=1, keepdims=True) + 1e-06)
    keys[0:docs, :] = normed.astype(jnp.bfloat16)
    for plane in senders:
        @pl.when(z == plane)
        def _():
            pl.semaphore_wait(barrier, 3 + sum(plane in sources for sources in senders.values()))

    def part(slot, first, size):
        return keys.at[pl.ds(slot * docs + first, size)]

    def plane_copy(n):
        source, target, first, size, where = (
            (0, 1, 0, half, x_peer),
            (0, 2, half, half, y_peer),
            (0, 1, half, half, x_peer),
            (0, 2, 0, half, y_peer),
            (1, 3, 0, half, y_peer),
            (2, 3, half, half, x_peer),
            (0, 4, 0, docs, core_peer),
            (1, 5, 0, docs, core_peer),
            (2, 6, 0, docs, core_peer),
            (3, 7, 0, docs, core_peer),
        )[n]
        return copy(part(source, first, size), part(target, first, size), plane_sems, (n,), where)

    def plane_label(n):
        source, target, count, where = ((0, 1, 1, x_peer), (0, 2, 1, y_peer), (1, 3, 1, y_peer), (0, near, near, core_peer))[n]
        return copy(key_labels.at[pl.ds(source, count)], key_labels.at[pl.ds(target, count)], label_sems, (n,), where)

    def start(*copies):
        for item in copies:
            item.start()

    def arrive(*copies):
        for item in copies:
            item.wait_recv()

    def sent(*copies):
        for item in copies:
            item.wait_send()

    firsts = [sum(CHUNKS[:i]) for i in range(len(CHUNKS))]

    def chunk(n, i, source, plane):
        rows = pl.ds(firsts[i], CHUNKS[i])
        block = blocks.at[n, rows]
        return copy(keys.at[rows] if source is None else block, block, chunk_sems, (n, i), above_me(plane))

    def twice(i):
        rows = pl.ds(firsts[i], CHUNKS[i])
        return copy(keys.at[rows], blocks.at[0, rows], twice_sems, (i,), above_me(0))

    def whole(n, plane):
        return copy(keys.at[pl.ds(0, docs)], blocks.at[2], block_sems, (n,), above_me(plane))

    def block_label(n, plane, at, source=None):
        held = block_labels.at[n]
        return copy(key_labels.at[0] if source is None else held, held, label_sems, (4 + at,), above_me(plane))

    def plane_start():
        start(plane_label(0), plane_label(1), plane_copy(0), plane_copy(1), plane_copy(2), plane_copy(3), plane_copy(6))

    def plane_diagonal():
        arrive(plane_copy(0))
        start(plane_copy(4))
        arrive(plane_copy(1))
        start(plane_copy(5))
        arrive(plane_label(0))
        start(plane_label(2))

    def plane_across():
        arrive(plane_copy(2))
        start(plane_copy(7))
        arrive(plane_copy(3))
        start(plane_copy(8))

    def plane_last():
        arrive(plane_copy(4), plane_copy(5))
        start(plane_copy(9))
        arrive(plane_label(1), plane_label(2))
        start(plane_label(3))

    def plane_ready():
        arrive(plane_label(3))
        for slot in range(slots):
            label_columns[slot] = jnp.broadcast_to(key_labels[slot], (docs, docs)).T
        arrive(*[plane_copy(n) for n in range(6, 10)])

    def plane_sent():
        sent(*[plane_copy(n) for n in range(10)], *[plane_label(n) for n in range(4)])

    same_place = lax.broadcasted_iota(jnp.int32, (docs, docs), 0) == lax.broadcasted_iota(jnp.int32, (docs, docs), 1)

    def score(queries, labels, own, fresh=True, keep=True):
        parts = len(queries)
        query = queries[0] if parts == 1 else jnp.concatenate(queries, axis=0)
        scores = lax.dot_general(keys[...], query, (((1,), (1,)), ((), ())), preferred_element_type=jnp.float32)
        tops = [jnp.full((8, docs), -1.0, jnp.float32) for _ in queries]
        for slot in range(slots):
            both = None
            for n in range(parts):
                same = label_columns[slot] == labels[n]
                if own and n == 0 and slot == 0:
                    same = same & jnp.logical_not(same_place)
                found = jnp.where(same, scores[slot * docs:(slot + 1) * docs, n * docs:(n + 1) * docs], -1.0)
                tops[n] = jnp.maximum(tops[n], jnp.max(found.reshape(docs // 8, 8, docs), axis=0))
                both = found if both is None else jnp.maximum(both, found)
            if keep:
                key_best[slot] = both if fresh else jnp.maximum(key_best[slot], both)
        return [jnp.max(top, axis=0, keepdims=True) for top in tops]

    def best_of_keys(slot):
        return jnp.max(key_best[slot].T, axis=0, keepdims=True)

    bins_per_unit = (BINS - 1) / 2.0
    centers = lax.broadcasted_iota(jnp.int32, (BINS, docs), 0).astype(jnp.float32) - bins_per_unit

    def histogram(rows):
        scaled = rows * bins_per_unit
        weights = sum(jnp.maximum(1.0 - jnp.abs(scaled[n:n + 1] - centers), 0.0) for n in range(rows.shape[0]))
        return jnp.sum(weights.T, axis=0, keepdims=True)

    spans = {1: (0, 1), 2: (1, 2), 3: (3, 2)}

    def partials(plane):
        first, count = spans[plane]
        return copy(row_best.at[pl.ds(0, count)], above.at[pl.ds(first, count)], partial_sems, (plane,), above_me(0))

    def spread(box, sems, to, source):
        return pltpu.make_async_remote_copy(
            src_ref=final_send, dst_ref=box.at[source], send_sem=sems.at[0, to], recv_sem=sems.at[1, source],
            device_id=(to % near, to // near), device_id_type=pl.DeviceIdType.MESH)

    def final_copy(to, source):
        return spread(final_box, final_sems, to, source)

    def side_copy(to, source):
        return spread(side_box, side_sems, to, source)

    def keep_final(slot, best):
        final_send[pl.ds(order_of(slot), 1), :] = best

    def with_others(act):
        for other in range(slots):
            pl.when(other != me)(functools.partial(act, other))

    def packet(slot, plane):
        return copy(packets.at[slot, plane - 1], answer_box, packet_sems, (slot, plane), at_slot(slot, plane))

    def take_answer(plane):
        pl.when(row == 0)(lambda: arrive(packet(1, plane)))
        pl.when(row != 0)(lambda: arrive(packet(0, plane)))
        out_ref[...] = answer_box[...]

    every = range(len(CHUNKS))
    once, again = every[:len(CHUNKS) - TWICE], every[len(CHUNKS) - TWICE:]

    for plane in (2, 3):
        @pl.when(z == plane)
        def _():
            other = 5 - plane
            aside = [block_label(2, other, 4), whole(0, other)]
            if plane == 3:
                down = [block_label(1, 0, 2), *[chunk(1, i, None, 0) for i in every]] + aside
            else:
                down = [*aside, block_label(0, 1, 0), block_label(0, 0, 1), *[chunk(0, i, None, 1) for i in once],
                        *[twice(i) for i in again], *[chunk(0, i, None, 1) for i in again]]
            start(*down)
            plane_start()
            plane_diagonal()
            plane_across()
            plane_last()
            plane_ready()
            arrive(block_label(2, plane, 4), whole(0, plane))
            row_best[0], row_best[1] = score([keys[0:docs, :], blocks[2]], [key_labels[0], block_labels[2]], True, keep=False)
            start(partials(plane))
            sent(*down)
            plane_sent()
            sent(partials(plane))
            take_answer(plane)

    @pl.when(z == 1)
    def _():
        plane_start()

        def forward(*indices):
            for i in indices:
                arrive(chunk(0, i, 0, 0))
                start(chunk(0, i, 0, 0))

        plane_diagonal()
        plane_across()
        forward(*once[:2])
        plane_last()
        forward(*once[2:])
        plane_ready()
        arrive(block_label(2, 1, 5), whole(1, 1))
        mine, row_best[0] = score([keys[0:docs, :], blocks[2]], [key_labels[0], block_labels[2]], True)
        start(partials(1))
        arrive(block_label(0, 1, 0), block_label(1, 1, 3, 1), *[chunk(1, i, 1, 1) for i in every],
               *[chunk(0, i, 0, 0) for i in again])
        second, third = score([blocks[0], blocks[1]], [block_labels[0], block_labels[1]], False, fresh=False)
        final_send[slots:slots + 1, :] = second
        final_send[slots + 1:slots + 2, :] = third
        for slot in range(slots):
            keep_final(slot, best_of_keys(slot) if slot else jnp.maximum(mine, best_of_keys(0)))
        for other in range(slots):
            side_copy(other, me).start()
        sent(*[chunk(0, i, 0, 0) for i in once])
        plane_sent()
        sent(partials(1), *[side_copy(other, me) for other in range(slots)])
        take_answer(1)

    @pl.when(z == 0)
    def _():
        start(block_label(2, 1, 5), whole(1, 1))
        plane_start()

        def forward(*indices):
            for i in indices:
                arrive(chunk(1, i, 1, 1))
                start(chunk(1, i, 1, 1))

        plane_diagonal()
        forward(*every[:2])
        plane_across()
        forward(*every[2:])
        arrive(block_label(1, 0, 2))
        start(block_label(1, 1, 3, 1))
        plane_last()
        plane_ready()
        mine, third = score([keys[0:docs, :], blocks[1]], [key_labels[0], block_labels[1]], True)
        arrive(block_label(0, 0, 1), *[chunk(0, i, 0, 0) for i in once], *[twice(i) for i in again])
        second = score([blocks[0]], [block_labels[0]], False, fresh=False)[0]
        for slot in range(1, slots):
            keep_final(slot, best_of_keys(slot))
        mine = jnp.maximum(mine, best_of_keys(0))
        arrive(partials(1), partials(3), partials(2))
        keep_final(0, jnp.maximum(mine, above[0]))
        final_send[slots:slots + 1, :] = jnp.maximum(second, jnp.maximum(above[1], above[4]))
        final_send[slots + 1:slots + 2, :] = jnp.maximum(third, jnp.maximum(above[2], above[3]))
        with_others(lambda other: final_copy(other, me).start())
        final_box[pl.ds(me, 1)] = final_send[...].reshape(1, slots + 2, docs)
        sent(block_label(2, 1, 5), whole(1, 1), block_label(1, 1, 3, 1), *[chunk(1, i, 1, 1) for i in every])
        plane_sent()
        arrive(*[side_copy(0, source) for source in range(slots)])
        final_best[1] = jnp.max(side_box[:, :slots, :], axis=0)
        totals = histogram(final_best[1])
        with_others(lambda other: final_copy(0, other).wait_recv())
        final_best[0] = jnp.max(final_box[:, :slots, :], axis=0)
        for plane in (2, 3):
            at = slots + plane - 2
            final_best[plane] = jnp.maximum(final_box[:, at, :], side_box[:, at, :])
        totals = totals + histogram(jnp.concatenate([final_best[plane] for plane in (0, 2, 3)], axis=0))
        totals = totals / doc_total
        out_ref[0] = final_best[0, pl.ds(me, 1), :]
        out_ref[1] = totals

        def finish(targets):
            for slot in targets:
                for plane in (1, 3, 2):
                    packets[slot, plane - 1, 0] = final_best[plane, pl.ds(order_of(slot), 1), :]
                    packets[slot, plane - 1, 1] = totals
                    packet(slot, plane).start()

        pl.when(row == 1)(lambda: finish((1,)))
        pl.when(row != 0)(lambda: finish((0,)))
        with_others(lambda other: final_copy(other, me).wait_send())

        def finished(targets):
            sent(*[packet(slot, plane) for slot in targets for plane in (3, 2, 1)])

        pl.when(row == 1)(lambda: finished((1,)))
        pl.when(row != 0)(lambda: finished((0,)))


def meet_shards(embeddings, document_cluster_index):
    rows, cols = lax.axis_size("rows"), lax.axis_size("cols")
    docs, width = embeddings.shape
    slots = rows * CORES
    hbm, vmem = pl.BlockSpec(memory_space=pl.ANY), pl.BlockSpec(memory_space=pltpu.VMEM)
    dma = pltpu.SemaphoreType.DMA
    line = lambda *lead: pltpu.VMEM((*lead, 1, docs), jnp.float32)
    found = pl.pallas_call(
        functools.partial(meet_kernel, docs * rows * cols),
        out_shape=pltpu.VMEM((2, 1, docs), jnp.float32),
        in_specs=[hbm, hbm],
        out_specs=vmem,
        scratch_shapes=[
            pltpu.VMEM((docs, width), jnp.bfloat16),
            pltpu.VMEM((1, docs), jnp.int32),
            pltpu.VMEM((slots * docs, width), jnp.bfloat16),
            pltpu.VMEM((3, docs, width), jnp.bfloat16),
            line(slots),
            line(3),
            pltpu.VMEM((slots, docs, docs), jnp.float32),
            pltpu.VMEM((slots, docs, docs), jnp.float32),
            line(2),
            line(5),
            pltpu.VMEM((slots + 2, docs), jnp.float32),
            pltpu.VMEM((slots, slots + 2, docs), jnp.float32),
            pltpu.VMEM((slots, slots + 2, docs), jnp.float32),
            pltpu.VMEM((4, slots, docs), jnp.float32),
            line(2, 3, 2),
            line(2),
            dma((2,)),
            dma((2, 10)),
            dma((2, 2, len(CHUNKS))),
            dma((2, len(CHUNKS))),
            dma((2, 2)),
            dma((2, 10)),
            dma((2, 4)),
            dma((2, slots)),
            dma((2, slots)),
            dma((2, 2, 4)),
        ],
        compiler_params=pltpu.CompilerParams(collective_id=0, has_side_effects=True),
    )(embeddings, document_cluster_index.reshape(1, docs))
    return found[0, 0], found[1, 0]


def solution(mesh):
    placed = (P(("rows", "cols"), None), P(("rows", "cols")))
    rows, planes = mesh.shape["rows"], mesh.shape["cols"] // CORES
    direct = rows == 4 and planes == rows
    return jax.shard_map(
        meet_shards if direct else shards, mesh=mesh, in_specs=placed,
        out_specs=(P(("rows", "cols")), P()), check_vma=False
    )
```

```python
import functools

import jax
import jax.numpy as jnp
from jax import lax
from jax.experimental import pallas as pl
from jax.experimental.pallas import tpu as pltpu
from jax.sharding import PartitionSpec as P

CAP = 64
GROUP_CLUSTERS = 16
BINS = 128
CORES = 2


def from_partner(value, axis, bit):
    mask = 2**bit
    pairs = [(source, source ^ mask) for source in range(lax.axis_size(axis))]
    return lax.ppermute(value, axis, pairs)


def rank_among_equals(keys):
    places = jnp.arange(keys.shape[0], dtype=jnp.int32)
    earlier_equal = (keys[:, None] == keys[None, :]) & (places[None, :] < places[:, None])
    return jnp.sum(earlier_equal.astype(jnp.int32), axis=1)


def shards(embeddings, document_cluster_index):
    row_count = lax.axis_size("rows")
    col_count = lax.axis_size("cols")
    doc_count = embeddings.shape[0]
    width = embeddings.shape[1]
    slot_count = CAP * row_count
    values = embeddings.astype(jnp.float32)
    normed = (values * lax.rsqrt(jnp.sum(values * values, axis=1, keepdims=True) + 1e-06)).astype(
        jnp.bfloat16
    )
    owner_devices = document_cluster_index // GROUP_CLUSTERS
    within_cluster = (document_cluster_index % GROUP_CLUSTERS).astype(jnp.float32)
    slot_ranks = rank_among_equals(owner_devices)
    places = owner_devices * CAP + slot_ranks
    outgoing = jnp.zeros((slot_count, width), jnp.bfloat16).at[places].set(normed)
    out_labels = (
        jnp.full((slot_count,), -1.0, jnp.float32)
        .at[places]
        .set(within_cluster)
        .astype(jnp.bfloat16)
    )
    resident, res_labels = (
        lax.all_to_all(outgoing, "rows", split_axis=0, concat_axis=0, tiled=True),
        lax.all_to_all(out_labels, "rows", split_axis=0, concat_axis=0, tiled=True),
    )
    home_labels = res_labels.astype(jnp.float32)
    partner_count = max(1, col_count // GROUP_CLUSTERS)
    owned_count = max(1, GROUP_CLUSTERS // col_count)
    slot_quota = 2 * slot_count // GROUP_CLUSTERS // partner_count
    send_total = col_count * owned_count * slot_quota
    local_cluster = res_labels.astype(jnp.int32)
    occupied = local_cluster >= 0
    cluster_rank = rank_among_equals(local_cluster)
    member_slot = cluster_rank % partner_count
    cluster_depth = cluster_rank // partner_count
    destination = local_cluster // owned_count * partner_count + member_slot
    send_place = (
        destination * (owned_count * slot_quota)
        + local_cluster % owned_count * slot_quota
        + cluster_depth
    )
    send_place = jnp.where(occupied, send_place, send_total)
    send_rows = (
        jnp.zeros((send_total, width), jnp.bfloat16).at[send_place].set(resident, mode="drop")
    )
    send_labels = (
        jnp.full((send_total,), -1.0, jnp.float32)
        .at[send_place]
        .set(home_labels, mode="drop")
        .astype(jnp.bfloat16)
    )
    got_rows, got_labels = (
        lax.all_to_all(send_rows, "cols", split_axis=0, concat_axis=0, tiled=True),
        lax.all_to_all(send_labels, "cols", split_axis=0, concat_axis=0, tiled=True),
    )
    member_index = lax.axis_index("cols") % partner_count
    gathered_rows, gathered_labels = (got_rows, got_labels)
    for bit in range(partner_count.bit_length() - 1):
        other_rows, other_labels = from_partner((gathered_rows, gathered_labels), "cols", bit)
        upper = member_index // 2**bit % 2 == 1
        gathered_rows = jnp.where(
            upper,
            jnp.concatenate([other_rows, gathered_rows], axis=0),
            jnp.concatenate([gathered_rows, other_rows], axis=0),
        )
        gathered_labels = jnp.where(
            upper,
            jnp.concatenate([other_labels, gathered_labels], axis=0),
            jnp.concatenate([gathered_labels, other_labels], axis=0),
        )
    similarity_scores = lax.dot_general(
        got_rows, gathered_rows, (((1,), (1,)), ((), ())), preferred_element_type=jnp.float32
    )
    own_labels = got_labels.astype(jnp.float32)
    all_labels = gathered_labels.astype(jnp.float32)
    column_index = jnp.arange(gathered_rows.shape[0], dtype=jnp.int32)
    own_index = member_index * send_total + jnp.arange(send_total, dtype=jnp.int32)
    same_cluster = (own_labels[:, None] == all_labels[None, :]) & (own_labels[:, None] >= 0.0)
    same_cluster = same_cluster & (own_index[:, None] != column_index[None, :])
    best_owned = jnp.max(jnp.where(same_cluster, similarity_scores, -1.0), axis=1)
    came_back = lax.all_to_all(best_owned, "cols", split_axis=0, concat_axis=0, tiled=True)
    row_best = jnp.where(occupied, came_back[jnp.minimum(send_place, send_total - 1)], -1.0)
    answers = lax.all_to_all(row_best, "rows", split_axis=0, concat_axis=0, tiled=True)
    max_similarity = answers[places]
    bin_width = 2.0 / (BINS - 1)
    centers = -1.0 + jnp.arange(BINS, dtype=jnp.float32) * bin_width
    bin_weights = jax.nn.relu(1.0 - jnp.abs(max_similarity[:, None] - centers[None, :]) / bin_width)
    bin_totals = lax.psum(jnp.sum(bin_weights, axis=0), ("rows", "cols"))
    return (max_similarity, bin_totals / (doc_count * row_count * col_count))


CHUNKS = (32, 32, 16, 16, 16, 16)
TWICE = (5, 0)


def meet_kernel(doc_total, emb_hbm, cluster_hbm, out_ref, emb_ref, cluster_ref, keys, blocks, key_labels,
                block_labels, label_columns, key_best, far_send, final_send, final_box, side_box, far_box, final_best,
                packets, answer_box, in_sems, plane_sems, chunk_sems, twice_sems, block_sems, label_sems, final_sems, side_sems,
                far_sems, packet_sems):
    row, col = lax.axis_index("rows"), lax.axis_index("cols")
    z, core = col // CORES, col % CORES
    row_at = (row, row + 1 - 2 * (row % 2), row + 2 - 4 * (row // 2), 3 - row)
    core_at = (core, 1 - core)
    near = len(row_at)
    slots = near * CORES
    docs, width = emb_ref.shape
    half = docs // 2

    def at_slot(slot, plane):
        return (row_at[slot % near], plane * CORES + core_at[slot // near])

    def above_me(plane):
        return (row, plane * CORES + core)

    me = core * near + row

    def order_of(slot):
        return core_at[slot // near] * near + row_at[slot % near]

    x_peer, y_peer, core_peer = at_slot(1, z), at_slot(2, z), at_slot(near, z)

    def copy(source, target, sems, at, where):
        return pltpu.make_async_remote_copy(
            src_ref=source, dst_ref=target, send_sem=sems.at[(0, *at)], recv_sem=sems.at[(1, *at)],
            device_id=where, device_id_type=pl.DeviceIdType.MESH)

    barrier = pltpu.get_barrier_semaphore()

    def greet(where):
        pl.semaphore_signal(barrier, inc=1, device_id=where, device_id_type=pl.DeviceIdType.MESH)

    senders = {0: (3, 2, 1), 1: (2, 0), 2: (3,), 3: (2,)}
    for plane, sources in senders.items():
        @pl.when(z == plane)
        def _():
            for source in sources:
                greet(above_me(source))
    for peer in (x_peer, y_peer, core_peer):
        greet(peer)
    load = pltpu.make_async_copy(emb_hbm, emb_ref, in_sems.at[0])
    load_labels = pltpu.make_async_copy(cluster_hbm, cluster_ref, in_sems.at[1])
    load.start()
    load_labels.start()
    load_labels.wait()
    key_labels[0] = cluster_ref[...].astype(jnp.float32)
    load.wait()
    values = emb_ref[...].astype(jnp.float32)
    normed = values * lax.rsqrt(jnp.sum(values * values, axis=1, keepdims=True) + 1e-06)
    keys[0:docs, :] = normed.astype(jnp.bfloat16)
    for plane in senders:
        @pl.when(z == plane)
        def _():
            pl.semaphore_wait(barrier, 3 + sum(plane in sources for sources in senders.values()))

    def part(slot, first, size):
        return keys.at[pl.ds(slot * docs + first, size)]

    def plane_copy(n):
        source, target, first, size, where = (
            (0, 1, 0, half, x_peer),
            (0, 2, half, half, y_peer),
            (0, 1, half, half, x_peer),
            (0, 2, 0, half, y_peer),
            (1, 3, 0, half, y_peer),
            (2, 3, half, half, x_peer),
            (0, 4, 0, docs, core_peer),
            (1, 5, 0, docs, core_peer),
            (2, 6, 0, docs, core_peer),
            (3, 7, 0, docs, core_peer),
        )[n]
        return copy(part(source, first, size), part(target, first, size), plane_sems, (n,), where)

    def plane_label(n):
        source, target, count, where = ((0, 1, 1, x_peer), (0, 2, 1, y_peer), (1, 3, 1, y_peer), (0, near, near, core_peer))[n]
        return copy(key_labels.at[pl.ds(source, count)], key_labels.at[pl.ds(target, count)], label_sems, (n,), where)

    def start(*copies):
        for item in copies:
            item.start()

    def arrive(*copies):
        for item in copies:
            item.wait_recv()

    def sent(*copies):
        for item in copies:
            item.wait_send()

    firsts = [sum(CHUNKS[:i]) for i in range(len(CHUNKS))]

    def chunk(n, i, source, plane):
        rows = pl.ds(firsts[i], CHUNKS[i])
        block = blocks.at[n, rows]
        return copy(keys.at[rows] if source is None else block, block, chunk_sems, (n, i), above_me(plane))

    def twice(i):
        rows = pl.ds(firsts[i], CHUNKS[i])
        return copy(keys.at[rows], blocks.at[0, rows], twice_sems, (i,), above_me(0))

    def whole(n, plane):
        return copy(keys.at[pl.ds(0, docs)], blocks.at[2], block_sems, (n,), above_me(plane))

    def block_label(n, plane, at, source=None):
        held = block_labels.at[n]
        return copy(key_labels.at[0] if source is None else held, held, label_sems, (4 + at,), above_me(plane))

    def plane_start():
        start(plane_label(0), plane_label(1), plane_copy(0), plane_copy(1), plane_copy(2), plane_copy(3), plane_copy(6))

    def plane_diagonal():
        arrive(plane_copy(0))
        start(plane_copy(4))
        arrive(plane_copy(1))
        start(plane_copy(5))
        arrive(plane_label(0))
        start(plane_label(2))

    def plane_across():
        arrive(plane_copy(2))
        start(plane_copy(7))
        arrive(plane_copy(3))
        start(plane_copy(8))

    def plane_last():
        arrive(plane_copy(4), plane_copy(5))
        start(plane_copy(9))
        arrive(plane_label(1), plane_label(2))
        start(plane_label(3))

    def plane_ready():
        arrive(plane_label(3))
        for slot in range(slots):
            label_columns[slot] = jnp.broadcast_to(key_labels[slot], (docs, docs)).T
        arrive(*[plane_copy(n) for n in range(6, 10)])

    def plane_sent():
        sent(*[plane_copy(n) for n in range(10)], *[plane_label(n) for n in range(4)])

    same_place = lax.broadcasted_iota(jnp.int32, (docs, docs), 0) == lax.broadcasted_iota(jnp.int32, (docs, docs), 1)

    def score(queries, labels, own, fresh=True, keep=True):
        parts = len(queries)
        query = queries[0] if parts == 1 else jnp.concatenate(queries, axis=0)
        scores = lax.dot_general(keys[...], query, (((1,), (1,)), ((), ())), preferred_element_type=jnp.float32)
        tops = [jnp.full((8, docs), -1.0, jnp.float32) for _ in queries]
        for slot in range(slots):
            both = None
            for n in range(parts):
                same = label_columns[slot] == labels[n]
                if own and n == 0 and slot == 0:
                    same = same & jnp.logical_not(same_place)
                found = jnp.where(same, scores[slot * docs:(slot + 1) * docs, n * docs:(n + 1) * docs], -1.0)
                tops[n] = jnp.maximum(tops[n], jnp.max(found.reshape(docs // 8, 8, docs), axis=0))
                both = found if both is None else jnp.maximum(both, found)
            if keep:
                key_best[slot] = both if fresh else jnp.maximum(key_best[slot], both)
        return [jnp.max(top, axis=0, keepdims=True) for top in tops]

    def best_of_keys(slot):
        return jnp.max(key_best[slot].T, axis=0, keepdims=True)

    bins_per_unit = (BINS - 1) / 2.0
    centers = lax.broadcasted_iota(jnp.int32, (BINS, docs), 0).astype(jnp.float32) - bins_per_unit

    def histogram(rows):
        scaled = rows * bins_per_unit
        weights = sum(jnp.maximum(1.0 - jnp.abs(scaled[n:n + 1] - centers), 0.0) for n in range(rows.shape[0]))
        return jnp.sum(weights.T, axis=0, keepdims=True)

    def spread(send, box, sems, to, source):
        return pltpu.make_async_remote_copy(
            src_ref=send, dst_ref=box.at[source], send_sem=sems.at[0, to], recv_sem=sems.at[1, source],
            device_id=(to % near, to // near), device_id_type=pl.DeviceIdType.MESH)

    def final_copy(to, source):
        return spread(final_send, final_box, final_sems, to, source)

    def side_copy(to, source):
        return spread(final_send, side_box, side_sems, to, source)

    def far_copy(to, plane, source):
        return spread(far_send, far_box.at[plane - 2], far_sems.at[:, plane - 2], to, source)

    def keep_final(slot, best):
        final_send[pl.ds(order_of(slot), 1), :] = best

    def with_others(act):
        for other in range(slots):
            pl.when(other != me)(functools.partial(act, other))

    def packet(slot, plane):
        return copy(packets.at[slot, plane - 1], answer_box, packet_sems, (slot, plane), at_slot(slot, plane))

    def take_answer(plane):
        pl.when(row == 0)(lambda: arrive(packet(1, plane)))
        pl.when(row != 0)(lambda: arrive(packet(0, plane)))
        out_ref[...] = answer_box[...]

    every = range(len(CHUNKS))

    def by_core(act):
        for at, count in enumerate(TWICE):
            cut = len(CHUNKS) - count
            pl.when(core == at)(functools.partial(act, every[:cut], every[cut:]))

    for plane in (2, 3):
        @pl.when(z == plane)
        def _():
            other = 5 - plane
            aside = [block_label(2, other, 4), whole(0, other)]
            if plane == 3:
                down = [block_label(1, 0, 2), *[chunk(1, i, None, 0) for i in every]] + aside
            else:
                down = [*aside, block_label(0, 1, 0), block_label(0, 0, 1)]
            start(*down)
            if plane == 2:
                by_core(lambda once, again: start(*[chunk(0, i, None, 1) for i in once], *[twice(i) for i in again],
                                                  *[chunk(0, i, None, 1) for i in again]))
            plane_start()
            plane_diagonal()
            plane_across()
            plane_last()
            plane_ready()
            arrive(block_label(2, plane, 4), whole(0, plane))
            own, theirs = score([keys[0:docs, :], blocks[2]], [key_labels[0], block_labels[2]], True, keep=False)
            far_send[0:1, :] = own
            far_send[1:2, :] = theirs
            far = [far_copy(to, plane, me) for to in range(slots)]
            start(*far)
            sent(*down)
            if plane == 2:
                by_core(lambda once, again: sent(*[chunk(0, i, None, 1) for i in every], *[twice(i) for i in again]))
            plane_sent()
            sent(*far)
            take_answer(plane)

    @pl.when(z == 1)
    def _():
        plane_start()

        def forward(*indices):
            for i in indices:
                arrive(chunk(0, i, 0, 0))
                start(chunk(0, i, 0, 0))

        plane_diagonal()
        plane_across()
        by_core(lambda once, again: forward(*once[:2]))
        plane_last()
        by_core(lambda once, again: forward(*once[2:]))
        plane_ready()
        arrive(block_label(2, 1, 5), whole(1, 1))
        mine, first = score([keys[0:docs, :], blocks[2]], [key_labels[0], block_labels[2]], True)
        arrive(block_label(0, 1, 0), block_label(1, 1, 3, 1), *[chunk(1, i, 1, 1) for i in every])
        by_core(lambda once, again: arrive(*[chunk(0, i, 0, 0) for i in again]))
        second, third = score([blocks[0], blocks[1]], [block_labels[0], block_labels[1]], False, fresh=False)
        final_send[slots:slots + 1, :] = second
        final_send[slots + 1:slots + 2, :] = third
        final_send[slots + 2:slots + 3, :] = first
        for slot in range(slots):
            keep_final(slot, best_of_keys(slot) if slot else jnp.maximum(mine, best_of_keys(0)))
        for other in range(slots):
            side_copy(other, me).start()
        by_core(lambda once, again: sent(*[chunk(0, i, 0, 0) for i in once]))
        plane_sent()
        sent(*[side_copy(other, me) for other in range(slots)])
        take_answer(1)

    @pl.when(z == 0)
    def _():
        start(block_label(2, 1, 5), whole(1, 1))
        plane_start()

        def forward(*indices):
            for i in indices:
                arrive(chunk(1, i, 1, 1))
                start(chunk(1, i, 1, 1))

        plane_diagonal()
        forward(*every[:2])
        plane_across()
        forward(*every[2:])
        arrive(block_label(1, 0, 2))
        start(block_label(1, 1, 3, 1))
        plane_last()
        plane_ready()
        mine, third = score([keys[0:docs, :], blocks[1]], [key_labels[0], block_labels[1]], True)
        arrive(block_label(0, 0, 1))
        by_core(lambda once, again: arrive(*[chunk(0, i, 0, 0) for i in once], *[twice(i) for i in again]))
        second = score([blocks[0]], [block_labels[0]], False, fresh=False)[0]
        for slot in range(1, slots):
            keep_final(slot, best_of_keys(slot))
        keep_final(0, jnp.maximum(mine, best_of_keys(0)))
        final_send[slots:slots + 1, :] = second
        final_send[slots + 1:slots + 2, :] = third
        final_send[slots + 2:slots + 3, :] = mine
        with_others(lambda other: final_copy(other, me).start())
        final_box[pl.ds(me, 1)] = final_send[...].reshape(1, slots + 3, docs)
        sent(block_label(2, 1, 5), whole(1, 1), block_label(1, 1, 3, 1), *[chunk(1, i, 1, 1) for i in every])
        plane_sent()
        arrive(*[side_copy(0, source) for source in range(slots)])
        final_best[1] = jnp.max(side_box[:, :slots, :], axis=0)
        totals = histogram(final_best[1])
        for plane in (2, 3):
            arrive(*[far_copy(0, plane, source) for source in range(slots)])
        outside = [side_box[:, slots + 2, :]] + [
            jnp.maximum(side_box[:, slots + n, :], jnp.maximum(far_box[n, :, 0, :], far_box[1 - n, :, 1, :])) for n in range(2)]
        with_others(lambda other: final_copy(0, other).wait_recv())
        final_best[0] = jnp.maximum(jnp.max(final_box[:, :slots, :], axis=0), outside[0])
        for plane in (2, 3):
            final_best[plane] = jnp.maximum(final_box[:, slots + plane - 2, :], outside[plane - 1])
        totals = totals + histogram(jnp.concatenate([final_best[plane] for plane in (0, 2, 3)], axis=0))
        totals = totals / doc_total
        out_ref[0] = final_best[0, pl.ds(me, 1), :]
        out_ref[1] = totals

        def finish(targets):
            for slot in targets:
                for plane in (1, 3, 2):
                    packets[slot, plane - 1, 0] = final_best[plane, pl.ds(order_of(slot), 1), :]
                    packets[slot, plane - 1, 1] = totals
                    packet(slot, plane).start()

        pl.when(row == 1)(lambda: finish((1,)))
        pl.when(row != 0)(lambda: finish((0,)))
        with_others(lambda other: final_copy(other, me).wait_send())

        def finished(targets):
            sent(*[packet(slot, plane) for slot in targets for plane in (3, 2, 1)])

        pl.when(row == 1)(lambda: finished((1,)))
        pl.when(row != 0)(lambda: finished((0,)))


def meet_shards(embeddings, document_cluster_index):
    rows, cols = lax.axis_size("rows"), lax.axis_size("cols")
    docs, width = embeddings.shape
    slots = rows * CORES
    hbm, vmem = pl.BlockSpec(memory_space=pl.ANY), pl.BlockSpec(memory_space=pltpu.VMEM)
    dma = pltpu.SemaphoreType.DMA
    line = lambda *lead: pltpu.VMEM((*lead, 1, docs), jnp.float32)
    found = pl.pallas_call(
        functools.partial(meet_kernel, docs * rows * cols),
        out_shape=pltpu.VMEM((2, 1, docs), jnp.float32),
        in_specs=[hbm, hbm],
        out_specs=vmem,
        scratch_shapes=[
            pltpu.VMEM((docs, width), jnp.bfloat16),
            pltpu.VMEM((1, docs), jnp.int32),
            pltpu.VMEM((slots * docs, width), jnp.bfloat16),
            pltpu.VMEM((3, docs, width), jnp.bfloat16),
            line(slots),
            line(3),
            pltpu.VMEM((slots, docs, docs), jnp.float32),
            pltpu.VMEM((slots, docs, docs), jnp.float32),
            pltpu.VMEM((2, docs), jnp.float32),
            pltpu.VMEM((slots + 3, docs), jnp.float32),
            pltpu.VMEM((slots, slots + 3, docs), jnp.float32),
            pltpu.VMEM((slots, slots + 3, docs), jnp.float32),
            pltpu.VMEM((2, slots, 2, docs), jnp.float32),
            pltpu.VMEM((4, slots, docs), jnp.float32),
            line(2, 3, 2),
            line(2),
            dma((2,)),
            dma((2, 10)),
            dma((2, 2, len(CHUNKS))),
            dma((2, len(CHUNKS))),
            dma((2, 2)),
            dma((2, 10)),
            dma((2, slots)),
            dma((2, slots)),
            dma((2, 2, slots)),
            dma((2, 2, 4)),
        ],
        compiler_params=pltpu.CompilerParams(collective_id=0, has_side_effects=True),
    )(embeddings, document_cluster_index.reshape(1, docs))
    return found[0, 0], found[1, 0]


def solution(mesh):
    placed = (P(("rows", "cols"), None), P(("rows", "cols")))
    rows, planes = mesh.shape["rows"], mesh.shape["cols"] // CORES
    direct = rows == 4 and planes == rows
    return jax.shard_map(
        meet_shards if direct else shards, mesh=mesh, in_specs=placed,
        out_specs=(P(("rows", "cols")), P()), check_vma=False
    )
```

```python
import functools

import jax
import jax.numpy as jnp
from jax import lax
from jax.experimental import pallas as pl
from jax.experimental.pallas import tpu as pltpu
from jax.sharding import PartitionSpec as P

CAP = 64
GROUP_CLUSTERS = 16
BINS = 128
CORES = 2


def from_partner(value, axis, bit):
    mask = 2**bit
    pairs = [(source, source ^ mask) for source in range(lax.axis_size(axis))]
    return lax.ppermute(value, axis, pairs)


def rank_among_equals(keys):
    places = jnp.arange(keys.shape[0], dtype=jnp.int32)
    earlier_equal = (keys[:, None] == keys[None, :]) & (places[None, :] < places[:, None])
    return jnp.sum(earlier_equal.astype(jnp.int32), axis=1)


def shards(embeddings, document_cluster_index):
    row_count = lax.axis_size("rows")
    col_count = lax.axis_size("cols")
    doc_count = embeddings.shape[0]
    width = embeddings.shape[1]
    slot_count = CAP * row_count
    values = embeddings.astype(jnp.float32)
    normed = (values * lax.rsqrt(jnp.sum(values * values, axis=1, keepdims=True) + 1e-06)).astype(
        jnp.bfloat16
    )
    owner_devices = document_cluster_index // GROUP_CLUSTERS
    within_cluster = (document_cluster_index % GROUP_CLUSTERS).astype(jnp.float32)
    slot_ranks = rank_among_equals(owner_devices)
    places = owner_devices * CAP + slot_ranks
    outgoing = jnp.zeros((slot_count, width), jnp.bfloat16).at[places].set(normed)
    out_labels = (
        jnp.full((slot_count,), -1.0, jnp.float32)
        .at[places]
        .set(within_cluster)
        .astype(jnp.bfloat16)
    )
    resident, res_labels = (
        lax.all_to_all(outgoing, "rows", split_axis=0, concat_axis=0, tiled=True),
        lax.all_to_all(out_labels, "rows", split_axis=0, concat_axis=0, tiled=True),
    )
    home_labels = res_labels.astype(jnp.float32)
    partner_count = max(1, col_count // GROUP_CLUSTERS)
    owned_count = max(1, GROUP_CLUSTERS // col_count)
    slot_quota = 2 * slot_count // GROUP_CLUSTERS // partner_count
    send_total = col_count * owned_count * slot_quota
    local_cluster = res_labels.astype(jnp.int32)
    occupied = local_cluster >= 0
    cluster_rank = rank_among_equals(local_cluster)
    member_slot = cluster_rank % partner_count
    cluster_depth = cluster_rank // partner_count
    destination = local_cluster // owned_count * partner_count + member_slot
    send_place = (
        destination * (owned_count * slot_quota)
        + local_cluster % owned_count * slot_quota
        + cluster_depth
    )
    send_place = jnp.where(occupied, send_place, send_total)
    send_rows = (
        jnp.zeros((send_total, width), jnp.bfloat16).at[send_place].set(resident, mode="drop")
    )
    send_labels = (
        jnp.full((send_total,), -1.0, jnp.float32)
        .at[send_place]
        .set(home_labels, mode="drop")
        .astype(jnp.bfloat16)
    )
    got_rows, got_labels = (
        lax.all_to_all(send_rows, "cols", split_axis=0, concat_axis=0, tiled=True),
        lax.all_to_all(send_labels, "cols", split_axis=0, concat_axis=0, tiled=True),
    )
    member_index = lax.axis_index("cols") % partner_count
    gathered_rows, gathered_labels = (got_rows, got_labels)
    for bit in range(partner_count.bit_length() - 1):
        other_rows, other_labels = from_partner((gathered_rows, gathered_labels), "cols", bit)
        upper = member_index // 2**bit % 2 == 1
        gathered_rows = jnp.where(
            upper,
            jnp.concatenate([other_rows, gathered_rows], axis=0),
            jnp.concatenate([gathered_rows, other_rows], axis=0),
        )
        gathered_labels = jnp.where(
            upper,
            jnp.concatenate([other_labels, gathered_labels], axis=0),
            jnp.concatenate([gathered_labels, other_labels], axis=0),
        )
    similarity_scores = lax.dot_general(
        got_rows, gathered_rows, (((1,), (1,)), ((), ())), preferred_element_type=jnp.float32
    )
    own_labels = got_labels.astype(jnp.float32)
    all_labels = gathered_labels.astype(jnp.float32)
    column_index = jnp.arange(gathered_rows.shape[0], dtype=jnp.int32)
    own_index = member_index * send_total + jnp.arange(send_total, dtype=jnp.int32)
    same_cluster = (own_labels[:, None] == all_labels[None, :]) & (own_labels[:, None] >= 0.0)
    same_cluster = same_cluster & (own_index[:, None] != column_index[None, :])
    best_owned = jnp.max(jnp.where(same_cluster, similarity_scores, -1.0), axis=1)
    came_back = lax.all_to_all(best_owned, "cols", split_axis=0, concat_axis=0, tiled=True)
    row_best = jnp.where(occupied, came_back[jnp.minimum(send_place, send_total - 1)], -1.0)
    answers = lax.all_to_all(row_best, "rows", split_axis=0, concat_axis=0, tiled=True)
    max_similarity = answers[places]
    bin_width = 2.0 / (BINS - 1)
    centers = -1.0 + jnp.arange(BINS, dtype=jnp.float32) * bin_width
    bin_weights = jax.nn.relu(1.0 - jnp.abs(max_similarity[:, None] - centers[None, :]) / bin_width)
    bin_totals = lax.psum(jnp.sum(bin_weights, axis=0), ("rows", "cols"))
    return (max_similarity, bin_totals / (doc_count * row_count * col_count))


CHUNKS = (32, 32, 16, 16, 16, 16)
TWICE = (5, 0)
LATE = 1


def meet_kernel(doc_total, emb_hbm, cluster_hbm, out_ref, emb_ref, cluster_ref, keys, blocks, key_labels,
                block_labels, label_columns, key_best, far_send, final_send, final_box, side_box, far_box, final_best,
                packets, answer_box, in_sems, plane_sems, chunk_sems, twice_sems, block_sems, label_sems, final_sems, side_sems,
                far_sems, packet_sems):
    row, col = lax.axis_index("rows"), lax.axis_index("cols")
    z, core = col // CORES, col % CORES
    row_at = (row, row + 1 - 2 * (row % 2), row + 2 - 4 * (row // 2), 3 - row)
    core_at = (core, 1 - core)
    near = len(row_at)
    slots = near * CORES
    docs, width = emb_ref.shape
    half = docs // 2

    def at_slot(slot, plane):
        return (row_at[slot % near], plane * CORES + core_at[slot // near])

    def above_me(plane):
        return (row, plane * CORES + core)

    me = core * near + row

    def order_of(slot):
        return core_at[slot // near] * near + row_at[slot % near]

    x_peer, y_peer, core_peer = at_slot(1, z), at_slot(2, z), at_slot(near, z)

    def copy(source, target, sems, at, where):
        return pltpu.make_async_remote_copy(
            src_ref=source, dst_ref=target, send_sem=sems.at[(0, *at)], recv_sem=sems.at[(1, *at)],
            device_id=where, device_id_type=pl.DeviceIdType.MESH)

    barrier = pltpu.get_barrier_semaphore()

    def greet(where):
        pl.semaphore_signal(barrier, inc=1, device_id=where, device_id_type=pl.DeviceIdType.MESH)

    senders = {0: (3, 2, 1), 1: (2, 0), 2: (3,), 3: (2,)}
    for plane, sources in senders.items():
        @pl.when(z == plane)
        def _():
            for source in sources:
                greet(above_me(source))
    for peer in (x_peer, y_peer, core_peer):
        greet(peer)
    load = pltpu.make_async_copy(emb_hbm, emb_ref, in_sems.at[0])
    load_labels = pltpu.make_async_copy(cluster_hbm, cluster_ref, in_sems.at[1])
    load.start()
    load_labels.start()
    load_labels.wait()
    key_labels[0] = cluster_ref[...].astype(jnp.float32)
    load.wait()
    values = emb_ref[...].astype(jnp.float32)
    normed = values * lax.rsqrt(jnp.sum(values * values, axis=1, keepdims=True) + 1e-06)
    keys[0:docs, :] = normed.astype(jnp.bfloat16)
    for plane in senders:
        @pl.when(z == plane)
        def _():
            pl.semaphore_wait(barrier, 3 + sum(plane in sources for sources in senders.values()))

    def part(slot, first, size):
        return keys.at[pl.ds(slot * docs + first, size)]

    def plane_copy(n):
        source, target, first, size, where = (
            (0, 1, 0, half, x_peer),
            (0, 2, half, half, y_peer),
            (0, 1, half, half, x_peer),
            (0, 2, 0, half, y_peer),
            (1, 3, 0, half, y_peer),
            (2, 3, half, half, x_peer),
            (0, 4, 0, docs, core_peer),
            (1, 5, 0, docs, core_peer),
            (2, 6, 0, docs, core_peer),
            (3, 7, 0, docs, core_peer),
        )[n]
        return copy(part(source, first, size), part(target, first, size), plane_sems, (n,), where)

    def plane_label(n):
        source, target, count, where = ((0, 1, 1, x_peer), (0, 2, 1, y_peer), (1, 3, 1, y_peer), (0, near, near, core_peer))[n]
        return copy(key_labels.at[pl.ds(source, count)], key_labels.at[pl.ds(target, count)], label_sems, (n,), where)

    def start(*copies):
        for item in copies:
            item.start()

    def arrive(*copies):
        for item in copies:
            item.wait_recv()

    def sent(*copies):
        for item in copies:
            item.wait_send()

    firsts = [sum(CHUNKS[:i]) for i in range(len(CHUNKS))]

    def chunk(n, i, source, plane):
        rows = pl.ds(firsts[i], CHUNKS[i])
        block = blocks.at[n, rows]
        return copy(keys.at[rows] if source is None else block, block, chunk_sems, (n, i), above_me(plane))

    def twice(i):
        rows = pl.ds(firsts[i], CHUNKS[i])
        return copy(keys.at[rows], blocks.at[0, rows], twice_sems, (i,), above_me(0))

    def whole(n, plane):
        return copy(keys.at[pl.ds(0, docs)], blocks.at[2], block_sems, (n,), above_me(plane))

    def block_label(n, plane, at, source=None):
        held = block_labels.at[n]
        return copy(key_labels.at[0] if source is None else held, held, label_sems, (4 + at,), above_me(plane))

    def plane_start():
        start(plane_label(0), plane_label(1), plane_copy(0), plane_copy(1), plane_copy(2), plane_copy(3), plane_copy(6))

    def plane_diagonal():
        arrive(plane_copy(0))
        start(plane_copy(4))
        arrive(plane_copy(1))
        start(plane_copy(5))
        arrive(plane_label(0))
        start(plane_label(2))

    def plane_across():
        arrive(plane_copy(2))
        start(plane_copy(7))
        arrive(plane_copy(3))
        start(plane_copy(8))

    def plane_last():
        arrive(plane_copy(4), plane_copy(5))
        start(plane_copy(9))
        arrive(plane_label(1), plane_label(2))
        start(plane_label(3))

    def plane_ready():
        arrive(plane_label(3))
        for slot in range(slots):
            label_columns[slot] = jnp.broadcast_to(key_labels[slot], (docs, docs)).T
        arrive(*[plane_copy(n) for n in range(6, 10)])

    def plane_sent():
        sent(*[plane_copy(n) for n in range(10)], *[plane_label(n) for n in range(4)])

    same_place = lax.broadcasted_iota(jnp.int32, (docs, docs), 0) == lax.broadcasted_iota(jnp.int32, (docs, docs), 1)

    def score(queries, labels, own, fresh=True, keep=True, done=None):
        parts = len(queries)
        query = queries[0] if parts == 1 else jnp.concatenate(queries, axis=0)
        scores = lax.dot_general(keys[...], query, (((1,), (1,)), ((), ())), preferred_element_type=jnp.float32)
        tops = [jnp.full((8, docs), -1.0, jnp.float32) for _ in queries]
        for slot in range(slots):
            both = None
            for n in range(parts):
                same = label_columns[slot] == labels[n]
                if own and n == 0 and slot == 0:
                    same = same & jnp.logical_not(same_place)
                found = jnp.where(same, scores[slot * docs:(slot + 1) * docs, n * docs:(n + 1) * docs], -1.0)
                tops[n] = jnp.maximum(tops[n], jnp.max(found.reshape(docs // 8, 8, docs), axis=0))
                both = found if both is None else jnp.maximum(both, found)
            if not fresh:
                both = jnp.maximum(key_best[slot], both)
            if done is not None:
                done(slot, jnp.max(both.T, axis=0, keepdims=True))
            elif keep:
                key_best[slot] = both
        return [jnp.max(top, axis=0, keepdims=True) for top in tops]

    bins_per_unit = (BINS - 1) / 2.0
    centers = lax.broadcasted_iota(jnp.int32, (BINS, docs), 0).astype(jnp.float32) - bins_per_unit

    def histogram(rows):
        scaled = rows * bins_per_unit
        count = rows.shape[0]
        missed = sum(jnp.minimum(jnp.abs(scaled[n:n + 1] - centers), 1.0) for n in range(count))
        return jnp.sum((count - missed).T, axis=0, keepdims=True)

    def spread(send, box, sems, to, source):
        return pltpu.make_async_remote_copy(
            src_ref=send, dst_ref=box.at[source], send_sem=sems.at[0, to], recv_sem=sems.at[1, source],
            device_id=(to % near, to // near), device_id_type=pl.DeviceIdType.MESH)

    def final_copy(to, source):
        return spread(final_send, final_box, final_sems, to, source)

    def side_copy(to, source):
        return spread(final_send, side_box, side_sems, to, source)

    def far_copy(to, plane, source):
        return spread(far_send, far_box.at[plane - 2], far_sems.at[:, plane - 2], to, source)

    def keep_final(mine):
        def keep(slot, best):
            final_send[pl.ds(order_of(slot), 1), :] = best if slot else jnp.maximum(mine, best)

        return keep

    def with_others(act):
        for other in range(slots):
            pl.when(other != me)(functools.partial(act, other))

    def packet(slot, plane):
        return copy(packets.at[slot, plane - 1], answer_box, packet_sems, (slot, plane), at_slot(slot, plane))

    def take_answer(plane):
        pl.when(row == 0)(lambda: arrive(packet(1, plane)))
        pl.when(row != 0)(lambda: arrive(packet(0, plane)))
        out_ref[...] = answer_box[...]

    every = range(len(CHUNKS))

    def by_core(act):
        for at, count in enumerate(TWICE):
            cut = len(CHUNKS) - count
            pl.when(core == at)(functools.partial(act, every[:cut], every[cut:]))

    for plane in (2, 3):
        @pl.when(z == plane)
        def _():
            other = 5 - plane
            aside = [block_label(2, other, 4), whole(0, other)]
            if plane == 3:
                down = [block_label(1, 0, 2), *[chunk(1, i, None, 0) for i in every]] + aside
            else:
                down = [*aside, block_label(0, 1, 0), block_label(0, 0, 1)]
            start(*down)
            if plane == 2:
                by_core(lambda once, again: start(
                    *[chunk(0, i, None, 1) for i in once], *[twice(i) for i in again[:-LATE]],
                    *[chunk(0, i, None, 1) for i in again], *[twice(i) for i in again[-LATE:]]))
            plane_start()
            plane_diagonal()
            plane_across()
            plane_last()
            plane_ready()
            arrive(block_label(2, plane, 4), whole(0, plane))
            own, theirs = score([keys[0:docs, :], blocks[2]], [key_labels[0], block_labels[2]], True, keep=False)
            far_send[0:1, :] = own
            far_send[1:2, :] = theirs
            far = [far_copy(to, plane, me) for to in range(slots)]
            start(*far)
            sent(*down)
            if plane == 2:
                by_core(lambda once, again: sent(*[chunk(0, i, None, 1) for i in every], *[twice(i) for i in again]))
            plane_sent()
            sent(*far)
            take_answer(plane)

    @pl.when(z == 1)
    def _():
        plane_start()

        def forward(*indices):
            for i in indices:
                arrive(chunk(0, i, 0, 0))
                start(chunk(0, i, 0, 0))

        plane_diagonal()
        plane_across()
        by_core(lambda once, again: forward(*once[:2]))
        plane_last()
        by_core(lambda once, again: forward(*once[2:]))
        plane_ready()
        arrive(block_label(2, 1, 5), whole(1, 1))
        mine, first = score([keys[0:docs, :], blocks[2]], [key_labels[0], block_labels[2]], True)
        arrive(block_label(0, 1, 0), block_label(1, 1, 3, 1), *[chunk(1, i, 1, 1) for i in every])
        by_core(lambda once, again: arrive(*[chunk(0, i, 0, 0) for i in again]))
        second, third = score(
            [blocks[0], blocks[1]], [block_labels[0], block_labels[1]], False, fresh=False, done=keep_final(mine))
        for n, best in enumerate((second, third, first)):
            final_send[slots + n:slots + n + 1, :] = best
        for other in range(slots):
            side_copy(other, me).start()
        by_core(lambda once, again: sent(*[chunk(0, i, 0, 0) for i in once]))
        plane_sent()
        sent(*[side_copy(other, me) for other in range(slots)])
        take_answer(1)

    @pl.when(z == 0)
    def _():
        start(block_label(2, 1, 5), whole(1, 1))
        plane_start()

        def forward(*indices):
            for i in indices:
                arrive(chunk(1, i, 1, 1))
                start(chunk(1, i, 1, 1))

        plane_diagonal()
        forward(*every[:2])
        plane_across()
        forward(*every[2:])
        arrive(block_label(1, 0, 2))
        start(block_label(1, 1, 3, 1))
        plane_last()
        plane_ready()
        mine, third = score([keys[0:docs, :], blocks[1]], [key_labels[0], block_labels[1]], True)
        arrive(block_label(0, 0, 1))
        by_core(lambda once, again: arrive(*[chunk(0, i, 0, 0) for i in once], *[twice(i) for i in again]))
        second = score([blocks[0]], [block_labels[0]], False, fresh=False, done=keep_final(mine))[0]
        for n, best in enumerate((second, third, mine)):
            final_send[slots + n:slots + n + 1, :] = best
        with_others(lambda other: final_copy(other, me).start())
        final_box[pl.ds(me, 1)] = final_send[...].reshape(1, slots + 3, docs)
        sent(block_label(2, 1, 5), whole(1, 1), block_label(1, 1, 3, 1), *[chunk(1, i, 1, 1) for i in every])
        plane_sent()
        arrive(*[side_copy(0, source) for source in range(slots)])
        final_best[1] = jnp.max(side_box[:, :slots, :], axis=0)
        totals = histogram(final_best[1])
        for plane in (2, 3):
            arrive(*[far_copy(0, plane, source) for source in range(slots)])
        outside = [side_box[:, slots + 2, :]] + [
            jnp.maximum(side_box[:, slots + n, :], jnp.maximum(far_box[n, :, 0, :], far_box[1 - n, :, 1, :])) for n in range(2)]
        with_others(lambda other: final_copy(0, other).wait_recv())
        final_best[0] = jnp.maximum(jnp.max(final_box[:, :slots, :], axis=0), outside[0])
        for plane in (2, 3):
            final_best[plane] = jnp.maximum(final_box[:, slots + plane - 2, :], outside[plane - 1])
        totals = totals + histogram(jnp.concatenate([final_best[plane] for plane in (0, 2, 3)], axis=0))
        totals = totals / doc_total
        out_ref[0] = final_best[0, pl.ds(me, 1), :]
        out_ref[1] = totals

        def finish(targets):
            for slot in targets:
                for plane in (1, 3, 2):
                    packets[slot, plane - 1, 0] = final_best[plane, pl.ds(order_of(slot), 1), :]
                    packets[slot, plane - 1, 1] = totals
                    packet(slot, plane).start()

        pl.when(row == 1)(lambda: finish((1,)))
        pl.when(row != 0)(lambda: finish((0,)))
        with_others(lambda other: final_copy(other, me).wait_send())

        def finished(targets):
            sent(*[packet(slot, plane) for slot in targets for plane in (3, 2, 1)])

        pl.when(row == 1)(lambda: finished((1,)))
        pl.when(row != 0)(lambda: finished((0,)))


def meet_shards(embeddings, document_cluster_index):
    rows, cols = lax.axis_size("rows"), lax.axis_size("cols")
    docs, width = embeddings.shape
    slots = rows * CORES
    hbm, vmem = pl.BlockSpec(memory_space=pl.ANY), pl.BlockSpec(memory_space=pltpu.VMEM)
    dma = pltpu.SemaphoreType.DMA
    line = lambda *lead: pltpu.VMEM((*lead, 1, docs), jnp.float32)
    found = pl.pallas_call(
        functools.partial(meet_kernel, docs * rows * cols),
        out_shape=pltpu.VMEM((2, 1, docs), jnp.float32),
        in_specs=[hbm, hbm],
        out_specs=vmem,
        scratch_shapes=[
            pltpu.VMEM((docs, width), jnp.bfloat16),
            pltpu.VMEM((1, docs), jnp.int32),
            pltpu.VMEM((slots * docs, width), jnp.bfloat16),
            pltpu.VMEM((3, docs, width), jnp.bfloat16),
            line(slots),
            line(3),
            pltpu.VMEM((slots, docs, docs), jnp.float32),
            pltpu.VMEM((slots, docs, docs), jnp.float32),
            pltpu.VMEM((2, docs), jnp.float32),
            pltpu.VMEM((slots + 3, docs), jnp.float32),
            pltpu.VMEM((slots, slots + 3, docs), jnp.float32),
            pltpu.VMEM((slots, slots + 3, docs), jnp.float32),
            pltpu.VMEM((2, slots, 2, docs), jnp.float32),
            pltpu.VMEM((4, slots, docs), jnp.float32),
            line(2, 3, 2),
            line(2),
            dma((2,)),
            dma((2, 10)),
            dma((2, 2, len(CHUNKS))),
            dma((2, len(CHUNKS))),
            dma((2, 2)),
            dma((2, 10)),
            dma((2, slots)),
            dma((2, slots)),
            dma((2, 2, slots)),
            dma((2, 2, 4)),
        ],
        compiler_params=pltpu.CompilerParams(collective_id=0, has_side_effects=True),
    )(embeddings, document_cluster_index.reshape(1, docs))
    return found[0, 0], found[1, 0]


def solution(mesh):
    placed = (P(("rows", "cols"), None), P(("rows", "cols")))
    rows, planes = mesh.shape["rows"], mesh.shape["cols"] // CORES
    direct = rows == 4 and planes == rows
    return jax.shard_map(
        meet_shards if direct else shards, mesh=mesh, in_specs=placed,
        out_specs=(P(("rows", "cols")), P()), check_vma=False
    )
```

```python
import functools

import jax
import jax.numpy as jnp
from jax import lax
from jax.experimental import pallas as pl
from jax.experimental.pallas import tpu as pltpu
from jax.sharding import PartitionSpec as P

CAP = 64
GROUP_CLUSTERS = 16
BINS = 128
CORES = 2


def from_partner(value, axis, bit):
    mask = 2**bit
    pairs = [(source, source ^ mask) for source in range(lax.axis_size(axis))]
    return lax.ppermute(value, axis, pairs)


def rank_among_equals(keys):
    places = jnp.arange(keys.shape[0], dtype=jnp.int32)
    earlier_equal = (keys[:, None] == keys[None, :]) & (places[None, :] < places[:, None])
    return jnp.sum(earlier_equal.astype(jnp.int32), axis=1)


def shards(embeddings, document_cluster_index):
    row_count = lax.axis_size("rows")
    col_count = lax.axis_size("cols")
    doc_count = embeddings.shape[0]
    width = embeddings.shape[1]
    slot_count = CAP * row_count
    values = embeddings.astype(jnp.float32)
    normed = (values * lax.rsqrt(jnp.sum(values * values, axis=1, keepdims=True) + 1e-06)).astype(
        jnp.bfloat16
    )
    owner_devices = document_cluster_index // GROUP_CLUSTERS
    within_cluster = (document_cluster_index % GROUP_CLUSTERS).astype(jnp.float32)
    slot_ranks = rank_among_equals(owner_devices)
    places = owner_devices * CAP + slot_ranks
    outgoing = jnp.zeros((slot_count, width), jnp.bfloat16).at[places].set(normed)
    out_labels = (
        jnp.full((slot_count,), -1.0, jnp.float32)
        .at[places]
        .set(within_cluster)
        .astype(jnp.bfloat16)
    )
    resident, res_labels = (
        lax.all_to_all(outgoing, "rows", split_axis=0, concat_axis=0, tiled=True),
        lax.all_to_all(out_labels, "rows", split_axis=0, concat_axis=0, tiled=True),
    )
    home_labels = res_labels.astype(jnp.float32)
    partner_count = max(1, col_count // GROUP_CLUSTERS)
    owned_count = max(1, GROUP_CLUSTERS // col_count)
    slot_quota = 2 * slot_count // GROUP_CLUSTERS // partner_count
    send_total = col_count * owned_count * slot_quota
    local_cluster = res_labels.astype(jnp.int32)
    occupied = local_cluster >= 0
    cluster_rank = rank_among_equals(local_cluster)
    member_slot = cluster_rank % partner_count
    cluster_depth = cluster_rank // partner_count
    destination = local_cluster // owned_count * partner_count + member_slot
    send_place = (
        destination * (owned_count * slot_quota)
        + local_cluster % owned_count * slot_quota
        + cluster_depth
    )
    send_place = jnp.where(occupied, send_place, send_total)
    send_rows = (
        jnp.zeros((send_total, width), jnp.bfloat16).at[send_place].set(resident, mode="drop")
    )
    send_labels = (
        jnp.full((send_total,), -1.0, jnp.float32)
        .at[send_place]
        .set(home_labels, mode="drop")
        .astype(jnp.bfloat16)
    )
    got_rows, got_labels = (
        lax.all_to_all(send_rows, "cols", split_axis=0, concat_axis=0, tiled=True),
        lax.all_to_all(send_labels, "cols", split_axis=0, concat_axis=0, tiled=True),
    )
    member_index = lax.axis_index("cols") % partner_count
    gathered_rows, gathered_labels = (got_rows, got_labels)
    for bit in range(partner_count.bit_length() - 1):
        other_rows, other_labels = from_partner((gathered_rows, gathered_labels), "cols", bit)
        upper = member_index // 2**bit % 2 == 1
        gathered_rows = jnp.where(
            upper,
            jnp.concatenate([other_rows, gathered_rows], axis=0),
            jnp.concatenate([gathered_rows, other_rows], axis=0),
        )
        gathered_labels = jnp.where(
            upper,
            jnp.concatenate([other_labels, gathered_labels], axis=0),
            jnp.concatenate([gathered_labels, other_labels], axis=0),
        )
    similarity_scores = lax.dot_general(
        got_rows, gathered_rows, (((1,), (1,)), ((), ())), preferred_element_type=jnp.float32
    )
    own_labels = got_labels.astype(jnp.float32)
    all_labels = gathered_labels.astype(jnp.float32)
    column_index = jnp.arange(gathered_rows.shape[0], dtype=jnp.int32)
    own_index = member_index * send_total + jnp.arange(send_total, dtype=jnp.int32)
    same_cluster = (own_labels[:, None] == all_labels[None, :]) & (own_labels[:, None] >= 0.0)
    same_cluster = same_cluster & (own_index[:, None] != column_index[None, :])
    best_owned = jnp.max(jnp.where(same_cluster, similarity_scores, -1.0), axis=1)
    came_back = lax.all_to_all(best_owned, "cols", split_axis=0, concat_axis=0, tiled=True)
    row_best = jnp.where(occupied, came_back[jnp.minimum(send_place, send_total - 1)], -1.0)
    answers = lax.all_to_all(row_best, "rows", split_axis=0, concat_axis=0, tiled=True)
    max_similarity = answers[places]
    bin_width = 2.0 / (BINS - 1)
    centers = -1.0 + jnp.arange(BINS, dtype=jnp.float32) * bin_width
    bin_weights = jax.nn.relu(1.0 - jnp.abs(max_similarity[:, None] - centers[None, :]) / bin_width)
    bin_totals = lax.psum(jnp.sum(bin_weights, axis=0), ("rows", "cols"))
    return (max_similarity, bin_totals / (doc_count * row_count * col_count))


CHUNKS = (32, 32, 16, 16, 16, 16)
TWICE = (5, 0)
LATE = 1


def meet_kernel(doc_total, emb_hbm, cluster_hbm, out_ref, emb_ref, cluster_ref, keys, keys_t, blocks, key_labels,
                block_labels, key_best, far_send, final_send, final_box, side_box, far_box, final_best,
                packets, answer_box, in_sems, plane_sems, chunk_sems, twice_sems, block_sems, label_sems, final_sems, side_sems,
                far_sems, packet_sems):
    row, col = lax.axis_index("rows"), lax.axis_index("cols")
    z, core = col // CORES, col % CORES
    row_at = (row, row + 1 - 2 * (row % 2), row + 2 - 4 * (row // 2), 3 - row)
    core_at = (core, 1 - core)
    near = len(row_at)
    slots = near * CORES
    docs, width = emb_ref.shape
    half = docs // 2

    def at_slot(slot, plane):
        return (row_at[slot % near], plane * CORES + core_at[slot // near])

    def above_me(plane):
        return (row, plane * CORES + core)

    me = core * near + row

    def order_of(slot):
        return core_at[slot // near] * near + row_at[slot % near]

    x_peer, y_peer, core_peer = at_slot(1, z), at_slot(2, z), at_slot(near, z)

    def copy(source, target, sems, at, where):
        return pltpu.make_async_remote_copy(
            src_ref=source, dst_ref=target, send_sem=sems.at[(0, *at)], recv_sem=sems.at[(1, *at)],
            device_id=where, device_id_type=pl.DeviceIdType.MESH)

    barrier = pltpu.get_barrier_semaphore()

    def greet(where):
        pl.semaphore_signal(barrier, inc=1, device_id=where, device_id_type=pl.DeviceIdType.MESH)

    senders = {0: (3, 2, 1), 1: (2, 0), 2: (3,), 3: (2,)}
    for plane, sources in senders.items():
        @pl.when(z == plane)
        def _():
            for source in sources:
                greet(above_me(source))
    for peer in (x_peer, y_peer, core_peer):
        greet(peer)
    load = pltpu.make_async_copy(emb_hbm, emb_ref, in_sems.at[0])
    load_labels = pltpu.make_async_copy(cluster_hbm, cluster_ref, in_sems.at[1])
    load.start()
    load_labels.start()
    load_labels.wait()
    key_labels[0] = cluster_ref[...].astype(jnp.float32)
    load.wait()
    values = emb_ref[...].astype(jnp.float32)
    normed = values * lax.rsqrt(jnp.sum(values * values, axis=1, keepdims=True) + 1e-06)
    keys[0:docs, :] = normed.astype(jnp.bfloat16)
    for plane in senders:
        @pl.when(z == plane)
        def _():
            pl.semaphore_wait(barrier, 3 + sum(plane in sources for sources in senders.values()))

    def part(slot, first, size):
        return keys.at[pl.ds(slot * docs + first, size)]

    def plane_copy(n):
        source, target, first, size, where = (
            (0, 1, 0, half, x_peer),
            (0, 2, half, half, y_peer),
            (0, 1, half, half, x_peer),
            (0, 2, 0, half, y_peer),
            (1, 3, 0, half, y_peer),
            (2, 3, half, half, x_peer),
            (0, 4, 0, docs, core_peer),
            (1, 5, 0, docs, core_peer),
            (2, 6, 0, docs, core_peer),
            (3, 7, 0, docs, core_peer),
        )[n]
        return copy(part(source, first, size), part(target, first, size), plane_sems, (n,), where)

    def plane_label(n):
        source, target, count, where = ((0, 1, 1, x_peer), (0, 2, 1, y_peer), (1, 3, 1, y_peer), (0, near, near, core_peer))[n]
        return copy(key_labels.at[pl.ds(source, count)], key_labels.at[pl.ds(target, count)], label_sems, (n,), where)

    def start(*copies):
        for item in copies:
            item.start()

    def arrive(*copies):
        for item in copies:
            item.wait_recv()

    def sent(*copies):
        for item in copies:
            item.wait_send()

    firsts = [sum(CHUNKS[:i]) for i in range(len(CHUNKS))]

    def chunk(n, i, source, plane):
        rows = pl.ds(firsts[i], CHUNKS[i])
        block = blocks.at[n, rows]
        return copy(keys.at[rows] if source is None else block, block, chunk_sems, (n, i), above_me(plane))

    def twice(i):
        rows = pl.ds(firsts[i], CHUNKS[i])
        return copy(keys.at[rows], blocks.at[0, rows], twice_sems, (i,), above_me(0))

    def whole(n, plane):
        return copy(keys.at[pl.ds(0, docs)], blocks.at[2], block_sems, (n,), above_me(plane))

    def block_label(n, plane, at, source=None):
        held = block_labels.at[n]
        return copy(key_labels.at[0] if source is None else held, held, label_sems, (4 + at,), above_me(plane))

    def turn(slot):
        keys_t[:, slot * docs:(slot + 1) * docs] = keys[slot * docs:(slot + 1) * docs, :].T

    def plane_start():
        start(plane_label(0), plane_label(1), plane_copy(0), plane_copy(1), plane_copy(2), plane_copy(3), plane_copy(6))
        turn(0)

    def plane_diagonal():
        arrive(plane_copy(0))
        start(plane_copy(4))
        arrive(plane_copy(1))
        start(plane_copy(5))
        arrive(plane_label(0))
        start(plane_label(2))

    def plane_across():
        arrive(plane_copy(2))
        start(plane_copy(7))
        arrive(plane_copy(3))
        start(plane_copy(8))
        turn(1)
        turn(2)

    def plane_last():
        arrive(plane_copy(4), plane_copy(5))
        start(plane_copy(9))
        arrive(plane_label(1), plane_label(2))
        start(plane_label(3))
        turn(3)

    def plane_ready():
        for n in range(6, 10):
            arrive(plane_copy(n))
            turn(n - 2)
        arrive(plane_label(3))

    def plane_sent():
        sent(*[plane_copy(n) for n in range(10)], *[plane_label(n) for n in range(4)])

    same_place = lax.broadcasted_iota(jnp.int32, (docs, docs), 0) == lax.broadcasted_iota(jnp.int32, (docs, docs), 1)

    def score(queries, labels, own, fresh=True, keep=True, done=None):
        parts = len(queries)
        query = queries[0] if parts == 1 else jnp.concatenate(queries, axis=0)
        scores = jnp.dot(query, keys_t[...], preferred_element_type=jnp.float32)
        columns = [jnp.broadcast_to(label, (docs, docs)).T for label in labels]
        tops = [None] * parts
        for slot in range(slots):
            best = None if fresh else key_best[slot]
            for n in range(parts):
                same = columns[n] == key_labels[slot]
                if own and n == 0 and slot == 0:
                    same = same & jnp.logical_not(same_place)
                found = jnp.where(same, scores[n * docs:(n + 1) * docs, slot * docs:(slot + 1) * docs], -1.0)
                tops[n] = found if slot == 0 else jnp.maximum(tops[n], found)
                group = jnp.max(found.reshape(docs // 8, 8, docs), axis=0)
                best = group if best is None else jnp.maximum(best, group)
            if done is not None:
                done(slot, jnp.max(best, axis=0, keepdims=True))
            elif keep:
                key_best[slot] = best
        return [jnp.max(top.T, axis=0, keepdims=True) for top in tops]

    bins_per_unit = (BINS - 1) / 2.0
    centers = lax.broadcasted_iota(jnp.int32, (BINS, docs), 0).astype(jnp.float32) - bins_per_unit

    def histogram(rows):
        scaled = rows * bins_per_unit
        count = rows.shape[0]
        missed = sum(jnp.minimum(jnp.abs(scaled[n:n + 1] - centers), 1.0) for n in range(count))
        return jnp.sum((count - missed).T, axis=0, keepdims=True)

    def spread(send, box, sems, to, source):
        return pltpu.make_async_remote_copy(
            src_ref=send, dst_ref=box.at[source], send_sem=sems.at[0, to], recv_sem=sems.at[1, source],
            device_id=(to % near, to // near), device_id_type=pl.DeviceIdType.MESH)

    def final_copy(to, source):
        return spread(final_send, final_box, final_sems, to, source)

    def side_copy(to, source):
        return spread(final_send, side_box, side_sems, to, source)

    def far_copy(to, plane, source):
        return spread(far_send, far_box.at[plane - 2], far_sems.at[:, plane - 2], to, source)

    def keep_final(mine):
        def keep(slot, best):
            final_send[pl.ds(order_of(slot), 1), :] = best if slot else jnp.maximum(mine, best)

        return keep

    def with_others(act):
        for other in range(slots):
            pl.when(other != me)(functools.partial(act, other))

    def packet(slot, plane):
        return copy(packets.at[slot, plane - 1], answer_box, packet_sems, (slot, plane), at_slot(slot, plane))

    def take_answer(plane):
        pl.when(row == 0)(lambda: arrive(packet(1, plane)))
        pl.when(row != 0)(lambda: arrive(packet(0, plane)))
        out_ref[...] = answer_box[...]

    every = range(len(CHUNKS))

    def by_core(act):
        for at, count in enumerate(TWICE):
            cut = len(CHUNKS) - count
            pl.when(core == at)(functools.partial(act, every[:cut], every[cut:]))

    for plane in (2, 3):
        @pl.when(z == plane)
        def _():
            other = 5 - plane
            aside = [block_label(2, other, 4), whole(0, other)]
            if plane == 3:
                down = [block_label(1, 0, 2), *[chunk(1, i, None, 0) for i in every]] + aside
            else:
                down = [*aside, block_label(0, 1, 0), block_label(0, 0, 1)]
            start(*down)
            if plane == 2:
                by_core(lambda once, again: start(
                    *[chunk(0, i, None, 1) for i in once], *[twice(i) for i in again[:-LATE]],
                    *[chunk(0, i, None, 1) for i in again], *[twice(i) for i in again[-LATE:]]))
            plane_start()
            plane_diagonal()
            plane_across()
            plane_last()
            plane_ready()
            arrive(block_label(2, plane, 4), whole(0, plane))
            own, theirs = score([keys[0:docs, :], blocks[2]], [key_labels[0], block_labels[2]], True, keep=False)
            far_send[0:1, :] = own
            far_send[1:2, :] = theirs
            far = [far_copy(to, plane, me) for to in range(slots)]
            start(*far)
            sent(*down)
            if plane == 2:
                by_core(lambda once, again: sent(*[chunk(0, i, None, 1) for i in every], *[twice(i) for i in again]))
            plane_sent()
            sent(*far)
            take_answer(plane)

    @pl.when(z == 1)
    def _():
        plane_start()

        def forward(*indices):
            for i in indices:
                arrive(chunk(0, i, 0, 0))
                start(chunk(0, i, 0, 0))

        plane_diagonal()
        plane_across()
        by_core(lambda once, again: forward(*once[:2]))
        plane_last()
        by_core(lambda once, again: forward(*once[2:]))
        plane_ready()
        arrive(block_label(2, 1, 5), whole(1, 1))
        mine, first = score([keys[0:docs, :], blocks[2]], [key_labels[0], block_labels[2]], True)
        arrive(block_label(0, 1, 0), block_label(1, 1, 3, 1), *[chunk(1, i, 1, 1) for i in every])
        by_core(lambda once, again: arrive(*[chunk(0, i, 0, 0) for i in again]))
        second, third = score(
            [blocks[0], blocks[1]], [block_labels[0], block_labels[1]], False, fresh=False, done=keep_final(mine))
        for n, best in enumerate((second, third, first)):
            final_send[slots + n:slots + n + 1, :] = best
        for other in range(slots):
            side_copy(other, me).start()
        by_core(lambda once, again: sent(*[chunk(0, i, 0, 0) for i in once]))
        plane_sent()
        sent(*[side_copy(other, me) for other in range(slots)])
        take_answer(1)

    @pl.when(z == 0)
    def _():
        start(block_label(2, 1, 5), whole(1, 1))
        plane_start()

        def forward(*indices):
            for i in indices:
                arrive(chunk(1, i, 1, 1))
                start(chunk(1, i, 1, 1))

        plane_diagonal()
        forward(*every[:2])
        plane_across()
        forward(*every[2:])
        arrive(block_label(1, 0, 2))
        start(block_label(1, 1, 3, 1))
        plane_last()
        plane_ready()
        mine, third = score([keys[0:docs, :], blocks[1]], [key_labels[0], block_labels[1]], True)
        arrive(block_label(0, 0, 1))
        by_core(lambda once, again: arrive(*[chunk(0, i, 0, 0) for i in once], *[twice(i) for i in again]))
        second = score([blocks[0]], [block_labels[0]], False, fresh=False, done=keep_final(mine))[0]
        for n, best in enumerate((second, third, mine)):
            final_send[slots + n:slots + n + 1, :] = best
        with_others(lambda other: final_copy(other, me).start())
        final_box[pl.ds(me, 1)] = final_send[...].reshape(1, slots + 3, docs)
        sent(block_label(2, 1, 5), whole(1, 1), block_label(1, 1, 3, 1), *[chunk(1, i, 1, 1) for i in every])
        plane_sent()
        arrive(*[side_copy(0, source) for source in range(slots)])
        final_best[1] = jnp.max(side_box[:, :slots, :], axis=0)
        totals = histogram(final_best[1])
        for plane in (2, 3):
            arrive(*[far_copy(0, plane, source) for source in range(slots)])
        outside = [side_box[:, slots + 2, :]] + [
            jnp.maximum(side_box[:, slots + n, :], jnp.maximum(far_box[n, :, 0, :], far_box[1 - n, :, 1, :])) for n in range(2)]
        with_others(lambda other: final_copy(0, other).wait_recv())
        final_best[0] = jnp.maximum(jnp.max(final_box[:, :slots, :], axis=0), outside[0])
        for plane in (2, 3):
            final_best[plane] = jnp.maximum(final_box[:, slots + plane - 2, :], outside[plane - 1])
        totals = totals + histogram(jnp.concatenate([final_best[plane] for plane in (0, 2, 3)], axis=0))
        totals = totals / doc_total
        out_ref[0] = final_best[0, pl.ds(me, 1), :]
        out_ref[1] = totals

        def finish(targets):
            for slot in targets:
                for plane in (1, 3, 2):
                    packets[slot, plane - 1, 0] = final_best[plane, pl.ds(order_of(slot), 1), :]
                    packets[slot, plane - 1, 1] = totals
                    packet(slot, plane).start()

        pl.when(row == 1)(lambda: finish((1,)))
        pl.when(row != 0)(lambda: finish((0,)))
        with_others(lambda other: final_copy(other, me).wait_send())

        def finished(targets):
            sent(*[packet(slot, plane) for slot in targets for plane in (3, 2, 1)])

        pl.when(row == 1)(lambda: finished((1,)))
        pl.when(row != 0)(lambda: finished((0,)))


def meet_shards(embeddings, document_cluster_index):
    rows, cols = lax.axis_size("rows"), lax.axis_size("cols")
    docs, width = embeddings.shape
    slots = rows * CORES
    hbm, vmem = pl.BlockSpec(memory_space=pl.ANY), pl.BlockSpec(memory_space=pltpu.VMEM)
    dma = pltpu.SemaphoreType.DMA
    line = lambda *lead: pltpu.VMEM((*lead, 1, docs), jnp.float32)
    found = pl.pallas_call(
        functools.partial(meet_kernel, docs * rows * cols),
        out_shape=pltpu.VMEM((2, 1, docs), jnp.float32),
        in_specs=[hbm, hbm],
        out_specs=vmem,
        scratch_shapes=[
            pltpu.VMEM((docs, width), jnp.bfloat16),
            pltpu.VMEM((1, docs), jnp.int32),
            pltpu.VMEM((slots * docs, width), jnp.bfloat16),
            pltpu.VMEM((width, slots * docs), jnp.bfloat16),
            pltpu.VMEM((3, docs, width), jnp.bfloat16),
            line(slots),
            line(3),
            pltpu.VMEM((slots, 8, docs), jnp.float32),
            pltpu.VMEM((2, docs), jnp.float32),
            pltpu.VMEM((slots + 3, docs), jnp.float32),
            pltpu.VMEM((slots, slots + 3, docs), jnp.float32),
            pltpu.VMEM((slots, slots + 3, docs), jnp.float32),
            pltpu.VMEM((2, slots, 2, docs), jnp.float32),
            pltpu.VMEM((4, slots, docs), jnp.float32),
            line(2, 3, 2),
            line(2),
            dma((2,)),
            dma((2, 10)),
            dma((2, 2, len(CHUNKS))),
            dma((2, len(CHUNKS))),
            dma((2, 2)),
            dma((2, 10)),
            dma((2, slots)),
            dma((2, slots)),
            dma((2, 2, slots)),
            dma((2, 2, 4)),
        ],
        compiler_params=pltpu.CompilerParams(collective_id=0, has_side_effects=True),
    )(embeddings, document_cluster_index.reshape(1, docs))
    return found[0, 0], found[1, 0]


def solution(mesh):
    placed = (P(("rows", "cols"), None), P(("rows", "cols")))
    rows, planes = mesh.shape["rows"], mesh.shape["cols"] // CORES
    direct = rows == 4 and planes == rows
    return jax.shard_map(
        meet_shards if direct else shards, mesh=mesh, in_specs=placed,
        out_specs=(P(("rows", "cols")), P()), check_vma=False
    )
```

```python
import functools

import jax
import jax.numpy as jnp
from jax import lax
from jax.experimental import pallas as pl
from jax.experimental.pallas import tpu as pltpu
from jax.sharding import PartitionSpec as P

CAP = 64
GROUP_CLUSTERS = 16
BINS = 128
CORES = 2


def from_partner(value, axis, bit):
    mask = 2**bit
    pairs = [(source, source ^ mask) for source in range(lax.axis_size(axis))]
    return lax.ppermute(value, axis, pairs)


def rank_among_equals(keys):
    places = jnp.arange(keys.shape[0], dtype=jnp.int32)
    earlier_equal = (keys[:, None] == keys[None, :]) & (places[None, :] < places[:, None])
    return jnp.sum(earlier_equal.astype(jnp.int32), axis=1)


def shards(embeddings, document_cluster_index):
    row_count = lax.axis_size("rows")
    col_count = lax.axis_size("cols")
    doc_count = embeddings.shape[0]
    width = embeddings.shape[1]
    slot_count = CAP * row_count
    values = embeddings.astype(jnp.float32)
    normed = (values * lax.rsqrt(jnp.sum(values * values, axis=1, keepdims=True) + 1e-06)).astype(
        jnp.bfloat16
    )
    owner_devices = document_cluster_index // GROUP_CLUSTERS
    within_cluster = (document_cluster_index % GROUP_CLUSTERS).astype(jnp.float32)
    slot_ranks = rank_among_equals(owner_devices)
    places = owner_devices * CAP + slot_ranks
    outgoing = jnp.zeros((slot_count, width), jnp.bfloat16).at[places].set(normed)
    out_labels = (
        jnp.full((slot_count,), -1.0, jnp.float32)
        .at[places]
        .set(within_cluster)
        .astype(jnp.bfloat16)
    )
    resident, res_labels = (
        lax.all_to_all(outgoing, "rows", split_axis=0, concat_axis=0, tiled=True),
        lax.all_to_all(out_labels, "rows", split_axis=0, concat_axis=0, tiled=True),
    )
    home_labels = res_labels.astype(jnp.float32)
    partner_count = max(1, col_count // GROUP_CLUSTERS)
    owned_count = max(1, GROUP_CLUSTERS // col_count)
    slot_quota = 2 * slot_count // GROUP_CLUSTERS // partner_count
    send_total = col_count * owned_count * slot_quota
    local_cluster = res_labels.astype(jnp.int32)
    occupied = local_cluster >= 0
    cluster_rank = rank_among_equals(local_cluster)
    member_slot = cluster_rank % partner_count
    cluster_depth = cluster_rank // partner_count
    destination = local_cluster // owned_count * partner_count + member_slot
    send_place = (
        destination * (owned_count * slot_quota)
        + local_cluster % owned_count * slot_quota
        + cluster_depth
    )
    send_place = jnp.where(occupied, send_place, send_total)
    send_rows = (
        jnp.zeros((send_total, width), jnp.bfloat16).at[send_place].set(resident, mode="drop")
    )
    send_labels = (
        jnp.full((send_total,), -1.0, jnp.float32)
        .at[send_place]
        .set(home_labels, mode="drop")
        .astype(jnp.bfloat16)
    )
    got_rows, got_labels = (
        lax.all_to_all(send_rows, "cols", split_axis=0, concat_axis=0, tiled=True),
        lax.all_to_all(send_labels, "cols", split_axis=0, concat_axis=0, tiled=True),
    )
    member_index = lax.axis_index("cols") % partner_count
    gathered_rows, gathered_labels = (got_rows, got_labels)
    for bit in range(partner_count.bit_length() - 1):
        other_rows, other_labels = from_partner((gathered_rows, gathered_labels), "cols", bit)
        upper = member_index // 2**bit % 2 == 1
        gathered_rows = jnp.where(
            upper,
            jnp.concatenate([other_rows, gathered_rows], axis=0),
            jnp.concatenate([gathered_rows, other_rows], axis=0),
        )
        gathered_labels = jnp.where(
            upper,
            jnp.concatenate([other_labels, gathered_labels], axis=0),
            jnp.concatenate([gathered_labels, other_labels], axis=0),
        )
    similarity_scores = lax.dot_general(
        got_rows, gathered_rows, (((1,), (1,)), ((), ())), preferred_element_type=jnp.float32
    )
    own_labels = got_labels.astype(jnp.float32)
    all_labels = gathered_labels.astype(jnp.float32)
    column_index = jnp.arange(gathered_rows.shape[0], dtype=jnp.int32)
    own_index = member_index * send_total + jnp.arange(send_total, dtype=jnp.int32)
    same_cluster = (own_labels[:, None] == all_labels[None, :]) & (own_labels[:, None] >= 0.0)
    same_cluster = same_cluster & (own_index[:, None] != column_index[None, :])
    best_owned = jnp.max(jnp.where(same_cluster, similarity_scores, -1.0), axis=1)
    came_back = lax.all_to_all(best_owned, "cols", split_axis=0, concat_axis=0, tiled=True)
    row_best = jnp.where(occupied, came_back[jnp.minimum(send_place, send_total - 1)], -1.0)
    answers = lax.all_to_all(row_best, "rows", split_axis=0, concat_axis=0, tiled=True)
    max_similarity = answers[places]
    bin_width = 2.0 / (BINS - 1)
    centers = -1.0 + jnp.arange(BINS, dtype=jnp.float32) * bin_width
    bin_weights = jax.nn.relu(1.0 - jnp.abs(max_similarity[:, None] - centers[None, :]) / bin_width)
    bin_totals = lax.psum(jnp.sum(bin_weights, axis=0), ("rows", "cols"))
    return (max_similarity, bin_totals / (doc_count * row_count * col_count))


CHUNKS = (32, 32, 16, 16, 16, 16)
TWICE = (5, 0)
LATE = 2


def meet_kernel(doc_total, emb_hbm, cluster_hbm, out_ref, emb_ref, cluster_ref, keys, keys_t, blocks, key_labels,
                block_labels, key_best, far_send, final_send, final_box, side_box, far_box, final_best,
                packets, answer_box, in_sems, plane_sems, chunk_sems, twice_sems, block_sems, label_sems, final_sems, side_sems,
                far_sems, packet_sems):
    row, col = lax.axis_index("rows"), lax.axis_index("cols")
    z, core = col // CORES, col % CORES
    row_at = (row, row + 1 - 2 * (row % 2), row + 2 - 4 * (row // 2), 3 - row)
    core_at = (core, 1 - core)
    near = len(row_at)
    slots = near * CORES
    docs, width = emb_ref.shape
    half = docs // 2

    def at_slot(slot, plane):
        return (row_at[slot % near], plane * CORES + core_at[slot // near])

    def above_me(plane):
        return (row, plane * CORES + core)

    me = core * near + row

    def order_of(slot):
        return core_at[slot // near] * near + row_at[slot % near]

    x_peer, y_peer, core_peer = at_slot(1, z), at_slot(2, z), at_slot(near, z)

    def copy(source, target, sems, at, where):
        return pltpu.make_async_remote_copy(
            src_ref=source, dst_ref=target, send_sem=sems.at[(0, *at)], recv_sem=sems.at[(1, *at)],
            device_id=where, device_id_type=pl.DeviceIdType.MESH)

    barrier = pltpu.get_barrier_semaphore()

    def greet(where):
        pl.semaphore_signal(barrier, inc=1, device_id=where, device_id_type=pl.DeviceIdType.MESH)

    senders = {0: (3, 2, 1), 1: (2, 0), 2: (3,), 3: (2,)}
    for plane, sources in senders.items():
        @pl.when(z == plane)
        def _():
            for source in sources:
                greet(above_me(source))
    for peer in (x_peer, y_peer, core_peer):
        greet(peer)
    load = pltpu.make_async_copy(emb_hbm, emb_ref, in_sems.at[0])
    load_labels = pltpu.make_async_copy(cluster_hbm, cluster_ref, in_sems.at[1])
    load.start()
    load_labels.start()
    load_labels.wait()
    key_labels[0] = cluster_ref[...].astype(jnp.float32)
    load.wait()
    values = emb_ref[...].astype(jnp.float32)
    normed = values * lax.rsqrt(jnp.sum(values * values, axis=1, keepdims=True) + 1e-06)
    keys[0:docs, :] = normed.astype(jnp.bfloat16)
    for plane in senders:
        @pl.when(z == plane)
        def _():
            pl.semaphore_wait(barrier, 3 + sum(plane in sources for sources in senders.values()))

    def part(slot, first, size):
        return keys.at[pl.ds(slot * docs + first, size)]

    def plane_copy(n):
        source, target, first, size, where = (
            (0, 1, 0, half, x_peer),
            (0, 2, half, half, y_peer),
            (0, 1, half, half, x_peer),
            (0, 2, 0, half, y_peer),
            (1, 3, 0, half, y_peer),
            (2, 3, half, half, x_peer),
            (0, 4, 0, docs, core_peer),
            (1, 5, 0, docs, core_peer),
            (2, 6, 0, docs, core_peer),
            (3, 7, 0, docs, core_peer),
        )[n]
        return copy(part(source, first, size), part(target, first, size), plane_sems, (n,), where)

    def plane_label(n):
        source, target, count, where = ((0, 1, 1, x_peer), (0, 2, 1, y_peer), (1, 3, 1, y_peer), (0, near, near, core_peer))[n]
        return copy(key_labels.at[pl.ds(source, count)], key_labels.at[pl.ds(target, count)], label_sems, (n,), where)

    def start(*copies):
        for item in copies:
            item.start()

    def arrive(*copies):
        for item in copies:
            item.wait_recv()

    def sent(*copies):
        for item in copies:
            item.wait_send()

    firsts = [sum(CHUNKS[:i]) for i in range(len(CHUNKS))]

    def chunk(n, i, source, plane):
        rows = pl.ds(firsts[i], CHUNKS[i])
        block = blocks.at[n, rows]
        return copy(keys.at[rows] if source is None else block, block, chunk_sems, (n, i), above_me(plane))

    def twice(i):
        rows = pl.ds(firsts[i], CHUNKS[i])
        return copy(keys.at[rows], blocks.at[0, rows], twice_sems, (i,), above_me(0))

    def whole(n, plane):
        return copy(keys.at[pl.ds(0, docs)], blocks.at[2], block_sems, (n,), above_me(plane))

    def block_label(n, plane, at, source=None):
        held = block_labels.at[n]
        return copy(key_labels.at[0] if source is None else held, held, label_sems, (4 + at,), above_me(plane))

    def turn(slot):
        keys_t[:, slot * docs:(slot + 1) * docs] = keys[slot * docs:(slot + 1) * docs, :].T

    def plane_start():
        start(plane_label(0), plane_label(1), plane_copy(0), plane_copy(1), plane_copy(2), plane_copy(3), plane_copy(6))
        turn(0)

    def plane_diagonal():
        arrive(plane_copy(0))
        start(plane_copy(4))
        arrive(plane_copy(1))
        start(plane_copy(5))
        arrive(plane_label(0))
        start(plane_label(2))

    def plane_across():
        arrive(plane_copy(2))
        start(plane_copy(7))
        arrive(plane_copy(3))
        start(plane_copy(8))
        turn(1)
        turn(2)

    def plane_last():
        arrive(plane_copy(4), plane_copy(5))
        start(plane_copy(9))
        arrive(plane_label(1), plane_label(2))
        start(plane_label(3))
        turn(3)

    def plane_ready():
        for n in range(6, 10):
            arrive(plane_copy(n))
            turn(n - 2)
        arrive(plane_label(3))

    def plane_sent():
        sent(*[plane_copy(n) for n in range(10)], *[plane_label(n) for n in range(4)])

    same_place = lax.broadcasted_iota(jnp.int32, (docs, docs), 0) == lax.broadcasted_iota(jnp.int32, (docs, docs), 1)

    def score(queries, labels, own, fresh=True, keep=True, done=None):
        parts = len(queries)
        query = queries[0] if parts == 1 else jnp.concatenate(queries, axis=0)
        scores = jnp.dot(query, keys_t[...], preferred_element_type=jnp.float32)
        columns = [jnp.broadcast_to(label, (docs, docs)).T for label in labels]
        tops = [None] * parts
        for slot in range(slots):
            best = None if fresh else key_best[slot]
            for n in range(parts):
                same = columns[n] == key_labels[slot]
                if own and n == 0 and slot == 0:
                    same = same & jnp.logical_not(same_place)
                found = jnp.where(same, scores[n * docs:(n + 1) * docs, slot * docs:(slot + 1) * docs], -1.0)
                tops[n] = found if slot == 0 else jnp.maximum(tops[n], found)
                group = jnp.max(found.reshape(docs // 8, 8, docs), axis=0)
                best = group if best is None else jnp.maximum(best, group)
            if done is not None:
                done(slot, jnp.max(best, axis=0, keepdims=True))
            elif keep:
                key_best[slot] = best
        return [jnp.max(top.T, axis=0, keepdims=True) for top in tops]

    bins_per_unit = (BINS - 1) / 2.0
    centers = lax.broadcasted_iota(jnp.int32, (BINS, docs), 0).astype(jnp.float32) - bins_per_unit

    def missed(rows):
        scaled = rows * bins_per_unit
        return sum(jnp.minimum(jnp.abs(scaled[n:n + 1] - centers), 1.0) for n in range(rows.shape[0]))

    def spread(send, box, sems, to, source):
        return pltpu.make_async_remote_copy(
            src_ref=send, dst_ref=box.at[source], send_sem=sems.at[0, to], recv_sem=sems.at[1, source],
            device_id=(to % near, to // near), device_id_type=pl.DeviceIdType.MESH)

    def final_copy(to, source):
        return spread(final_send, final_box, final_sems, to, source)

    def side_copy(to, source):
        return spread(final_send, side_box, side_sems, to, source)

    def far_copy(to, plane, source):
        return spread(far_send, far_box.at[plane - 2], far_sems.at[:, plane - 2], to, source)

    def keep_final(mine):
        def keep(slot, best):
            final_send[pl.ds(order_of(slot), 1), :] = best if slot else jnp.maximum(mine, best)

        return keep

    reached = (1, 0, near + 1, near, 2, near + 2, 3, near + 3)

    def with_others(act):
        for other in reached:
            pl.when(other != me)(functools.partial(act, other))

    def packet(slot, plane):
        return copy(packets.at[slot, plane - 1], answer_box, packet_sems, (slot, plane), at_slot(slot, plane))

    def take_answer(plane):
        pl.when(row == 0)(lambda: arrive(packet(1, plane)))
        pl.when(row != 0)(lambda: arrive(packet(0, plane)))
        out_ref[...] = answer_box[...]

    every = range(len(CHUNKS))

    def by_core(act):
        for at, count in enumerate(TWICE):
            cut = len(CHUNKS) - count
            pl.when(core == at)(functools.partial(act, every[:cut], every[cut:]))

    for plane in (2, 3):
        @pl.when(z == plane)
        def _():
            other = 5 - plane
            aside = [block_label(2, other, 4), whole(0, other)]
            if plane == 3:
                down = [block_label(1, 0, 2), *[chunk(1, i, None, 0) for i in every]] + aside
            else:
                down = [*aside, block_label(0, 1, 0), block_label(0, 0, 1)]
            start(*down)
            if plane == 2:
                by_core(lambda once, again: start(
                    *[chunk(0, i, None, 1) for i in once], *[twice(i) for i in again[:-LATE]],
                    *[chunk(0, i, None, 1) for i in again], *[twice(i) for i in again[-LATE:]]))
            plane_start()
            plane_diagonal()
            plane_across()
            plane_last()
            plane_ready()
            arrive(block_label(2, plane, 4), whole(0, plane))
            own, theirs = score([keys[0:docs, :], blocks[2]], [key_labels[0], block_labels[2]], True, keep=False)
            far_send[0:1, :] = own
            far_send[1:2, :] = theirs
            far = [far_copy(to, plane, me) for to in range(slots)]
            start(*far)
            sent(*down)
            if plane == 2:
                by_core(lambda once, again: sent(*[chunk(0, i, None, 1) for i in every], *[twice(i) for i in again]))
            plane_sent()
            sent(*far)
            take_answer(plane)

    @pl.when(z == 1)
    def _():
        plane_start()

        def forward(*indices):
            for i in indices:
                arrive(chunk(0, i, 0, 0))
                start(chunk(0, i, 0, 0))

        plane_diagonal()
        plane_across()
        by_core(lambda once, again: forward(*once[:2]))
        plane_last()
        by_core(lambda once, again: forward(*once[2:]))
        plane_ready()
        arrive(block_label(2, 1, 5), whole(1, 1))
        mine, first = score([keys[0:docs, :], blocks[2]], [key_labels[0], block_labels[2]], True)
        arrive(block_label(0, 1, 0), block_label(1, 1, 3, 1), *[chunk(1, i, 1, 1) for i in every])
        by_core(lambda once, again: arrive(*[chunk(0, i, 0, 0) for i in again]))
        second, third = score(
            [blocks[0], blocks[1]], [block_labels[0], block_labels[1]], False, fresh=False, done=keep_final(mine))
        for n, best in enumerate((second, third, first)):
            final_send[slots + n:slots + n + 1, :] = best
        for other in reached:
            side_copy(other, me).start()
        by_core(lambda once, again: sent(*[chunk(0, i, 0, 0) for i in once]))
        plane_sent()
        sent(*[side_copy(other, me) for other in range(slots)])
        take_answer(1)

    @pl.when(z == 0)
    def _():
        start(block_label(2, 1, 5), whole(1, 1))
        plane_start()

        def forward(*indices):
            for i in indices:
                arrive(chunk(1, i, 1, 1))
                start(chunk(1, i, 1, 1))

        plane_diagonal()
        forward(*every[:2])
        plane_across()
        forward(*every[2:])
        arrive(block_label(1, 0, 2))
        start(block_label(1, 1, 3, 1))
        plane_last()
        plane_ready()
        mine, third = score([keys[0:docs, :], blocks[1]], [key_labels[0], block_labels[1]], True)
        arrive(block_label(0, 0, 1))
        by_core(lambda once, again: arrive(*[chunk(0, i, 0, 0) for i in once], *[twice(i) for i in again]))
        second = score([blocks[0]], [block_labels[0]], False, fresh=False, done=keep_final(mine))[0]
        for n, best in enumerate((second, third, mine)):
            final_send[slots + n:slots + n + 1, :] = best
        with_others(lambda other: final_copy(other, me).start())
        final_box[pl.ds(me, 1)] = final_send[...].reshape(1, slots + 3, docs)
        sent(block_label(2, 1, 5), whole(1, 1), block_label(1, 1, 3, 1), *[chunk(1, i, 1, 1) for i in every])
        plane_sent()
        arrive(*[side_copy(0, source) for source in range(slots)])
        final_best[1] = jnp.max(side_box[:, :slots, :], axis=0)
        lacking = missed(final_best[1])
        for plane in (2, 3):
            arrive(*[far_copy(0, plane, source) for source in range(slots)])
        for n in range(2):
            final_best[2 + n] = jnp.maximum(
                side_box[:, slots + n, :], jnp.maximum(far_box[n, :, 0, :], far_box[1 - n, :, 1, :]))
        for slot in (0, near, 1, 2, near + 1, near + 2, 3, near + 3):
            source = order_of(slot)
            if slot:
                final_copy(0, source).wait_recv()
            for n in range(2):
                place = pl.ds(source, 1)
                best = jnp.maximum(final_best[2 + n, place, :], final_box[source, slots + n:slots + n + 1, :])
                final_best[2 + n, place, :] = best
                lacking = lacking + missed(best)
        final_best[0] = jnp.maximum(jnp.max(final_box[:, :slots, :], axis=0), side_box[:, slots + 2, :])
        lacking = lacking + missed(final_best[0])
        totals = jnp.sum((4 * slots - lacking).T, axis=0, keepdims=True) / doc_total
        out_ref[0] = final_best[0, pl.ds(me, 1), :]
        out_ref[1] = totals

        def finish(targets):
            for slot in targets:
                for plane in (1, 3, 2):
                    packets[slot, plane - 1, 0] = final_best[plane, pl.ds(order_of(slot), 1), :]
                    packets[slot, plane - 1, 1] = totals
                    packet(slot, plane).start()

        pl.when(row == 1)(lambda: finish((1,)))
        pl.when(row != 0)(lambda: finish((0,)))
        with_others(lambda other: final_copy(other, me).wait_send())

        def finished(targets):
            sent(*[packet(slot, plane) for slot in targets for plane in (3, 2, 1)])

        pl.when(row == 1)(lambda: finished((1,)))
        pl.when(row != 0)(lambda: finished((0,)))


def meet_shards(embeddings, document_cluster_index):
    rows, cols = lax.axis_size("rows"), lax.axis_size("cols")
    docs, width = embeddings.shape
    slots = rows * CORES
    hbm, vmem = pl.BlockSpec(memory_space=pl.ANY), pl.BlockSpec(memory_space=pltpu.VMEM)
    dma = pltpu.SemaphoreType.DMA
    line = lambda *lead: pltpu.VMEM((*lead, 1, docs), jnp.float32)
    found = pl.pallas_call(
        functools.partial(meet_kernel, docs * rows * cols),
        out_shape=pltpu.VMEM((2, 1, docs), jnp.float32),
        in_specs=[hbm, hbm],
        out_specs=vmem,
        scratch_shapes=[
            pltpu.VMEM((docs, width), jnp.bfloat16),
            pltpu.VMEM((1, docs), jnp.int32),
            pltpu.VMEM((slots * docs, width), jnp.bfloat16),
            pltpu.VMEM((width, slots * docs), jnp.bfloat16),
            pltpu.VMEM((3, docs, width), jnp.bfloat16),
            line(slots),
            line(3),
            pltpu.VMEM((slots, 8, docs), jnp.float32),
            pltpu.VMEM((2, docs), jnp.float32),
            pltpu.VMEM((slots + 3, docs), jnp.float32),
            pltpu.VMEM((slots, slots + 3, docs), jnp.float32),
            pltpu.VMEM((slots, slots + 3, docs), jnp.float32),
            pltpu.VMEM((2, slots, 2, docs), jnp.float32),
            pltpu.VMEM((4, slots, docs), jnp.float32),
            line(2, 3, 2),
            line(2),
            dma((2,)),
            dma((2, 10)),
            dma((2, 2, len(CHUNKS))),
            dma((2, len(CHUNKS))),
            dma((2, 2)),
            dma((2, 10)),
            dma((2, slots)),
            dma((2, slots)),
            dma((2, 2, slots)),
            dma((2, 2, 4)),
        ],
        compiler_params=pltpu.CompilerParams(collective_id=0, has_side_effects=True),
    )(embeddings, document_cluster_index.reshape(1, docs))
    return found[0, 0], found[1, 0]


def solution(mesh):
    placed = (P(("rows", "cols"), None), P(("rows", "cols")))
    rows, planes = mesh.shape["rows"], mesh.shape["cols"] // CORES
    direct = rows == 4 and planes == rows
    return jax.shard_map(
        meet_shards if direct else shards, mesh=mesh, in_specs=placed,
        out_specs=(P(("rows", "cols")), P()), check_vma=False
    )
```

```python
import functools

import jax
import jax.numpy as jnp
from jax import lax
from jax.experimental import pallas as pl
from jax.experimental.pallas import tpu as pltpu
from jax.sharding import PartitionSpec as P

CAP = 64
GROUP_CLUSTERS = 16
BINS = 128
CORES = 2


def from_partner(value, axis, bit):
    mask = 2**bit
    pairs = [(source, source ^ mask) for source in range(lax.axis_size(axis))]
    return lax.ppermute(value, axis, pairs)


def rank_among_equals(keys):
    places = jnp.arange(keys.shape[0], dtype=jnp.int32)
    earlier_equal = (keys[:, None] == keys[None, :]) & (places[None, :] < places[:, None])
    return jnp.sum(earlier_equal.astype(jnp.int32), axis=1)


def shards(embeddings, document_cluster_index):
    row_count = lax.axis_size("rows")
    col_count = lax.axis_size("cols")
    doc_count = embeddings.shape[0]
    width = embeddings.shape[1]
    slot_count = CAP * row_count
    values = embeddings.astype(jnp.float32)
    normed = (values * lax.rsqrt(jnp.sum(values * values, axis=1, keepdims=True) + 1e-06)).astype(
        jnp.bfloat16
    )
    owner_devices = document_cluster_index // GROUP_CLUSTERS
    within_cluster = (document_cluster_index % GROUP_CLUSTERS).astype(jnp.float32)
    slot_ranks = rank_among_equals(owner_devices)
    places = owner_devices * CAP + slot_ranks
    outgoing = jnp.zeros((slot_count, width), jnp.bfloat16).at[places].set(normed)
    out_labels = (
        jnp.full((slot_count,), -1.0, jnp.float32)
        .at[places]
        .set(within_cluster)
        .astype(jnp.bfloat16)
    )
    resident, res_labels = (
        lax.all_to_all(outgoing, "rows", split_axis=0, concat_axis=0, tiled=True),
        lax.all_to_all(out_labels, "rows", split_axis=0, concat_axis=0, tiled=True),
    )
    home_labels = res_labels.astype(jnp.float32)
    partner_count = max(1, col_count // GROUP_CLUSTERS)
    owned_count = max(1, GROUP_CLUSTERS // col_count)
    slot_quota = 2 * slot_count // GROUP_CLUSTERS // partner_count
    send_total = col_count * owned_count * slot_quota
    local_cluster = res_labels.astype(jnp.int32)
    occupied = local_cluster >= 0
    cluster_rank = rank_among_equals(local_cluster)
    member_slot = cluster_rank % partner_count
    cluster_depth = cluster_rank // partner_count
    destination = local_cluster // owned_count * partner_count + member_slot
    send_place = (
        destination * (owned_count * slot_quota)
        + local_cluster % owned_count * slot_quota
        + cluster_depth
    )
    send_place = jnp.where(occupied, send_place, send_total)
    send_rows = (
        jnp.zeros((send_total, width), jnp.bfloat16).at[send_place].set(resident, mode="drop")
    )
    send_labels = (
        jnp.full((send_total,), -1.0, jnp.float32)
        .at[send_place]
        .set(home_labels, mode="drop")
        .astype(jnp.bfloat16)
    )
    got_rows, got_labels = (
        lax.all_to_all(send_rows, "cols", split_axis=0, concat_axis=0, tiled=True),
        lax.all_to_all(send_labels, "cols", split_axis=0, concat_axis=0, tiled=True),
    )
    member_index = lax.axis_index("cols") % partner_count
    gathered_rows, gathered_labels = (got_rows, got_labels)
    for bit in range(partner_count.bit_length() - 1):
        other_rows, other_labels = from_partner((gathered_rows, gathered_labels), "cols", bit)
        upper = member_index // 2**bit % 2 == 1
        gathered_rows = jnp.where(
            upper,
            jnp.concatenate([other_rows, gathered_rows], axis=0),
            jnp.concatenate([gathered_rows, other_rows], axis=0),
        )
        gathered_labels = jnp.where(
            upper,
            jnp.concatenate([other_labels, gathered_labels], axis=0),
            jnp.concatenate([gathered_labels, other_labels], axis=0),
        )
    similarity_scores = lax.dot_general(
        got_rows, gathered_rows, (((1,), (1,)), ((), ())), preferred_element_type=jnp.float32
    )
    own_labels = got_labels.astype(jnp.float32)
    all_labels = gathered_labels.astype(jnp.float32)
    column_index = jnp.arange(gathered_rows.shape[0], dtype=jnp.int32)
    own_index = member_index * send_total + jnp.arange(send_total, dtype=jnp.int32)
    same_cluster = (own_labels[:, None] == all_labels[None, :]) & (own_labels[:, None] >= 0.0)
    same_cluster = same_cluster & (own_index[:, None] != column_index[None, :])
    best_owned = jnp.max(jnp.where(same_cluster, similarity_scores, -1.0), axis=1)
    came_back = lax.all_to_all(best_owned, "cols", split_axis=0, concat_axis=0, tiled=True)
    row_best = jnp.where(occupied, came_back[jnp.minimum(send_place, send_total - 1)], -1.0)
    answers = lax.all_to_all(row_best, "rows", split_axis=0, concat_axis=0, tiled=True)
    max_similarity = answers[places]
    bin_width = 2.0 / (BINS - 1)
    centers = -1.0 + jnp.arange(BINS, dtype=jnp.float32) * bin_width
    bin_weights = jax.nn.relu(1.0 - jnp.abs(max_similarity[:, None] - centers[None, :]) / bin_width)
    bin_totals = lax.psum(jnp.sum(bin_weights, axis=0), ("rows", "cols"))
    return (max_similarity, bin_totals / (doc_count * row_count * col_count))


CHUNKS = (2, 2, 1, 1, 1, 1)
TWICE = (5, 0)
LATE = 2


def meet_kernel(doc_total, emb_hbm, cluster_hbm, out_ref, emb_ref, cluster_ref, keys, keys_t, blocks, key_labels,
                block_labels, key_best, far_send, final_send, final_box, side_box, far_box, final_best,
                packets, answer_box, in_sems, plane_sems, chunk_sems, twice_sems, block_sems, label_sems, final_sems, side_sems,
                far_sems, packet_sems):
    row, col = lax.axis_index("rows"), lax.axis_index("cols")
    z, core = col // CORES, col % CORES
    row_at = (row, row + 1 - 2 * (row % 2), row + 2 - 4 * (row // 2), 3 - row)
    core_at = (core, 1 - core)
    near = len(row_at)
    slots = near * CORES
    docs, width = emb_ref.shape
    half = docs // 2

    def at_slot(slot, plane):
        return (row_at[slot % near], plane * CORES + core_at[slot // near])

    def above_me(plane):
        return (row, plane * CORES + core)

    me = core * near + row

    def order_of(slot):
        return core_at[slot // near] * near + row_at[slot % near]

    x_peer, y_peer, core_peer = at_slot(1, z), at_slot(2, z), at_slot(near, z)

    def copy(source, target, sems, at, where):
        return pltpu.make_async_remote_copy(
            src_ref=source, dst_ref=target, send_sem=sems.at[(0, *at)], recv_sem=sems.at[(1, *at)],
            device_id=where, device_id_type=pl.DeviceIdType.MESH)

    barrier = pltpu.get_barrier_semaphore()

    def greet(where):
        pl.semaphore_signal(barrier, inc=1, device_id=where, device_id_type=pl.DeviceIdType.MESH)

    senders = {0: (3, 2, 1), 1: (2, 0), 2: (3,), 3: (2,)}
    for plane, sources in senders.items():
        @pl.when(z == plane)
        def _():
            for source in sources:
                greet(above_me(source))
    for peer in (x_peer, y_peer, core_peer):
        greet(peer)
    load = pltpu.make_async_copy(emb_hbm, emb_ref, in_sems.at[0])
    load_labels = pltpu.make_async_copy(cluster_hbm, cluster_ref, in_sems.at[1])
    load.start()
    load_labels.start()
    load_labels.wait()
    key_labels[0] = cluster_ref[...].astype(jnp.float32)
    load.wait()
    values = emb_ref[...].astype(jnp.float32)
    normed = values * lax.rsqrt(jnp.sum(values * values, axis=1, keepdims=True) + 1e-06)
    keys[0:docs, :] = normed.astype(jnp.bfloat16)
    for plane in senders:
        @pl.when(z == plane)
        def _():
            pl.semaphore_wait(barrier, 3 + sum(plane in sources for sources in senders.values()))

    def part(slot, first, size):
        return keys.at[pl.ds(slot * docs + first, size)]

    def plane_copy(n):
        source, target, first, size, where = (
            (0, 1, 0, half, x_peer),
            (0, 2, half, half, y_peer),
            (0, 1, half, half, x_peer),
            (0, 2, 0, half, y_peer),
            (1, 3, 0, half, y_peer),
            (2, 3, half, half, x_peer),
            (0, 4, 0, docs, core_peer),
            (1, 5, 0, docs, core_peer),
            (2, 6, 0, docs, core_peer),
            (3, 7, 0, docs, core_peer),
        )[n]
        return copy(part(source, first, size), part(target, first, size), plane_sems, (n,), where)

    def plane_label(n):
        source, target, count, where = ((0, 1, 1, x_peer), (0, 2, 1, y_peer), (1, 3, 1, y_peer), (0, near, near, core_peer))[n]
        return copy(key_labels.at[pl.ds(source, count)], key_labels.at[pl.ds(target, count)], label_sems, (n,), where)

    def start(*copies):
        for item in copies:
            item.start()

    def arrive(*copies):
        for item in copies:
            item.wait_recv()

    def sent(*copies):
        for item in copies:
            item.wait_send()

    eighth = docs // 8

    def chunk_rows(i):
        return pl.ds(sum(CHUNKS[:i]) * eighth, CHUNKS[i] * eighth)

    def chunk(n, i, source, plane):
        rows = chunk_rows(i)
        block = blocks.at[n, rows]
        return copy(keys.at[rows] if source is None else block, block, chunk_sems, (n, i), above_me(plane))

    def twice(i):
        rows = chunk_rows(i)
        return copy(keys.at[rows], blocks.at[0, rows], twice_sems, (i,), above_me(0))

    def whole(n, plane):
        return copy(keys.at[pl.ds(0, docs)], blocks.at[2], block_sems, (n,), above_me(plane))

    def block_label(n, plane, at, source=None):
        held = block_labels.at[n]
        return copy(key_labels.at[0] if source is None else held, held, label_sems, (4 + at,), above_me(plane))

    def turn(slot):
        keys_t[:, slot * docs:(slot + 1) * docs] = keys[slot * docs:(slot + 1) * docs, :].T

    def plane_start():
        start(plane_label(0), plane_label(1), plane_copy(0), plane_copy(1), plane_copy(2), plane_copy(3), plane_copy(6))
        turn(0)

    def plane_diagonal():
        arrive(plane_copy(0))
        start(plane_copy(4))
        arrive(plane_copy(1))
        start(plane_copy(5))
        arrive(plane_label(0))
        start(plane_label(2))

    def plane_across():
        arrive(plane_copy(2))
        start(plane_copy(7))
        arrive(plane_copy(3))
        start(plane_copy(8))
        turn(1)
        turn(2)

    def plane_last():
        arrive(plane_copy(4), plane_copy(5))
        start(plane_copy(9))
        arrive(plane_label(1), plane_label(2))
        start(plane_label(3))
        turn(3)

    def plane_ready():
        for n in range(6, 10):
            arrive(plane_copy(n))
            turn(n - 2)
        arrive(plane_label(3))

    def plane_sent():
        sent(*[plane_copy(n) for n in range(10)], *[plane_label(n) for n in range(4)])

    same_place = lax.broadcasted_iota(jnp.int32, (docs, docs), 0) == lax.broadcasted_iota(jnp.int32, (docs, docs), 1)

    def score(queries, labels, own, fresh=True, keep=True, done=None):
        parts = len(queries)
        query = queries[0] if parts == 1 else jnp.concatenate(queries, axis=0)
        scores = jnp.dot(query, keys_t[...], preferred_element_type=jnp.float32)
        columns = [jnp.broadcast_to(label, (docs, docs)).T for label in labels]
        tops = [None] * parts
        for slot in range(slots):
            best = None if fresh else key_best[slot]
            for n in range(parts):
                same = columns[n] == key_labels[slot]
                if own and n == 0 and slot == 0:
                    same = same & jnp.logical_not(same_place)
                found = jnp.where(same, scores[n * docs:(n + 1) * docs, slot * docs:(slot + 1) * docs], -1.0)
                tops[n] = found if slot == 0 else jnp.maximum(tops[n], found)
                group = jnp.max(found.reshape(docs // 8, 8, docs), axis=0)
                best = group if best is None else jnp.maximum(best, group)
            if done is not None:
                done(slot, jnp.max(best, axis=0, keepdims=True))
            elif keep:
                key_best[slot] = best
        return [jnp.max(top.T, axis=0, keepdims=True) for top in tops]

    bins_per_unit = (BINS - 1) / 2.0
    centers = lax.broadcasted_iota(jnp.int32, (BINS, docs), 0).astype(jnp.float32) - bins_per_unit

    def missed(rows):
        scaled = rows * bins_per_unit
        return sum(jnp.minimum(jnp.abs(scaled[n:n + 1] - centers), 1.0) for n in range(rows.shape[0]))

    def spread(send, box, sems, to, source):
        return pltpu.make_async_remote_copy(
            src_ref=send, dst_ref=box.at[source], send_sem=sems.at[0, to], recv_sem=sems.at[1, source],
            device_id=(to % near, to // near), device_id_type=pl.DeviceIdType.MESH)

    def final_copy(to, source):
        return spread(final_send, final_box, final_sems, to, source)

    def side_copy(to, source):
        return spread(final_send, side_box, side_sems, to, source)

    def far_copy(to, plane, source):
        return spread(far_send, far_box.at[plane - 2], far_sems.at[:, plane - 2], to, source)

    def keep_final(mine):
        def keep(slot, best):
            final_send[pl.ds(order_of(slot), 1), :] = best if slot else jnp.maximum(mine, best)

        return keep

    reached = (1, 0, near + 1, near, 2, near + 2, 3, near + 3)

    def with_others(act):
        for other in reached:
            pl.when(other != me)(functools.partial(act, other))

    def packet(slot, plane):
        return copy(packets.at[slot, plane - 1], answer_box, packet_sems, (slot, plane), at_slot(slot, plane))

    def take_answer(plane):
        pl.when(row == 0)(lambda: arrive(packet(1, plane)))
        pl.when(row != 0)(lambda: arrive(packet(0, plane)))
        out_ref[...] = answer_box[...]

    every = range(len(CHUNKS))

    def by_core(act):
        for at, count in enumerate(TWICE):
            cut = len(CHUNKS) - count
            pl.when(core == at)(functools.partial(act, every[:cut], every[cut:]))

    for plane in (2, 3):
        @pl.when(z == plane)
        def _():
            other = 5 - plane
            aside = [block_label(2, other, 4), whole(0, other)]
            if plane == 3:
                down = [block_label(1, 0, 2), *[chunk(1, i, None, 0) for i in every]] + aside
            else:
                down = [*aside, block_label(0, 1, 0), block_label(0, 0, 1)]
            start(*down)
            if plane == 2:
                by_core(lambda once, again: start(
                    *[chunk(0, i, None, 1) for i in once], *[twice(i) for i in again[:-LATE]],
                    *[chunk(0, i, None, 1) for i in again], *[twice(i) for i in again[-LATE:]]))
            plane_start()
            plane_diagonal()
            plane_across()
            plane_last()
            plane_ready()
            arrive(block_label(2, plane, 4), whole(0, plane))
            own, theirs = score([keys[0:docs, :], blocks[2]], [key_labels[0], block_labels[2]], True, keep=False)
            far_send[0:1, :] = own
            far_send[1:2, :] = theirs
            far = [far_copy(to, plane, me) for to in range(slots)]
            start(*far)
            sent(*down)
            if plane == 2:
                by_core(lambda once, again: sent(*[chunk(0, i, None, 1) for i in every], *[twice(i) for i in again]))
            plane_sent()
            sent(*far)
            take_answer(plane)

    @pl.when(z == 1)
    def _():
        plane_start()

        def forward(*indices):
            for i in indices:
                arrive(chunk(0, i, 0, 0))
                start(chunk(0, i, 0, 0))

        plane_diagonal()
        plane_across()
        by_core(lambda once, again: forward(*once[:2]))
        plane_last()
        by_core(lambda once, again: forward(*once[2:]))
        plane_ready()
        arrive(block_label(2, 1, 5), whole(1, 1))
        mine, first = score([keys[0:docs, :], blocks[2]], [key_labels[0], block_labels[2]], True)
        arrive(block_label(0, 1, 0), block_label(1, 1, 3, 1), *[chunk(1, i, 1, 1) for i in every])
        by_core(lambda once, again: arrive(*[chunk(0, i, 0, 0) for i in again]))
        second, third = score(
            [blocks[0], blocks[1]], [block_labels[0], block_labels[1]], False, fresh=False, done=keep_final(mine))
        for n, best in enumerate((second, third, first)):
            final_send[slots + n:slots + n + 1, :] = best
        for other in reached:
            side_copy(other, me).start()
        by_core(lambda once, again: sent(*[chunk(0, i, 0, 0) for i in once]))
        plane_sent()
        sent(*[side_copy(other, me) for other in range(slots)])
        take_answer(1)

    @pl.when(z == 0)
    def _():
        start(block_label(2, 1, 5), whole(1, 1))
        plane_start()

        def forward(*indices):
            for i in indices:
                arrive(chunk(1, i, 1, 1))
                start(chunk(1, i, 1, 1))

        plane_diagonal()
        forward(*every[:2])
        plane_across()
        forward(*every[2:])
        arrive(block_label(1, 0, 2))
        start(block_label(1, 1, 3, 1))
        plane_last()
        plane_ready()
        mine, third = score([keys[0:docs, :], blocks[1]], [key_labels[0], block_labels[1]], True)
        arrive(block_label(0, 0, 1))
        by_core(lambda once, again: arrive(*[chunk(0, i, 0, 0) for i in once], *[twice(i) for i in again]))
        second = score([blocks[0]], [block_labels[0]], False, fresh=False, done=keep_final(mine))[0]
        for n, best in enumerate((second, third, mine)):
            final_send[slots + n:slots + n + 1, :] = best
        with_others(lambda other: final_copy(other, me).start())
        final_box[pl.ds(me, 1)] = final_send[...].reshape(1, slots + 3, docs)
        sent(block_label(2, 1, 5), whole(1, 1), block_label(1, 1, 3, 1), *[chunk(1, i, 1, 1) for i in every])
        plane_sent()
        arrive(*[side_copy(0, source) for source in range(slots)])
        final_best[1] = jnp.max(side_box[:, :slots, :], axis=0)
        lacking = missed(final_best[1])
        for plane in (2, 3):
            arrive(*[far_copy(0, plane, source) for source in range(slots)])
        for n in range(2):
            final_best[2 + n] = jnp.maximum(
                side_box[:, slots + n, :], jnp.maximum(far_box[n, :, 0, :], far_box[1 - n, :, 1, :]))
        for slot in (0, near, 1, 2, near + 1, near + 2, 3, near + 3):
            source = order_of(slot)
            if slot:
                final_copy(0, source).wait_recv()
            for n in range(2):
                place = pl.ds(source, 1)
                best = jnp.maximum(final_best[2 + n, place, :], final_box[source, slots + n:slots + n + 1, :])
                final_best[2 + n, place, :] = best
                lacking = lacking + missed(best)
        final_best[0] = jnp.maximum(jnp.max(final_box[:, :slots, :], axis=0), side_box[:, slots + 2, :])
        lacking = lacking + missed(final_best[0])
        totals = jnp.sum((4 * slots - lacking).T, axis=0, keepdims=True) / doc_total
        out_ref[0] = final_best[0, pl.ds(me, 1), :]
        out_ref[1] = totals

        def finish(targets):
            for slot in targets:
                for plane in (1, 3, 2):
                    packets[slot, plane - 1, 0] = final_best[plane, pl.ds(order_of(slot), 1), :]
                    packets[slot, plane - 1, 1] = totals
                    packet(slot, plane).start()

        pl.when(row == 1)(lambda: finish((1,)))
        pl.when(row != 0)(lambda: finish((0,)))
        with_others(lambda other: final_copy(other, me).wait_send())

        def finished(targets):
            sent(*[packet(slot, plane) for slot in targets for plane in (3, 2, 1)])

        pl.when(row == 1)(lambda: finished((1,)))
        pl.when(row != 0)(lambda: finished((0,)))


def meet_shards(embeddings, document_cluster_index):
    rows, cols = lax.axis_size("rows"), lax.axis_size("cols")
    docs, width = embeddings.shape
    slots = rows * CORES
    hbm, vmem = pl.BlockSpec(memory_space=pl.ANY), pl.BlockSpec(memory_space=pltpu.VMEM)
    dma = pltpu.SemaphoreType.DMA
    line = lambda *lead: pltpu.VMEM((*lead, 1, docs), jnp.float32)
    found = pl.pallas_call(
        functools.partial(meet_kernel, docs * rows * cols),
        out_shape=pltpu.VMEM((2, 1, docs), jnp.float32),
        in_specs=[hbm, hbm],
        out_specs=vmem,
        scratch_shapes=[
            pltpu.VMEM((docs, width), jnp.bfloat16),
            pltpu.VMEM((1, docs), jnp.int32),
            pltpu.VMEM((slots * docs, width), jnp.bfloat16),
            pltpu.VMEM((width, slots * docs), jnp.bfloat16),
            pltpu.VMEM((3, docs, width), jnp.bfloat16),
            line(slots),
            line(3),
            pltpu.VMEM((slots, 8, docs), jnp.float32),
            pltpu.VMEM((2, docs), jnp.float32),
            pltpu.VMEM((slots + 3, docs), jnp.float32),
            pltpu.VMEM((slots, slots + 3, docs), jnp.float32),
            pltpu.VMEM((slots, slots + 3, docs), jnp.float32),
            pltpu.VMEM((2, slots, 2, docs), jnp.float32),
            pltpu.VMEM((4, slots, docs), jnp.float32),
            line(2, 3, 2),
            line(2),
            dma((2,)),
            dma((2, 10)),
            dma((2, 2, len(CHUNKS))),
            dma((2, len(CHUNKS))),
            dma((2, 2)),
            dma((2, 10)),
            dma((2, slots)),
            dma((2, slots)),
            dma((2, 2, slots)),
            dma((2, 2, 4)),
        ],
        compiler_params=pltpu.CompilerParams(collective_id=0, has_side_effects=True),
    )(embeddings, document_cluster_index.reshape(1, docs))
    return found[0, 0], found[1, 0]


def solution(mesh):
    placed = (P(("rows", "cols"), None), P(("rows", "cols")))
    rows, planes = mesh.shape["rows"], mesh.shape["cols"] // CORES
    direct = rows == 4 and planes == rows
    return jax.shard_map(
        meet_shards if direct else shards, mesh=mesh, in_specs=placed,
        out_specs=(P(("rows", "cols")), P()), check_vma=False
    )
```

```python
import functools

import jax
import jax.numpy as jnp
from jax import lax
from jax.experimental import pallas as pl
from jax.experimental.pallas import tpu as pltpu
from jax.sharding import PartitionSpec as P

CAP = 64
GROUP_CLUSTERS = 16
BINS = 128
CORES = 2


def from_partner(value, axis, bit):
    mask = 2**bit
    pairs = [(source, source ^ mask) for source in range(lax.axis_size(axis))]
    return lax.ppermute(value, axis, pairs)


def rank_among_equals(keys):
    places = jnp.arange(keys.shape[0], dtype=jnp.int32)
    earlier_equal = (keys[:, None] == keys[None, :]) & (places[None, :] < places[:, None])
    return jnp.sum(earlier_equal.astype(jnp.int32), axis=1)


def shards(embeddings, document_cluster_index):
    row_count = lax.axis_size("rows")
    col_count = lax.axis_size("cols")
    doc_count = embeddings.shape[0]
    width = embeddings.shape[1]
    slot_count = CAP * row_count
    values = embeddings.astype(jnp.float32)
    normed = (values * lax.rsqrt(jnp.sum(values * values, axis=1, keepdims=True) + 1e-06)).astype(
        jnp.bfloat16
    )
    owner_devices = document_cluster_index // GROUP_CLUSTERS
    within_cluster = (document_cluster_index % GROUP_CLUSTERS).astype(jnp.float32)
    slot_ranks = rank_among_equals(owner_devices)
    places = owner_devices * CAP + slot_ranks
    outgoing = jnp.zeros((slot_count, width), jnp.bfloat16).at[places].set(normed)
    out_labels = (
        jnp.full((slot_count,), -1.0, jnp.float32)
        .at[places]
        .set(within_cluster)
        .astype(jnp.bfloat16)
    )
    resident, res_labels = (
        lax.all_to_all(outgoing, "rows", split_axis=0, concat_axis=0, tiled=True),
        lax.all_to_all(out_labels, "rows", split_axis=0, concat_axis=0, tiled=True),
    )
    home_labels = res_labels.astype(jnp.float32)
    partner_count = max(1, col_count // GROUP_CLUSTERS)
    owned_count = max(1, GROUP_CLUSTERS // col_count)
    slot_quota = 2 * slot_count // GROUP_CLUSTERS // partner_count
    send_total = col_count * owned_count * slot_quota
    local_cluster = res_labels.astype(jnp.int32)
    occupied = local_cluster >= 0
    cluster_rank = rank_among_equals(local_cluster)
    member_slot = cluster_rank % partner_count
    cluster_depth = cluster_rank // partner_count
    destination = local_cluster // owned_count * partner_count + member_slot
    send_place = (
        destination * (owned_count * slot_quota)
        + local_cluster % owned_count * slot_quota
        + cluster_depth
    )
    send_place = jnp.where(occupied, send_place, send_total)
    send_rows = (
        jnp.zeros((send_total, width), jnp.bfloat16).at[send_place].set(resident, mode="drop")
    )
    send_labels = (
        jnp.full((send_total,), -1.0, jnp.float32)
        .at[send_place]
        .set(home_labels, mode="drop")
        .astype(jnp.bfloat16)
    )
    got_rows, got_labels = (
        lax.all_to_all(send_rows, "cols", split_axis=0, concat_axis=0, tiled=True),
        lax.all_to_all(send_labels, "cols", split_axis=0, concat_axis=0, tiled=True),
    )
    member_index = lax.axis_index("cols") % partner_count
    gathered_rows, gathered_labels = (got_rows, got_labels)
    for bit in range(partner_count.bit_length() - 1):
        other_rows, other_labels = from_partner((gathered_rows, gathered_labels), "cols", bit)
        upper = member_index // 2**bit % 2 == 1
        gathered_rows = jnp.where(
            upper,
            jnp.concatenate([other_rows, gathered_rows], axis=0),
            jnp.concatenate([gathered_rows, other_rows], axis=0),
        )
        gathered_labels = jnp.where(
            upper,
            jnp.concatenate([other_labels, gathered_labels], axis=0),
            jnp.concatenate([gathered_labels, other_labels], axis=0),
        )
    similarity_scores = lax.dot_general(
        got_rows, gathered_rows, (((1,), (1,)), ((), ())), preferred_element_type=jnp.float32
    )
    own_labels = got_labels.astype(jnp.float32)
    all_labels = gathered_labels.astype(jnp.float32)
    column_index = jnp.arange(gathered_rows.shape[0], dtype=jnp.int32)
    own_index = member_index * send_total + jnp.arange(send_total, dtype=jnp.int32)
    same_cluster = (own_labels[:, None] == all_labels[None, :]) & (own_labels[:, None] >= 0.0)
    same_cluster = same_cluster & (own_index[:, None] != column_index[None, :])
    best_owned = jnp.max(jnp.where(same_cluster, similarity_scores, -1.0), axis=1)
    came_back = lax.all_to_all(best_owned, "cols", split_axis=0, concat_axis=0, tiled=True)
    row_best = jnp.where(occupied, came_back[jnp.minimum(send_place, send_total - 1)], -1.0)
    answers = lax.all_to_all(row_best, "rows", split_axis=0, concat_axis=0, tiled=True)
    max_similarity = answers[places]
    bin_width = 2.0 / (BINS - 1)
    centers = -1.0 + jnp.arange(BINS, dtype=jnp.float32) * bin_width
    bin_weights = jax.nn.relu(1.0 - jnp.abs(max_similarity[:, None] - centers[None, :]) / bin_width)
    bin_totals = lax.psum(jnp.sum(bin_weights, axis=0), ("rows", "cols"))
    return (max_similarity, bin_totals / (doc_count * row_count * col_count))


CHUNKS = (2, 2, 1, 1, 1, 1)
TWICE = (5, 0)
LATE = 2


def meet_kernel(doc_total, emb_hbm, cluster_hbm, out_ref, emb_ref, cluster_ref, keys, keys_t, blocks, key_labels,
                block_labels, key_best, far_send, final_send, final_box, side_box, far_box, final_best,
                packets, answer_box, in_sems, plane_sems, chunk_sems, twice_sems, block_sems, label_sems, final_sems, side_sems,
                far_sems, packet_sems):
    row, col = lax.axis_index("rows"), lax.axis_index("cols")
    z, core = col // CORES, col % CORES
    row_at = (row, row + 1 - 2 * (row % 2), row + 2 - 4 * (row // 2), 3 - row)
    core_at = (core, 1 - core)
    near = len(row_at)
    slots = near * CORES
    docs, width = emb_ref.shape
    half = docs // 2

    def at_slot(slot, plane):
        return (row_at[slot % near], plane * CORES + core_at[slot // near])

    def above_me(plane):
        return (row, plane * CORES + core)

    me = core * near + row

    def order_of(slot):
        return core_at[slot // near] * near + row_at[slot % near]

    x_peer, y_peer, core_peer = at_slot(1, z), at_slot(2, z), at_slot(near, z)

    def copy(source, target, sems, at, where):
        return pltpu.make_async_remote_copy(
            src_ref=source, dst_ref=target, send_sem=sems.at[(0, *at)], recv_sem=sems.at[(1, *at)],
            device_id=where, device_id_type=pl.DeviceIdType.MESH)

    barrier = pltpu.get_barrier_semaphore()

    def greet(where):
        pl.semaphore_signal(barrier, inc=1, device_id=where, device_id_type=pl.DeviceIdType.MESH)

    senders = {0: (3, 2, 1), 1: (2, 0), 2: (3,), 3: (2,)}
    for plane, sources in senders.items():
        @pl.when(z == plane)
        def _():
            for source in sources:
                greet(above_me(source))
    for peer in (x_peer, y_peer, core_peer):
        greet(peer)
    load = pltpu.make_async_copy(emb_hbm, emb_ref, in_sems.at[0])
    load_labels = pltpu.make_async_copy(cluster_hbm, cluster_ref, in_sems.at[1])
    load.start()
    load_labels.start()
    load_labels.wait()
    key_labels[0] = cluster_ref[...].astype(jnp.float32)
    load.wait()
    values = emb_ref[...].astype(jnp.float32)
    normed = values * lax.rsqrt(jnp.sum(values * values, axis=1, keepdims=True) + 1e-06)
    keys[0:docs, :] = normed.astype(jnp.bfloat16)
    for plane in senders:
        @pl.when(z == plane)
        def _():
            pl.semaphore_wait(barrier, 3 + sum(plane in sources for sources in senders.values()))

    def part(slot, first, size):
        return keys.at[pl.ds(slot * docs + first, size)]

    def plane_copy(n):
        source, target, first, size, where = (
            (0, 1, 0, half, x_peer),
            (0, 2, half, half, y_peer),
            (0, 1, half, half, x_peer),
            (0, 2, 0, half, y_peer),
            (1, 3, 0, half, y_peer),
            (2, 3, half, half, x_peer),
            (0, 4, 0, docs, core_peer),
            (1, 5, 0, docs, core_peer),
            (2, 6, 0, docs, core_peer),
            (3, 7, 0, docs, core_peer),
        )[n]
        return copy(part(source, first, size), part(target, first, size), plane_sems, (n,), where)

    def plane_label(n):
        source, target, count, where = ((0, 1, 1, x_peer), (0, 2, 1, y_peer), (1, 3, 1, y_peer), (0, near, near, core_peer))[n]
        return copy(key_labels.at[pl.ds(source, count)], key_labels.at[pl.ds(target, count)], label_sems, (n,), where)

    def start(*copies):
        for item in copies:
            item.start()

    def arrive(*copies):
        for item in copies:
            item.wait_recv()

    def sent(*copies):
        for item in copies:
            item.wait_send()

    eighth = docs // 8

    def chunk_rows(i):
        return pl.ds(sum(CHUNKS[:i]) * eighth, CHUNKS[i] * eighth)

    def chunk(n, i, source, plane):
        rows = chunk_rows(i)
        block = blocks.at[n, rows]
        return copy(keys.at[rows] if source is None else block, block, chunk_sems, (n, i), above_me(plane))

    def twice(i):
        rows = chunk_rows(i)
        return copy(keys.at[rows], blocks.at[0, rows], twice_sems, (i,), above_me(0))

    def whole(n, plane):
        return copy(keys.at[pl.ds(0, docs)], blocks.at[2], block_sems, (n,), above_me(plane))

    def block_label(n, plane, at, source=None):
        held = block_labels.at[n]
        return copy(key_labels.at[0] if source is None else held, held, label_sems, (4 + at,), above_me(plane))

    def turn(slot):
        keys_t[:, slot * docs:(slot + 1) * docs] = keys[slot * docs:(slot + 1) * docs, :].T

    def plane_start():
        start(plane_copy(0), plane_copy(1), plane_label(0), plane_label(1), plane_copy(2), plane_copy(3), plane_copy(6))
        turn(0)

    def plane_diagonal():
        arrive(plane_copy(0))
        start(plane_copy(4))
        arrive(plane_copy(1))
        start(plane_copy(5))
        arrive(plane_label(0))
        start(plane_label(2))

    def plane_across():
        arrive(plane_copy(2))
        start(plane_copy(7))
        arrive(plane_copy(3))
        start(plane_copy(8))
        turn(1)
        turn(2)

    def plane_last():
        arrive(plane_copy(4), plane_copy(5))
        start(plane_copy(9))
        arrive(plane_label(1), plane_label(2))
        start(plane_label(3))
        turn(3)

    def plane_ready():
        for n in range(6, 10):
            arrive(plane_copy(n))
            turn(n - 2)
        arrive(plane_label(3))

    def plane_sent():
        sent(*[plane_copy(n) for n in range(10)], *[plane_label(n) for n in range(4)])

    same_place = lax.broadcasted_iota(jnp.int32, (docs, docs), 0) == lax.broadcasted_iota(jnp.int32, (docs, docs), 1)

    def score(queries, labels, own, fresh=True, keep=True, done=None):
        parts = len(queries)
        query = queries[0] if parts == 1 else jnp.concatenate(queries, axis=0)
        scores = jnp.dot(query, keys_t[...], preferred_element_type=jnp.float32)
        columns = [jnp.broadcast_to(label, (docs, docs)).T for label in labels]
        tops = [None] * parts
        for slot in range(slots):
            best = None if fresh else key_best[slot]
            for n in range(parts):
                same = columns[n] == key_labels[slot]
                if own and n == 0 and slot == 0:
                    same = same & jnp.logical_not(same_place)
                found = jnp.where(same, scores[n * docs:(n + 1) * docs, slot * docs:(slot + 1) * docs], -1.0)
                tops[n] = found if slot == 0 else jnp.maximum(tops[n], found)
                group = jnp.max(found.reshape(docs // 8, 8, docs), axis=0)
                best = group if best is None else jnp.maximum(best, group)
            if done is not None:
                done(slot, jnp.max(best, axis=0, keepdims=True))
            elif keep:
                key_best[slot] = best
        return [jnp.max(top.T, axis=0, keepdims=True) for top in tops]

    bins_per_unit = (BINS - 1) / 2.0
    centers = lax.broadcasted_iota(jnp.int32, (BINS, docs), 0).astype(jnp.float32) - bins_per_unit

    def missed(rows):
        scaled = rows * bins_per_unit
        return sum(jnp.minimum(jnp.abs(scaled[n:n + 1] - centers), 1.0) for n in range(rows.shape[0]))

    def spread(send, box, sems, to, source):
        return pltpu.make_async_remote_copy(
            src_ref=send, dst_ref=box.at[source], send_sem=sems.at[0, to], recv_sem=sems.at[1, source],
            device_id=(to % near, to // near), device_id_type=pl.DeviceIdType.MESH)

    def final_copy(to, source):
        return spread(final_send, final_box, final_sems, to, source)

    def side_copy(to, source):
        return spread(final_send, side_box, side_sems, to, source)

    def far_copy(to, plane, source):
        return spread(far_send, far_box.at[plane - 2], far_sems.at[:, plane - 2], to, source)

    def keep_final(mine):
        def keep(slot, best):
            final_send[pl.ds(order_of(slot), 1), :] = best if slot else jnp.maximum(mine, best)

        return keep

    reached = (1, 0, near + 1, near, 2, near + 2, 3, near + 3)

    def with_others(act):
        for other in reached:
            pl.when(other != me)(functools.partial(act, other))

    def packet(slot, plane):
        return copy(packets.at[slot, plane - 1], answer_box, packet_sems, (slot, plane), at_slot(slot, plane))

    def take_answer(plane):
        pl.when(row == 0)(lambda: arrive(packet(1, plane)))
        pl.when(row != 0)(lambda: arrive(packet(0, plane)))
        out_ref[...] = answer_box[...]

    every = range(len(CHUNKS))

    def by_core(act):
        for at, count in enumerate(TWICE):
            cut = len(CHUNKS) - count
            pl.when(core == at)(functools.partial(act, every[:cut], every[cut:]))

    for plane in (2, 3):
        @pl.when(z == plane)
        def _():
            other = 5 - plane
            aside = [block_label(2, other, 4), whole(0, other)]
            if plane == 3:
                down = [*[chunk(1, i, None, 0) for i in every], block_label(1, 0, 2)] + aside
            else:
                down = [*aside, block_label(0, 1, 0), block_label(0, 0, 1)]
            start(*down)
            if plane == 2:
                by_core(lambda once, again: start(
                    *[chunk(0, i, None, 1) for i in once], *[twice(i) for i in again[:-LATE]],
                    *[chunk(0, i, None, 1) for i in again], *[twice(i) for i in again[-LATE:]]))
            plane_start()
            plane_diagonal()
            plane_across()
            plane_last()
            plane_ready()
            arrive(block_label(2, plane, 4), whole(0, plane))
            own, theirs = score([keys[0:docs, :], blocks[2]], [key_labels[0], block_labels[2]], True, keep=False)
            far_send[0:1, :] = own
            far_send[1:2, :] = theirs
            far = [far_copy(to, plane, me) for to in range(slots)]
            start(*far)
            sent(*down)
            if plane == 2:
                by_core(lambda once, again: sent(*[chunk(0, i, None, 1) for i in every], *[twice(i) for i in again]))
            plane_sent()
            sent(*far)
            take_answer(plane)

    @pl.when(z == 1)
    def _():
        plane_start()

        def forward(*indices):
            for i in indices:
                arrive(chunk(0, i, 0, 0))
                start(chunk(0, i, 0, 0))

        plane_diagonal()
        plane_across()
        by_core(lambda once, again: forward(*once[:2]))
        plane_last()
        by_core(lambda once, again: forward(*once[2:]))
        plane_ready()
        arrive(block_label(2, 1, 5), whole(1, 1))
        mine, first = score([keys[0:docs, :], blocks[2]], [key_labels[0], block_labels[2]], True)
        arrive(block_label(0, 1, 0), block_label(1, 1, 3, 1), *[chunk(1, i, 1, 1) for i in every])
        by_core(lambda once, again: arrive(*[chunk(0, i, 0, 0) for i in again]))
        second, third = score(
            [blocks[0], blocks[1]], [block_labels[0], block_labels[1]], False, fresh=False, done=keep_final(mine))
        for n, best in enumerate((second, third, first)):
            final_send[slots + n:slots + n + 1, :] = best
        for other in reached:
            side_copy(other, me).start()
        by_core(lambda once, again: sent(*[chunk(0, i, 0, 0) for i in once]))
        plane_sent()
        sent(*[side_copy(other, me) for other in range(slots)])
        take_answer(1)

    @pl.when(z == 0)
    def _():
        start(block_label(2, 1, 5), whole(1, 1))
        plane_start()

        def forward(*indices):
            for i in indices:
                arrive(chunk(1, i, 1, 1))
                start(chunk(1, i, 1, 1))

        plane_diagonal()
        forward(*every[:2])
        plane_across()
        forward(*every[2:])
        arrive(block_label(1, 0, 2))
        start(block_label(1, 1, 3, 1))
        plane_last()
        plane_ready()
        mine, third = score([keys[0:docs, :], blocks[1]], [key_labels[0], block_labels[1]], True)
        arrive(block_label(0, 0, 1))
        by_core(lambda once, again: arrive(*[chunk(0, i, 0, 0) for i in once], *[twice(i) for i in again]))
        second = score([blocks[0]], [block_labels[0]], False, fresh=False, done=keep_final(mine))[0]
        for n, best in enumerate((second, third, mine)):
            final_send[slots + n:slots + n + 1, :] = best
        with_others(lambda other: final_copy(other, me).start())
        final_box[pl.ds(me, 1)] = final_send[...].reshape(1, slots + 3, docs)
        sent(block_label(2, 1, 5), whole(1, 1), block_label(1, 1, 3, 1), *[chunk(1, i, 1, 1) for i in every])
        plane_sent()
        arrive(*[side_copy(0, source) for source in range(slots)])
        final_best[1] = jnp.max(side_box[:, :slots, :], axis=0)
        lacking = missed(final_best[1])
        for plane in (2, 3):
            arrive(*[far_copy(0, plane, source) for source in range(slots)])
        for n in range(2):
            final_best[2 + n] = jnp.maximum(
                side_box[:, slots + n, :], jnp.maximum(far_box[n, :, 0, :], far_box[1 - n, :, 1, :]))
        for slot in (0, near, 1, 2, near + 1, near + 2, 3, near + 3):
            source = order_of(slot)
            if slot:
                final_copy(0, source).wait_recv()
            for n in range(2):
                place = pl.ds(source, 1)
                best = jnp.maximum(final_best[2 + n, place, :], final_box[source, slots + n:slots + n + 1, :])
                final_best[2 + n, place, :] = best
                lacking = lacking + missed(best)
        final_best[0] = jnp.maximum(jnp.max(final_box[:, :slots, :], axis=0), side_box[:, slots + 2, :])
        lacking = lacking + missed(final_best[0])
        totals = jnp.sum((4 * slots - lacking).T, axis=0, keepdims=True) / doc_total

        def finish(targets):
            for slot in targets:
                for plane in (1, 3, 2):
                    packets[slot, plane - 1, 0] = final_best[plane, pl.ds(order_of(slot), 1), :]
                    packets[slot, plane - 1, 1] = totals
                    packet(slot, plane).start()

        pl.when(row == 1)(lambda: finish((1,)))
        pl.when(row != 0)(lambda: finish((0,)))
        out_ref[0] = final_best[0, pl.ds(me, 1), :]
        out_ref[1] = totals
        with_others(lambda other: final_copy(other, me).wait_send())

        def finished(targets):
            sent(*[packet(slot, plane) for slot in targets for plane in (3, 2, 1)])

        pl.when(row == 1)(lambda: finished((1,)))
        pl.when(row != 0)(lambda: finished((0,)))


def meet_shards(embeddings, document_cluster_index):
    rows, cols = lax.axis_size("rows"), lax.axis_size("cols")
    docs, width = embeddings.shape
    slots = rows * CORES
    hbm, vmem = pl.BlockSpec(memory_space=pl.ANY), pl.BlockSpec(memory_space=pltpu.VMEM)
    dma = pltpu.SemaphoreType.DMA
    line = lambda *lead: pltpu.VMEM((*lead, 1, docs), jnp.float32)
    found = pl.pallas_call(
        functools.partial(meet_kernel, docs * rows * cols),
        out_shape=pltpu.VMEM((2, 1, docs), jnp.float32),
        in_specs=[hbm, hbm],
        out_specs=vmem,
        scratch_shapes=[
            pltpu.VMEM((docs, width), jnp.bfloat16),
            pltpu.VMEM((1, docs), jnp.int32),
            pltpu.VMEM((slots * docs, width), jnp.bfloat16),
            pltpu.VMEM((width, slots * docs), jnp.bfloat16),
            pltpu.VMEM((3, docs, width), jnp.bfloat16),
            line(slots),
            line(3),
            pltpu.VMEM((slots, 8, docs), jnp.float32),
            pltpu.VMEM((2, docs), jnp.float32),
            pltpu.VMEM((slots + 3, docs), jnp.float32),
            pltpu.VMEM((slots, slots + 3, docs), jnp.float32),
            pltpu.VMEM((slots, slots + 3, docs), jnp.float32),
            pltpu.VMEM((2, slots, 2, docs), jnp.float32),
            pltpu.VMEM((4, slots, docs), jnp.float32),
            line(2, 3, 2),
            line(2),
            dma((2,)),
            dma((2, 10)),
            dma((2, 2, len(CHUNKS))),
            dma((2, len(CHUNKS))),
            dma((2, 2)),
            dma((2, 10)),
            dma((2, slots)),
            dma((2, slots)),
            dma((2, 2, slots)),
            dma((2, 2, 4)),
        ],
        compiler_params=pltpu.CompilerParams(collective_id=0, has_side_effects=True),
    )(embeddings, document_cluster_index.reshape(1, docs))
    return found[0, 0], found[1, 0]


def solution(mesh):
    placed = (P(("rows", "cols"), None), P(("rows", "cols")))
    rows, planes = mesh.shape["rows"], mesh.shape["cols"] // CORES
    direct = rows == 4 and planes == rows
    return jax.shard_map(
        meet_shards if direct else shards, mesh=mesh, in_specs=placed,
        out_specs=(P(("rows", "cols")), P()), check_vma=False
    )
```

```python
import functools

import jax
import jax.numpy as jnp
from jax import lax
from jax.experimental import pallas as pl
from jax.experimental.pallas import tpu as pltpu
from jax.sharding import PartitionSpec as P

CAP = 64
GROUP_CLUSTERS = 16
BINS = 128
CORES = 2


def from_partner(value, axis, bit):
    mask = 2**bit
    pairs = [(source, source ^ mask) for source in range(lax.axis_size(axis))]
    return lax.ppermute(value, axis, pairs)


def rank_among_equals(keys):
    places = jnp.arange(keys.shape[0], dtype=jnp.int32)
    earlier_equal = (keys[:, None] == keys[None, :]) & (places[None, :] < places[:, None])
    return jnp.sum(earlier_equal.astype(jnp.int32), axis=1)


def shards(embeddings, document_cluster_index):
    row_count = lax.axis_size("rows")
    col_count = lax.axis_size("cols")
    doc_count = embeddings.shape[0]
    width = embeddings.shape[1]
    slot_count = CAP * row_count
    values = embeddings.astype(jnp.float32)
    normed = (values * lax.rsqrt(jnp.sum(values * values, axis=1, keepdims=True) + 1e-06)).astype(
        jnp.bfloat16
    )
    owner_devices = document_cluster_index // GROUP_CLUSTERS
    within_cluster = (document_cluster_index % GROUP_CLUSTERS).astype(jnp.float32)
    slot_ranks = rank_among_equals(owner_devices)
    places = owner_devices * CAP + slot_ranks
    outgoing = jnp.zeros((slot_count, width), jnp.bfloat16).at[places].set(normed)
    out_labels = (
        jnp.full((slot_count,), -1.0, jnp.float32)
        .at[places]
        .set(within_cluster)
        .astype(jnp.bfloat16)
    )
    resident, res_labels = (
        lax.all_to_all(outgoing, "rows", split_axis=0, concat_axis=0, tiled=True),
        lax.all_to_all(out_labels, "rows", split_axis=0, concat_axis=0, tiled=True),
    )
    home_labels = res_labels.astype(jnp.float32)
    partner_count = max(1, col_count // GROUP_CLUSTERS)
    owned_count = max(1, GROUP_CLUSTERS // col_count)
    slot_quota = 2 * slot_count // GROUP_CLUSTERS // partner_count
    send_total = col_count * owned_count * slot_quota
    local_cluster = res_labels.astype(jnp.int32)
    occupied = local_cluster >= 0
    cluster_rank = rank_among_equals(local_cluster)
    member_slot = cluster_rank % partner_count
    cluster_depth = cluster_rank // partner_count
    destination = local_cluster // owned_count * partner_count + member_slot
    send_place = (
        destination * (owned_count * slot_quota)
        + local_cluster % owned_count * slot_quota
        + cluster_depth
    )
    send_place = jnp.where(occupied, send_place, send_total)
    send_rows = (
        jnp.zeros((send_total, width), jnp.bfloat16).at[send_place].set(resident, mode="drop")
    )
    send_labels = (
        jnp.full((send_total,), -1.0, jnp.float32)
        .at[send_place]
        .set(home_labels, mode="drop")
        .astype(jnp.bfloat16)
    )
    got_rows, got_labels = (
        lax.all_to_all(send_rows, "cols", split_axis=0, concat_axis=0, tiled=True),
        lax.all_to_all(send_labels, "cols", split_axis=0, concat_axis=0, tiled=True),
    )
    member_index = lax.axis_index("cols") % partner_count
    gathered_rows, gathered_labels = (got_rows, got_labels)
    for bit in range(partner_count.bit_length() - 1):
        other_rows, other_labels = from_partner((gathered_rows, gathered_labels), "cols", bit)
        upper = member_index // 2**bit % 2 == 1
        gathered_rows = jnp.where(
            upper,
            jnp.concatenate([other_rows, gathered_rows], axis=0),
            jnp.concatenate([gathered_rows, other_rows], axis=0),
        )
        gathered_labels = jnp.where(
            upper,
            jnp.concatenate([other_labels, gathered_labels], axis=0),
            jnp.concatenate([gathered_labels, other_labels], axis=0),
        )
    similarity_scores = lax.dot_general(
        got_rows, gathered_rows, (((1,), (1,)), ((), ())), preferred_element_type=jnp.float32
    )
    own_labels = got_labels.astype(jnp.float32)
    all_labels = gathered_labels.astype(jnp.float32)
    column_index = jnp.arange(gathered_rows.shape[0], dtype=jnp.int32)
    own_index = member_index * send_total + jnp.arange(send_total, dtype=jnp.int32)
    same_cluster = (own_labels[:, None] == all_labels[None, :]) & (own_labels[:, None] >= 0.0)
    same_cluster = same_cluster & (own_index[:, None] != column_index[None, :])
    best_owned = jnp.max(jnp.where(same_cluster, similarity_scores, -1.0), axis=1)
    came_back = lax.all_to_all(best_owned, "cols", split_axis=0, concat_axis=0, tiled=True)
    row_best = jnp.where(occupied, came_back[jnp.minimum(send_place, send_total - 1)], -1.0)
    answers = lax.all_to_all(row_best, "rows", split_axis=0, concat_axis=0, tiled=True)
    max_similarity = answers[places]
    bin_width = 2.0 / (BINS - 1)
    centers = -1.0 + jnp.arange(BINS, dtype=jnp.float32) * bin_width
    bin_weights = jax.nn.relu(1.0 - jnp.abs(max_similarity[:, None] - centers[None, :]) / bin_width)
    bin_totals = lax.psum(jnp.sum(bin_weights, axis=0), ("rows", "cols"))
    return (max_similarity, bin_totals / (doc_count * row_count * col_count))


CHUNKS = (2, 2, 1, 1, 1, 1)
TWICE = (5, 0)
LATE = 2


def meet_kernel(doc_total, emb_hbm, cluster_hbm, out_ref, emb_ref, cluster_ref, keys, keys_t, blocks, key_labels,
                block_labels, key_best, far_send, final_send, final_box, side_box, far_box, final_best,
                packets, answer_box, in_sems, plane_sems, chunk_sems, twice_sems, block_sems, label_sems, final_sems, side_sems,
                far_sems, packet_sems):
    row, col = lax.axis_index("rows"), lax.axis_index("cols")
    z, core = col // CORES, col % CORES
    row_at = (row, row + 1 - 2 * (row % 2), row + 2 - 4 * (row // 2), 3 - row)
    core_at = (core, 1 - core)
    near = len(row_at)
    slots = near * CORES
    docs, width = emb_ref.shape
    half = docs // 2

    def at_slot(slot, plane):
        return (row_at[slot % near], plane * CORES + core_at[slot // near])

    def above_me(plane):
        return (row, plane * CORES + core)

    me = core * near + row

    def order_of(slot):
        return core_at[slot // near] * near + row_at[slot % near]

    x_peer, y_peer, core_peer = at_slot(1, z), at_slot(2, z), at_slot(near, z)

    def copy(source, target, sems, at, where):
        return pltpu.make_async_remote_copy(
            src_ref=source, dst_ref=target, send_sem=sems.at[(0, *at)], recv_sem=sems.at[(1, *at)],
            device_id=where, device_id_type=pl.DeviceIdType.MESH)

    barrier = pltpu.get_barrier_semaphore()

    def greet(where):
        pl.semaphore_signal(barrier, inc=1, device_id=where, device_id_type=pl.DeviceIdType.MESH)

    senders = {0: (3, 2, 1), 1: (2, 0), 2: (3,), 3: (2,)}
    for plane, sources in senders.items():
        @pl.when(z == plane)
        def _():
            for source in sources:
                greet(above_me(source))
    for peer in (x_peer, y_peer, core_peer):
        greet(peer)
    load = pltpu.make_async_copy(emb_hbm, emb_ref, in_sems.at[0])
    load_labels = pltpu.make_async_copy(cluster_hbm, cluster_ref, in_sems.at[1])
    load.start()
    load_labels.start()
    load_labels.wait()
    key_labels[0] = cluster_ref[...].astype(jnp.float32)
    load.wait()
    values = emb_ref[...].astype(jnp.float32)
    normed = values * lax.rsqrt(jnp.sum(values * values, axis=1, keepdims=True) + 1e-06)
    keys[0:docs, :] = normed.astype(jnp.bfloat16)
    for plane in senders:
        @pl.when(z == plane)
        def _():
            pl.semaphore_wait(barrier, 3 + sum(plane in sources for sources in senders.values()))

    def part(slot, first, size):
        return keys.at[pl.ds(slot * docs + first, size)]

    def plane_copy(n):
        source, target, first, size, where = (
            (0, 1, 0, half, x_peer),
            (0, 2, half, half, y_peer),
            (0, 1, half, half, x_peer),
            (0, 2, 0, half, y_peer),
            (1, 3, 0, half, y_peer),
            (2, 3, half, half, x_peer),
            (0, 4, 0, docs, core_peer),
            (1, 5, 0, docs, core_peer),
            (2, 6, 0, docs, core_peer),
            (3, 7, 0, docs, core_peer),
        )[n]
        return copy(part(source, first, size), part(target, first, size), plane_sems, (n,), where)

    def plane_label(n):
        source, target, count, where = ((0, 1, 1, x_peer), (0, 2, 1, y_peer), (1, 3, 1, y_peer), (0, near, near, core_peer))[n]
        return copy(key_labels.at[pl.ds(source, count)], key_labels.at[pl.ds(target, count)], label_sems, (n,), where)

    def start(*copies):
        for item in copies:
            item.start()

    def arrive(*copies):
        for item in copies:
            item.wait_recv()

    def sent(*copies):
        for item in copies:
            item.wait_send()

    eighth = docs // 8

    def chunk_rows(i):
        return pl.ds(sum(CHUNKS[:i]) * eighth, CHUNKS[i] * eighth)

    def chunk(n, i, source, plane):
        rows = chunk_rows(i)
        block = blocks.at[n, rows]
        return copy(keys.at[rows] if source is None else block, block, chunk_sems, (n, i), above_me(plane))

    def twice(i):
        rows = chunk_rows(i)
        return copy(keys.at[rows], blocks.at[0, rows], twice_sems, (i,), above_me(0))

    def whole(n, plane):
        return copy(keys.at[pl.ds(0, docs)], blocks.at[2], block_sems, (n,), above_me(plane))

    def block_label(n, plane, at, source=None):
        held = block_labels.at[n]
        return copy(key_labels.at[0] if source is None else held, held, label_sems, (4 + at,), above_me(plane))

    def turn(slot):
        keys_t[:, slot * docs:(slot + 1) * docs] = keys[slot * docs:(slot + 1) * docs, :].T

    def plane_start():
        start(plane_copy(0), plane_copy(1), plane_label(0), plane_label(1), plane_copy(2), plane_copy(3), plane_copy(6))
        turn(0)

    def plane_diagonal():
        arrive(plane_copy(0))
        start(plane_copy(4))
        arrive(plane_copy(1))
        start(plane_copy(5))
        arrive(plane_label(0))
        start(plane_label(2))

    def plane_across():
        arrive(plane_copy(2))
        start(plane_copy(7))
        arrive(plane_copy(3))
        start(plane_copy(8))
        turn(1)
        turn(2)

    def plane_last():
        arrive(plane_copy(4), plane_copy(5))
        start(plane_copy(9))
        arrive(plane_label(1), plane_label(2))
        start(plane_label(3))
        turn(3)

    def plane_ready():
        for n in range(6, 10):
            arrive(plane_copy(n))
            turn(n - 2)
        arrive(plane_label(3))

    def plane_sent():
        sent(*[plane_copy(n) for n in range(10)], *[plane_label(n) for n in range(4)])

    same_place = lax.broadcasted_iota(jnp.int32, (docs, docs), 0) == lax.broadcasted_iota(jnp.int32, (docs, docs), 1)

    def score(queries, labels, own, fresh=True, keep=True, done=None):
        parts = len(queries)
        query = queries[0] if parts == 1 else jnp.concatenate(queries, axis=0)
        scores = jnp.dot(query, keys_t[...], preferred_element_type=jnp.float32)
        columns = [jnp.broadcast_to(label, (docs, docs)).T for label in labels]
        tops = [None] * parts
        for slot in range(slots):
            best = None if fresh else key_best[slot]
            for n in range(parts):
                same = columns[n] == key_labels[slot]
                if own and n == 0 and slot == 0:
                    same = same & jnp.logical_not(same_place)
                found = jnp.where(same, scores[n * docs:(n + 1) * docs, slot * docs:(slot + 1) * docs], -1.0)
                tops[n] = found if slot == 0 else jnp.maximum(tops[n], found)
                group = jnp.max(found.reshape(docs // 8, 8, docs), axis=0)
                best = group if best is None else jnp.maximum(best, group)
            if done is not None:
                done(slot, jnp.max(best, axis=0, keepdims=True))
            elif keep:
                key_best[slot] = best
        return [jnp.max(top.T, axis=0, keepdims=True) for top in tops]

    bins_per_unit = (BINS - 1) / 2.0
    centers = lax.broadcasted_iota(jnp.int32, (BINS, docs), 0).astype(jnp.float32) - bins_per_unit

    def missed(rows):
        scaled = rows * bins_per_unit
        return sum(jnp.minimum(jnp.abs(scaled[n:n + 1] - centers), 1.0) for n in range(rows.shape[0]))

    def spread(send, box, sems, to, source):
        return pltpu.make_async_remote_copy(
            src_ref=send, dst_ref=box.at[source], send_sem=sems.at[0, to], recv_sem=sems.at[1, source],
            device_id=(to % near, to // near), device_id_type=pl.DeviceIdType.MESH)

    def final_copy(to, source):
        return spread(final_send, final_box, final_sems, to, source)

    def side_copy(to, source):
        return spread(final_send, side_box, side_sems, to, source)

    def far_copy(to, plane, source):
        return spread(far_send, far_box.at[plane - 2], far_sems.at[:, plane - 2], to, source)

    def keep_final(mine):
        def keep(slot, best):
            final_send[pl.ds(order_of(slot), 1), :] = best if slot else jnp.maximum(mine, best)

        return keep

    reached = (1, 0, near + 1, near, 2, near + 2, 3, near + 3)

    def with_others(act):
        for other in reached:
            pl.when(other != me)(functools.partial(act, other))

    def packet(slot, plane):
        return copy(packets.at[slot, plane - 1], answer_box, packet_sems, (slot, plane), at_slot(slot, plane))

    def take_answer(plane):
        pl.when(row == 0)(lambda: arrive(packet(1, plane)))
        pl.when(row != 0)(lambda: arrive(packet(0, plane)))
        out_ref[...] = answer_box[...]

    every = range(len(CHUNKS))

    def by_core(act):
        for at, count in enumerate(TWICE):
            cut = len(CHUNKS) - count
            pl.when(core == at)(functools.partial(act, every[:cut], every[cut:]))

    for plane in (2, 3):
        @pl.when(z == plane)
        def _():
            other = 5 - plane
            aside = [block_label(2, other, 4), whole(0, other)]
            if plane == 3:
                down = [*[chunk(1, i, None, 0) for i in every], block_label(1, 0, 2)] + aside
            else:
                down = [*aside, block_label(0, 1, 0), block_label(0, 0, 1)]
            start(*down)
            if plane == 2:
                by_core(lambda once, again: start(
                    *[chunk(0, i, None, 1) for i in once], *[twice(i) for i in again[:-LATE]],
                    *[chunk(0, i, None, 1) for i in again], *[twice(i) for i in again[-LATE:]]))
            plane_start()
            plane_diagonal()
            plane_across()
            plane_last()
            plane_ready()
            arrive(block_label(2, plane, 4), whole(0, plane))
            own, theirs = score([keys[0:docs, :], blocks[2]], [key_labels[0], block_labels[2]], True, keep=False)
            far_send[0:1, :] = own
            far_send[1:2, :] = theirs
            far = [far_copy(to, plane, me) for to in range(slots)]
            start(*far)
            sent(*down)
            if plane == 2:
                by_core(lambda once, again: sent(*[chunk(0, i, None, 1) for i in every], *[twice(i) for i in again]))
            plane_sent()
            sent(*far)
            take_answer(plane)

    @pl.when(z == 1)
    def _():
        plane_start()

        def forward(*indices):
            for i in indices:
                arrive(chunk(0, i, 0, 0))
                start(chunk(0, i, 0, 0))

        plane_diagonal()
        plane_across()
        by_core(lambda once, again: forward(*once[:2]))
        plane_last()
        by_core(lambda once, again: forward(*once[2:]))
        plane_ready()
        arrive(block_label(2, 1, 5), whole(1, 1))
        mine, first = score([keys[0:docs, :], blocks[2]], [key_labels[0], block_labels[2]], True)
        arrive(block_label(0, 1, 0), block_label(1, 1, 3, 1), *[chunk(1, i, 1, 1) for i in every])
        by_core(lambda once, again: arrive(*[chunk(0, i, 0, 0) for i in again]))
        second, third = score(
            [blocks[0], blocks[1]], [block_labels[0], block_labels[1]], False, fresh=False, done=keep_final(mine))
        for n, best in enumerate((second, third, first)):
            final_send[slots + n:slots + n + 1, :] = best
        for other in reached:
            side_copy(other, me).start()
        by_core(lambda once, again: sent(*[chunk(0, i, 0, 0) for i in once]))
        plane_sent()
        sent(*[side_copy(other, me) for other in range(slots)])
        take_answer(1)

    @pl.when(z == 0)
    def _():
        start(block_label(2, 1, 5), whole(1, 1))
        plane_start()

        def forward(*indices):
            for i in indices:
                arrive(chunk(1, i, 1, 1))
                start(chunk(1, i, 1, 1))

        plane_diagonal()
        forward(*every[:2])
        plane_across()
        forward(*every[2:])
        arrive(block_label(1, 0, 2))
        start(block_label(1, 1, 3, 1))
        plane_last()
        plane_ready()
        mine, third = score([keys[0:docs, :], blocks[1]], [key_labels[0], block_labels[1]], True)
        arrive(block_label(0, 0, 1))
        by_core(lambda once, again: arrive(*[chunk(0, i, 0, 0) for i in once], *[twice(i) for i in again]))
        second = score([blocks[0]], [block_labels[0]], False, fresh=False, done=keep_final(mine))[0]
        for n, best in enumerate((second, third, mine)):
            final_send[slots + n:slots + n + 1, :] = best
        with_others(lambda other: final_copy(other, me).start())
        final_box[pl.ds(me, 1)] = final_send[...].reshape(1, slots + 3, docs)
        sent(block_label(2, 1, 5), whole(1, 1), block_label(1, 1, 3, 1), *[chunk(1, i, 1, 1) for i in every])
        plane_sent()
        arrive(*[side_copy(0, source) for source in range(slots)])
        final_best[1] = jnp.max(side_box[:, :slots, :], axis=0)
        lacking = missed(final_best[1])
        for plane in (2, 3):
            arrive(*[far_copy(0, plane, source) for source in range(slots)])
        for n in range(2):
            final_best[2 + n] = jnp.maximum(
                side_box[:, slots + n, :], jnp.maximum(far_box[n, :, 0, :], far_box[1 - n, :, 1, :]))
        top = side_box[:, slots + 2, :]
        for slot in (0, near, 1, 2, near + 1, near + 2, 3, near + 3):
            source = order_of(slot)
            if slot:
                final_copy(0, source).wait_recv()
            top = jnp.maximum(top, final_box[source, :slots, :])
            for n in range(2):
                place = pl.ds(source, 1)
                best = jnp.maximum(final_best[2 + n, place, :], final_box[source, slots + n:slots + n + 1, :])
                final_best[2 + n, place, :] = best
                lacking = lacking + missed(best)
        final_best[0] = top
        lacking = lacking + missed(top)
        totals = jnp.sum((4 * slots - lacking).T, axis=0, keepdims=True) / doc_total

        def finish(targets):
            for slot in targets:
                for plane in (1, 3, 2):
                    packets[slot, plane - 1, 0] = final_best[plane, pl.ds(order_of(slot), 1), :]
                    packets[slot, plane - 1, 1] = totals
                    packet(slot, plane).start()

        pl.when(row == 1)(lambda: finish((1,)))
        pl.when(row != 0)(lambda: finish((0,)))
        out_ref[0] = final_best[0, pl.ds(me, 1), :]
        out_ref[1] = totals
        with_others(lambda other: final_copy(other, me).wait_send())

        def finished(targets):
            sent(*[packet(slot, plane) for slot in targets for plane in (3, 2, 1)])

        pl.when(row == 1)(lambda: finished((1,)))
        pl.when(row != 0)(lambda: finished((0,)))


def meet_shards(embeddings, document_cluster_index):
    rows, cols = lax.axis_size("rows"), lax.axis_size("cols")
    docs, width = embeddings.shape
    slots = rows * CORES
    hbm, vmem = pl.BlockSpec(memory_space=pl.ANY), pl.BlockSpec(memory_space=pltpu.VMEM)
    dma = pltpu.SemaphoreType.DMA
    line = lambda *lead: pltpu.VMEM((*lead, 1, docs), jnp.float32)
    found = pl.pallas_call(
        functools.partial(meet_kernel, docs * rows * cols),
        out_shape=pltpu.VMEM((2, 1, docs), jnp.float32),
        in_specs=[hbm, hbm],
        out_specs=vmem,
        scratch_shapes=[
            pltpu.VMEM((docs, width), jnp.bfloat16),
            pltpu.VMEM((1, docs), jnp.int32),
            pltpu.VMEM((slots * docs, width), jnp.bfloat16),
            pltpu.VMEM((width, slots * docs), jnp.bfloat16),
            pltpu.VMEM((3, docs, width), jnp.bfloat16),
            line(slots),
            line(3),
            pltpu.VMEM((slots, 8, docs), jnp.float32),
            pltpu.VMEM((2, docs), jnp.float32),
            pltpu.VMEM((slots + 3, docs), jnp.float32),
            pltpu.VMEM((slots, slots + 3, docs), jnp.float32),
            pltpu.VMEM((slots, slots + 3, docs), jnp.float32),
            pltpu.VMEM((2, slots, 2, docs), jnp.float32),
            pltpu.VMEM((4, slots, docs), jnp.float32),
            line(2, 3, 2),
            line(2),
            dma((2,)),
            dma((2, 10)),
            dma((2, 2, len(CHUNKS))),
            dma((2, len(CHUNKS))),
            dma((2, 2)),
            dma((2, 10)),
            dma((2, slots)),
            dma((2, slots)),
            dma((2, 2, slots)),
            dma((2, 2, 4)),
        ],
        compiler_params=pltpu.CompilerParams(collective_id=0, has_side_effects=True),
    )(embeddings, document_cluster_index.reshape(1, docs))
    return found[0, 0], found[1, 0]


def solution(mesh):
    placed = (P(("rows", "cols"), None), P(("rows", "cols")))
    rows, planes = mesh.shape["rows"], mesh.shape["cols"] // CORES
    direct = rows == 4 and planes == rows
    return jax.shard_map(
        meet_shards if direct else shards, mesh=mesh, in_specs=placed,
        out_specs=(P(("rows", "cols")), P()), check_vma=False
    )
```
